32 devices in a mesh: expert: 4 (over z), ctx: 4 (over y, x), dp: 2 (over core).
Axes of the slice: x: 2, y: 2, z: 4, core: 2. Of those that a mesh axis runs over, the one named last changes fastest.
Arguments:
- tokens: bfloat16 [8, 1024, 1024], P(('expert', 'dp'), 'ctx'), may hold values from -6 to 6
- out_grad: bfloat16 [8, 1024, 1024], P(('expert', 'dp'), 'ctx'), may hold values from -6 to 6
- token_ids: int32 [8, 1024], P(('expert', 'dp'), 'ctx'), may hold values from 0 to 32767, as said below
- hash_table: int32 [32768], replicated, may hold values from 0 to 3, as said below
- doc_lengths: int32 [8, 8], P(('expert', 'dp')), may hold values from 1 to 896, 1024 in all within a row
- w_qkv: bfloat16 [1024, 3072], replicated, may hold values from -0.1875 to 0.1875
- w_out: bfloat16 [1024, 1024], replicated, may hold values from -3 to 3
- gain_attn: float32 [1024], replicated, may hold values from 0.5 to 1.5
- gain_ffn: float32 [1024], replicated, may hold values from 0.5 to 1.5
- expert_in: bfloat16 [4, 1024, 4096], P('expert', None, ('ctx', 'dp')), may hold values from -0.1875 to 0.1875
- expert_out: bfloat16 [4, 4096, 1024], P('expert', ('ctx', 'dp')), may hold values from -0.09375 to 0.09375
Outputs:
- block_out: bfloat16 [8, 1024, 1024], P(('expert', 'dp'), 'ctx')
- grad_tokens: float32 [8, 1024, 1024], P(('expert', 'dp'), 'ctx')
- grad_w_qkv: float32 [1024, 3072], replicated
- grad_w_out: float32 [1024, 1024], replicated
- grad_gain_attn: float32 [1024], replicated
- grad_gain_ffn: float32 [1024], replicated
- grad_expert_in: float32 [4, 1024, 4096], P('expert', None, ('ctx', 'dp'))
- grad_expert_out: float32 [4, 4096, 1024], P('expert', ('ctx', 'dp'))
The draws below stay inside these ranges and needn't reach their ends.
Inputs may be any that keep to these rules, and one draw needn't show every extreme that they name: hash_table names every expert for exactly 8192 ids. `token_ids`: of the 256 tokens of one device, at most 80 map to one expert through hash_table, and in every device exactly 80 map to some expert.
All inputs are finite; a program needn't handle non-finite values.
Results may differ from the reference program's by a relative error of at most 0.012.
Values may be sent and summed in bfloat16 or wider, within the bound.
No kernel may reach another device: no remote copies, remote signals or barrier semaphores. Data moves between devices by JAX's collectives and lax.ppermute only.
A program may use at most 192 MiB of HBM per device.

```python
import math
import jax
import jax.numpy as jnp
import numpy as np
from jax import lax

D = 1024
HEADS = 16
HEAD = 64
FF = 4096
VOCAB = 32768
TOK_DEV = 256
DOCS = 8
EXPERTS = 4
CAP = 80
STREAMS = 8
STREAM_LEN = 1024
N_CTX = 4


def routing_tables(key):
    shuffled = jax.random.permutation(jax.random.fold_in(key, 7), VOCAB).astype(jnp.int32)
    return (shuffled % EXPERTS, jnp.argsort(shuffled).astype(jnp.int32))


def draw_hash_table(key, part):
    tables = routing_tables(key)
    return tables[0].astype(jnp.int32)


def route_block(key, inverse):
    sub_keys = jax.random.split(key, 4)
    favored = jax.random.randint(sub_keys[0], (), 0, EXPERTS)
    slot_count = EXPERTS * CAP
    slot_expert = jnp.arange(slot_count, dtype=jnp.int32) // CAP
    priority = jax.random.permutation(sub_keys[1], slot_count).astype(jnp.int32) - jnp.where(slot_expert == favored, slot_count, 0)
    picked = jnp.argsort(priority)[:TOK_DEV].astype(jnp.int32)
    picked = jax.random.permutation(sub_keys[2], picked)
    expert_row = picked // CAP
    within = jax.random.randint(sub_keys[3], (TOK_DEV,), 0, VOCAB // EXPERTS)
    return jnp.take(inverse, within * EXPERTS + expert_row, axis=0)


def draw_token_ids(key, part):
    tables = routing_tables(key)
    block_total = STREAMS * STREAM_LEN // TOK_DEV
    block_keys = jax.random.split(jax.random.fold_in(key, 11), block_total)

    def one_block(block_key):
        return route_block(block_key, tables[1])
    drawn = jax.vmap(one_block)(block_keys)
    return drawn.reshape(STREAMS, STREAM_LEN).astype(jnp.int32)


def level_of(rng, shape, cuts, low, largest):
    def one(dim, parts):
        draws = jax.random.uniform(jax.random.fold_in(jax.random.fold_in(rng, 6), dim), (parts,), jnp.float32, low / len(cuts), largest / len(cuts))
        return jnp.repeat(jnp.exp(draws), shape[dim] // parts).reshape((-1,) + (1,) * (len(shape) - dim - 1))

    level = one(*cuts[0])
    for cut in cuts[1:]:
        level = level * one(*cut)
    return level


def profile(count, total, limit, skew):
    loads = [(1 << 20) // math.isqrt(standing ** skew) + 1 for standing in range(2, count + 1)]
    spare, holding = total - limit - (count - 1), [1] * (count - 1)
    while spare > 0:
        candidates = [i for i in range(count - 1) if holding[i] < limit]
        pool, remaining = sum([loads[i] for i in candidates]), spare
        for i in candidates:
            more = min(limit - holding[i], max(1, remaining * loads[i] // pool), spare)
            holding[i] = holding[i] + more
            spare = spare - more
    return np.array([limit] + holding)


def ragged(own_key, count, total, most, skew):
    if count == 2:
        one = jax.random.randint(own_key, (), max(1, total - most), min(most, total - 1) + 1)
        return jnp.stack([one, total - one])
    sizes = jnp.asarray(profile(count, total, most, skew), jnp.int32)
    pairs = (count - 1) // 2
    giver, receiver = sizes[1:1 + 2 * pairs:2], sizes[2:2 + 2 * pairs:2]
    room = jnp.minimum(giver - 1, most - receiver)
    shifted = jax.random.randint(jax.random.fold_in(own_key, 1), (pairs,), 0, 1 << 20) % (room + 1)
    sizes = sizes.at[1:1 + 2 * pairs:2].set(giver - shifted).at[2:2 + 2 * pairs:2].set(receiver + shifted)
    return sizes[jax.random.permutation(jax.random.fold_in(own_key, 2), count)]


def normal_values(rng, shape, deviation, most, cuts=(), held_as=jnp.bfloat16):
    entries = deviation * jax.random.normal(rng, shape, jnp.float32)
    if cuts:
        entries = entries * level_of(rng, shape, cuts, -0.22, 0.18)
    return jnp.clip(entries, -most, most).astype(held_as)


def setup_inputs(seed: int = 0) -> dict:
    seeds = jax.random.split(jax.random.key(seed), 12)
    tokens = normal_values(seeds[0], (STREAMS, STREAM_LEN, D), 1.0, 6.0, ((0, 8), (1, 4)))
    out_grad = normal_values(seeds[1], (STREAMS, STREAM_LEN, D), 1.0, 6.0, ((0, 8), (1, 4)))
    token_ids = draw_token_ids(jax.random.fold_in(seeds[11], 71), 0)
    hash_table = draw_hash_table(jax.random.fold_in(seeds[11], 71), 0)
    doc_lengths = jax.vmap(lambda own: ragged(own, DOCS, STREAM_LEN, STREAM_LEN - TOK_DEV // 2, 2))(jax.random.split(seeds[4], STREAMS)).reshape((STREAMS, DOCS)).astype(jnp.int32)
    w_qkv = normal_values(seeds[5], (D, 3 * D), D ** -0.5, 0.1875)
    w_out = normal_values(seeds[6], (D, D), ((STREAM_LEN / (4.0 * D)) ** 0.5), 3.0)
    gain_attn = jnp.clip(1.0 + 0.1 * jax.random.normal(seeds[7], (D,), jnp.float32), 0.5, 1.5)
    gain_ffn = jnp.clip(1.0 + 0.1 * jax.random.normal(seeds[8], (D,), jnp.float32), 0.5, 1.5)
    expert_in = normal_values(seeds[9], (EXPERTS, D, FF), D ** -0.5, 0.1875, ((0, 4), (2, 8)))
    expert_out = normal_values(seeds[10], (EXPERTS, FF, D), FF ** -0.5, 0.09375, ((0, 4), (1, 8)))
    return dict(tokens=tokens, out_grad=out_grad, token_ids=token_ids, hash_table=hash_table, doc_lengths=doc_lengths, w_qkv=w_qkv, w_out=w_out, gain_attn=gain_attn, gain_ffn=gain_ffn, expert_in=expert_in, expert_out=expert_out)


eps = 1e-06
score_scale = 0.125
exact_mode = lax.Precision.HIGHEST

@jax.custom_vjp
def low(v):
    return lax.optimization_barrier(v.astype(jnp.bfloat16)).astype(jnp.float32)

@jax.custom_vjp
def low_back(v):
    return v

def low_keep(v):
    return (low(v), None)

def low_pass(kept, grad):
    return (grad,)

def back_keep(v):
    return (v, None)

def back_low(kept, grad):
    return (low(grad),)
low.defvjp(low_keep, low_pass)
low_back.defvjp(back_keep, back_low)

def rms_norm(values, gain):
    return values * lax.rsqrt(lax.optimization_barrier(jnp.mean(values * values, axis=-1, keepdims=True)) + eps) * gain

def doc_numbers(lengths, total_len):
    doc_ends = jnp.cumsum(lengths).astype(jnp.int32)
    places = jnp.arange(total_len, dtype=jnp.int32)
    return lax.optimization_barrier(jnp.sum((places[:, None] >= doc_ends[None, :]).astype(jnp.int32), axis=1)).astype(jnp.int32)

def attend_stream(normed, lengths, w_qkv_f, w_out_f):
    seq_len = normed.shape[0]
    projected = low_back(low(jnp.dot(low(normed), w_qkv_f, precision=exact_mode)))
    queries = projected[:, :D].reshape(seq_len, HEADS, HEAD)
    key_rows = projected[:, D:2 * D].reshape(seq_len, HEADS, HEAD)
    value_rows = projected[:, 2 * D:].reshape(seq_len, HEADS, HEAD)
    places = jnp.arange(seq_len, dtype=jnp.int32)
    documents = doc_numbers(lengths, seq_len)
    allowed = (places[None, :] <= places[:, None]) & (documents[None, :] == documents[:, None])
    scores = low_back(jnp.einsum('qhd,khd->hqk', queries, key_rows, precision=exact_mode) * score_scale)
    weights = jnp.where(allowed[None], jnp.exp(scores), 0.0)
    totals = lax.optimization_barrier(jnp.sum(weights, axis=2))
    unnormed = low_back(jnp.einsum('hqk,khd->qhd', low(weights), value_rows, precision=exact_mode))
    attended = unnormed / totals.T[:, :, None]
    mixed = low(attended.reshape(seq_len, D))
    return low_back(jnp.dot(mixed, w_out_f, precision=exact_mode))

def expert_block(rows_in, first_proj, second_proj):
    pre_act = low_back(jnp.dot(rows_in, first_proj, precision=exact_mode))
    activated = low(jax.nn.gelu(pre_act))
    return jnp.dot(activated, second_proj, precision=exact_mode)

def slot_positions(chosen):
    member = (chosen[:, None] == jnp.arange(EXPERTS, dtype=jnp.int32)[None, :]).astype(jnp.int32)
    slot_index = (lax.optimization_barrier(jnp.sum(jnp.cumsum(member, axis=0) * member, axis=1)) - 1).astype(jnp.int32)
    return (slot_index * EXPERTS + chosen).astype(jnp.int32)

def slot_sources(places):
    return jnp.full((CAP * EXPERTS,), TOK_DEV, jnp.int32).at[places].set(jnp.arange(TOK_DEV, dtype=jnp.int32))

def take_rows(matrix, indices):
    return jnp.take(matrix, indices, axis=0)

def reference(tokens, out_grad, token_ids, hash_table, doc_lengths, w_qkv, w_out, gain_attn, gain_ffn, expert_in, expert_out):
    block_total = STREAMS * N_CTX
    chosen = jnp.take(hash_table, token_ids.reshape(block_total, TOK_DEV), axis=0).astype(jnp.int32)
    positions = jax.vmap(slot_positions)(chosen)
    sources = jax.vmap(slot_sources)(positions)

    def forward(inputs, w_qkv_f, w_out_f, gain_one, gain_two, first_all, second_all):
        normed = rms_norm(inputs, gain_one)

        def attend_one(pair):
            return attend_stream(pair[0], pair[1], w_qkv_f, w_out_f)
        branch = lax.map(jax.checkpoint(attend_one), (normed, doc_lengths))
        hidden = inputs + branch
        rows_low = low_back(low(rms_norm(hidden, gain_two))).reshape(block_total, TOK_DEV, D)
        padded = jnp.concatenate([rows_low, jnp.zeros((block_total, 1, D), jnp.float32)], axis=1)
        sent = jax.vmap(take_rows)(padded, sources)
        by_expert = sent.reshape(block_total, CAP, EXPERTS, D).transpose(2, 0, 1, 3).reshape(EXPERTS, block_total * CAP, D)

        def expert_one(triple):
            return expert_block(triple[0], triple[1], triple[2])
        results = lax.map(jax.checkpoint(expert_one), (by_expert, first_all, second_all))
        results = low_back(low(results))
        back = results.reshape(EXPERTS, block_total, CAP, D).transpose(1, 2, 0, 3).reshape(block_total, CAP * EXPERTS, D)
        combined = jax.vmap(take_rows)(back, positions)
        return hidden + combined.reshape(STREAMS, STREAM_LEN, D)
    outputs, pullback = jax.vjp(forward, tokens.astype(jnp.float32), w_qkv.astype(jnp.float32), w_out.astype(jnp.float32), gain_attn, gain_ffn, expert_in.astype(jnp.float32), expert_out.astype(jnp.float32))
    grads = pullback(out_grad.astype(jnp.float32))
    return (outputs.astype(jnp.bfloat16), grads[0], grads[1], grads[2], grads[3], grads[4], grads[5], grads[6])
```

```python
import functools
import jax
import jax.numpy as jnp
from jax import lax
from jax.experimental import pallas as pl
from jax.experimental.pallas import tpu as pltpu
from jax.sharding import PartitionSpec as P

HEADS = 16
HEAD = 64
PAIR = 2 * HEAD

eps = 1e-06
score_scale = 0.125
F32 = jnp.float32
BF16 = jnp.bfloat16


def swap(value, axis, bits):
    size = lax.axis_size(axis)
    return lax.ppermute(value, axis, [(i, i ^ bits) for i in range(size)])


def after(value, *others):
    return lax.optimization_barrier((value,) + others)[0]


def matmul(a, b):
    return jnp.dot(a, b, preferred_element_type=F32)


def matmul_nt(a, b):
    return lax.dot_general(a, b, (((1,), (1,)), ((), ())), preferred_element_type=F32)


def matmul_tn(a, b):
    return lax.dot_general(a, b, (((0,), (0,)), ((), ())), preferred_element_type=F32)


def gather_blocks(value, axis):
    size = lax.axis_size(axis)
    if size != 4:
        return [value] + [swap(value, axis, r) for r in range(1, size)]
    half = value.shape[0] // 2
    one = swap(value, axis, 1)
    two = swap(value, axis, 2)
    top = swap(one[:half], axis, 2)
    bottom = swap(two[half:], axis, 1)
    return [value, one, two, jnp.concatenate([top, bottom], axis=0)]


def scatter_sum(pieces, axis):
    total = pieces[0].astype(F32)
    for r in range(1, len(pieces)):
        total = total + swap(pieces[r], axis, r).astype(F32)
    return total


def gelu_parts(pre):
    c = 0.7978845608028654
    square = pre * pre
    inner = c * (pre + 0.044715 * pre * square)
    t = jnp.tanh(inner)
    value = 0.5 * pre * (1.0 + t)
    slope = 0.5 * (1.0 + t) + 0.5 * pre * (1.0 - t * t) * (c * (1.0 + 3.0 * 0.044715 * square))
    return value, slope


def forward_kernel(rank_ref, ends_ref, proj_ref, mixed_ref, att_ref, tot_ref, *, n, rows):
    rank = rank_ref[0]
    pairs = mixed_ref.shape[1] // PAIR
    low = lax.broadcasted_iota(jnp.int32, (rows, PAIR), 1) < HEAD
    q_iota = lax.broadcasted_iota(jnp.int32, (rows, rows), 0)
    k_iota = lax.broadcasted_iota(jnp.int32, (rows, rows), 1)
    one = jnp.ones((), BF16)
    zero = jnp.zeros((), BF16)
    for i in range(n):
        q_at = pl.multiple_of((rank ^ i) * rows, rows)
        for p in range(pairs):
            col = 3 * PAIR * p
            q2 = proj_ref[pl.ds(q_at, rows), col : col + PAIR]
            qs = (jnp.where(low, q2, zero), jnp.where(low, zero, q2))
            sums = [None, None]
            for j in range(i + 1):
                k_at = pl.multiple_of((rank ^ j) * rows, rows)
                k2 = proj_ref[pl.ds(k_at, rows), col + PAIR : col + 2 * PAIR]
                v2 = proj_ref[pl.ds(k_at, rows), col + 2 * PAIR : col + 3 * PAIR]
                vs = (jnp.where(low, v2, one), jnp.where(low, one, v2))
                seen = q_iota + i * rows < ends_ref[:, j * rows : (j + 1) * rows]
                if i == j:
                    seen = seen & (k_iota <= q_iota)
                for h in range(2):
                    weights = jnp.where(seen, jnp.exp(matmul_nt(qs[h], k2)), 0.0).astype(BF16)
                    part = matmul(weights, vs[h])
                    sums[h] = part if sums[h] is None else sums[h] + part
            total = jnp.where(
                low, pltpu.roll(sums[0], HEAD, 1), pltpu.roll(sums[1], HEAD, 1)
            )
            att = jnp.where(low, sums[0], sums[1]) / total
            out = slice(p * PAIR, (p + 1) * PAIR)
            att_ref[pl.ds(q_at, rows), out] = att
            mixed_ref[pl.ds(q_at, rows), out] = att.astype(BF16)
            tot_ref[pl.ds(q_at, rows), out] = total


def attend_forward(rank, ends, proj, n, rows):
    length, width = proj.shape[0], proj.shape[1] // 3
    vmem = pl.BlockSpec(memory_space=pltpu.VMEM)
    shape = functools.partial(jax.ShapeDtypeStruct, (length, width))
    pairs = width // HEAD
    blocks = n * (n + 1) // 2 * pairs
    return pl.pallas_call(
        functools.partial(forward_kernel, n=n, rows=rows),
        out_shape=(shape(BF16), shape(F32), shape(F32)),
        in_specs=[pl.BlockSpec(memory_space=pltpu.SMEM), vmem, vmem],
        out_specs=(vmem, vmem, vmem),
        compiler_params=pltpu.CompilerParams(vmem_limit_bytes=40 << 20),
        cost_estimate=pl.CostEstimate(
            flops=blocks * rows * rows * PAIR * 4,
            bytes_accessed=length * width * 16,
            transcendentals=blocks * rows * rows,
        ),
    )(rank, ends, proj)


def backward_kernel(
    rank_ref, starts_ref, proj_ref, att_ref, tot_ref, g_ref, out_ref, dq_ref, do_ref, sh_ref, *, n, rows
):
    rank = rank_ref[0]
    low = lax.broadcasted_iota(jnp.int32, (rows, PAIR), 1) < HEAD
    k_iota = lax.broadcasted_iota(jnp.int32, (rows, rows), 0)
    q_iota = lax.broadcasted_iota(jnp.int32, (rows, rows), 1)
    zero = jnp.zeros((), BF16)

    def both(value):
        return jnp.where(low, value, zero), jnp.where(low, zero, value)

    for i in range(n):
        at = pl.ds(pl.multiple_of((rank ^ i) * rows, rows), rows)
        here = slice(i * rows, (i + 1) * rows)
        scaled = g_ref[at, :].astype(F32) / tot_ref[at, :]
        do_ref[here, :] = scaled.astype(BF16)
        turned = (scaled * att_ref[at, :]).T
        sh_ref[0:1, here] = jnp.sum(turned[:HEAD], axis=0, keepdims=True)
        sh_ref[1:2, here] = jnp.sum(turned[HEAD:], axis=0, keepdims=True)
    for j in range(n):
        k_at = pl.ds(pl.multiple_of((rank ^ j) * rows, rows), rows)
        k2 = proj_ref[k_at, PAIR : 2 * PAIR]
        v2 = proj_ref[k_at, 2 * PAIR : 3 * PAIR]
        ks = both(k2)
        dk = None
        dv = None
        for i in range(j, n):
            q_at = pl.ds(pl.multiple_of((rank ^ i) * rows, rows), rows)
            here = slice(i * rows, (i + 1) * rows)
            qs = both(proj_ref[q_at, 0:PAIR])
            dos = both(do_ref[here, :])
            seen = k_iota + j * rows >= starts_ref[:, here]
            if i == j:
                seen = seen & (k_iota <= q_iota)
            dq = None
            for h in range(2):
                weights = jnp.where(seen, jnp.exp(matmul_nt(k2, qs[h])), 0.0)
                slope = matmul_nt(v2, dos[h]) - sh_ref[h : h + 1, here]
                ds = (weights * slope).astype(BF16)
                dv_part = matmul(weights.astype(BF16), dos[h])
                dk_part = matmul(ds, qs[h])
                dq_part = matmul_tn(ds, ks[h])
                dv = dv_part if dv is None else dv + dv_part
                dk = dk_part if dk is None else dk + dk_part
                dq = dq_part if dq is None else dq + dq_part
            if j == 0:
                dq_ref[here, :] = dq
            else:
                dq_ref[here, :] += dq
        out_ref[k_at, PAIR : 2 * PAIR] = dk.astype(BF16)
        out_ref[k_at, 2 * PAIR : 3 * PAIR] = dv.astype(BF16)
        out_ref[k_at, 0:PAIR] = (dq_ref[j * rows : (j + 1) * rows, :] * score_scale).astype(BF16)


def attend_backward(rank, starts, proj, att, tot, g, pair, n, rows):
    length = proj.shape[0]
    blocks = n * (n + 1) // 2 * 2

    def columns(width):
        return pl.BlockSpec((length, width), lambda s, r: (0, pair))

    return pl.pallas_call(
        functools.partial(backward_kernel, n=n, rows=rows),
        out_shape=jax.ShapeDtypeStruct((length, 3 * PAIR), BF16),
        grid_spec=pltpu.PrefetchScalarGridSpec(
            num_scalar_prefetch=1,
            grid=(1,),
            in_specs=[
                pl.BlockSpec((1, length), lambda s, r: (0, 0)),
                columns(3 * PAIR),
                columns(PAIR),
                columns(PAIR),
                columns(PAIR),
            ],
            out_specs=pl.BlockSpec((length, 3 * PAIR), lambda s, r: (0, 0)),
            scratch_shapes=[
                pltpu.VMEM((length, PAIR), F32),
                pltpu.VMEM((length, PAIR), BF16),
                pltpu.VMEM((8, length), F32),
            ],
        ),
        compiler_params=pltpu.CompilerParams(vmem_limit_bytes=40 << 20),
        cost_estimate=pl.CostEstimate(
            flops=blocks * rows * rows * PAIR * 10,
            bytes_accessed=length * PAIR * 24,
            transcendentals=blocks * rows * rows,
        ),
    )(rank, starts, proj, att, tot, g)


def qkv_out_kernel(ids_ref, *refs, n, pairs, width):
    own, other = refs[:pairs], refs[pairs : 2 * pairs]
    w_ref, out_ref, sum_ref = refs[2 * pairs :]
    group = pairs * PAIR

    def fill(sources):
        for r in range(n):
            for p in range(pairs):
                for part in range(3):
                    at = pl.multiple_of(
                        part * width + (ids_ref[0] ^ r) * group + p * PAIR, PAIR
                    )
                    out_ref[:, pl.ds(at, PAIR)] = sources[p][
                        r, 0, :, part * PAIR : (part + 1) * PAIR
                    ].astype(F32)

    @pl.when(pl.program_id(0) == 0)
    def _():
        fill(own)

    @pl.when(pl.program_id(0) == 1)
    def _():
        fill(other)

    total = None
    for at in range(0, 3 * width, PAIR):
        term = out_ref[:, at : at + PAIR] * w_ref[:, at : at + PAIR].astype(F32)
        total = term if total is None else total + term
    sum_ref[...] = total


def qkv_out(ids, own, other, w_qkv, n, owners):
    pairs = len(own)
    rows = own[0].shape[2]
    model_width = w_qkv.shape[0]

    def place(s, k, ids_ref):
        return ((ids_ref[2] ^ s) * owners + (ids_ref[1] ^ k), 0)

    own_spec = pl.BlockSpec(
        (n, 1, rows, 3 * PAIR), lambda s, k, ids_ref: (0, jnp.where(s == 0, k, owners - 1), 0, 0)
    )
    other_spec = pl.BlockSpec(
        (n, 1, rows, 3 * PAIR), lambda s, k, ids_ref: (0, jnp.where(s == 0, 0, k), 0, 0)
    )
    return pl.pallas_call(
        functools.partial(qkv_out_kernel, n=n, pairs=pairs, width=model_width),
        out_shape=(
            jax.ShapeDtypeStruct((model_width, 3 * model_width), F32),
            jax.ShapeDtypeStruct((model_width, PAIR), F32),
        ),
        grid_spec=pltpu.PrefetchScalarGridSpec(
            num_scalar_prefetch=1,
            grid=(2, owners),
            in_specs=[own_spec] * pairs
            + [other_spec] * pairs
            + [pl.BlockSpec((rows, 3 * model_width), place)],
            out_specs=(
                pl.BlockSpec((rows, 3 * model_width), place),
                pl.BlockSpec((rows, PAIR), place),
            ),
        ),
        compiler_params=pltpu.CompilerParams(vmem_limit_bytes=32 << 20),
        cost_estimate=pl.CostEstimate(
            flops=6 * model_width * model_width,
            bytes_accessed=24 * model_width * model_width,
            transcendentals=0,
        ),
    )(ids, *own, *other, w_qkv)


def out_out_kernel(ids_ref, own_ref, other_ref, out_ref, *, owners):
    rows, half = own_ref.shape[2], own_ref.shape[3]
    for k in range(owners):
        at = pl.ds(pl.multiple_of((ids_ref[1] ^ k) * rows, rows), rows)
        mine = pl.ds(pl.multiple_of(ids_ref[2] * half, half), half)
        theirs = pl.ds(pl.multiple_of((1 - ids_ref[2]) * half, half), half)
        out_ref[at, mine] = own_ref[0, k].astype(F32)
        out_ref[at, theirs] = other_ref[0, k].astype(F32)


def out_out(ids, own, other, n, owners):
    rows, half = own.shape[2], own.shape[3]
    block = pl.BlockSpec((1, owners, rows, half), lambda r, ids_ref: (r, 0, 0, 0))
    return pl.pallas_call(
        functools.partial(out_out_kernel, owners=owners),
        out_shape=jax.ShapeDtypeStruct((n * owners * rows, 2 * half), F32),
        grid_spec=pltpu.PrefetchScalarGridSpec(
            num_scalar_prefetch=1,
            grid=(n,),
            in_specs=[block, block],
            out_specs=pl.BlockSpec(
                (owners * rows, 2 * half), lambda r, ids_ref: (ids_ref[0] ^ r, 0)
            ),
        ),
        compiler_params=pltpu.CompilerParams(vmem_limit_bytes=16 << 20),
    )(ids, own, other)


def on_device(
    tokens,
    out_grad,
    token_ids,
    hash_table,
    doc_lengths,
    w_qkv,
    w_out,
    gain_attn,
    gain_ffn,
    expert_in,
    expert_out,
):
    rows = tokens.shape[1]
    width = tokens.shape[2]
    n = lax.axis_size("ctx")
    owners = lax.axis_size("expert")
    rank = lax.axis_index("ctx")
    z = lax.axis_index("expert")
    core = lax.axis_index("dp")
    group = width // n
    pairs = group // PAIR
    length = n * rows
    ids = jnp.stack([rank, z, core]).astype(jnp.int32)

    capacity = rows * 5 // (4 * owners)
    slots = owners * capacity
    chosen = jnp.take(hash_table, token_ids[0], axis=0)
    order = jnp.arange(rows, dtype=jnp.int32)
    ahead = (chosen[:, None] == chosen[None, :]) & (order[None, :] < order[:, None])
    slot = jnp.sum(ahead.astype(jnp.int32), axis=1)
    code = (chosen ^ z) * capacity + slot
    picks = (jnp.arange(slots, dtype=jnp.int32)[:, None] == code[None, :]).astype(BF16)
    places = (code[:, None] == jnp.arange(slots, dtype=jnp.int32)[None, :]).astype(BF16)

    def dispatch(matrix):
        return matmul(picks, matrix).astype(BF16)

    inputs_low = tokens[0]
    blocks = gather_blocks(inputs_low, "ctx")

    upstream = out_grad[0]
    up_rows = dispatch(upstream)

    def send_rows(matrix):
        return [matrix[:capacity]] + [
            swap(matrix[k * capacity : (k + 1) * capacity], "expert", k) for k in range(1, owners)
        ]

    def spread(piece):
        line = jnp.concatenate([piece, swap(piece, "ctx", 1)], axis=0)
        return jnp.concatenate([line, swap(line, "dp", 1)], axis=0)

    def unspread(partial):
        quarter = partial.shape[0] // 4
        low = partial.astype(BF16)
        line = partial[: 2 * quarter] + swap(low[2 * quarter :], "dp", 1).astype(F32)
        low = line.astype(BF16)
        return line[:quarter] + swap(low[quarter:], "ctx", 1).astype(F32)

    up_arrived = send_rows(up_rows)
    chunks = [list(range(0, owners // 2)), *[[k] for k in range(owners // 2, owners)]]

    def column(source, part, r, p):
        return lax.dynamic_slice_in_dim(
            source, part * width + (rank ^ r) * group + p * PAIR, PAIR, 1
        )

    w_turned = jnp.concatenate(
        [column(w_qkv, part, r, p) for r in range(n) for p in range(pairs) for part in range(3)],
        axis=1,
    )
    out_turned = jnp.concatenate(
        [lax.dynamic_slice_in_dim(w_out, (rank ^ r) * group, group, 0) for r in range(n)], axis=0
    )
    w_own = w_turned[:, : 3 * group]
    scale_row = jnp.tile(
        jnp.concatenate([jnp.full((PAIR,), score_scale, F32), jnp.ones((2 * PAIR,), F32)]), pairs
    )

    def norm_one(block):
        values = block.astype(F32)
        inverse = lax.rsqrt(jnp.mean(values * values, axis=-1, keepdims=True) + eps)
        return (values * inverse * gain_attn).astype(BF16), inverse

    normed_blocks = [norm_one(block) for block in blocks]
    inverse_one = normed_blocks[0][1]
    normed = jnp.concatenate([block for block, _ in normed_blocks], axis=0)
    proj = (matmul(normed, w_own) * scale_row).astype(BF16)
    doc_ends = jnp.cumsum(doc_lengths[0])
    spots = jnp.arange(length, dtype=jnp.int32)
    later = doc_ends[:, None] > spots[None, :]
    ends = jnp.min(jnp.where(later, doc_ends[:, None], length), axis=0)[None, :].astype(jnp.int32)
    starts = jnp.max(jnp.where(later, 0, doc_ends[:, None]), axis=0)[None, :].astype(jnp.int32)
    mixed_own, att, tot = attend_forward(ids, ends, proj, n, rows)

    first_in, first_out = after(
        (expert_in[0], expert_out[0]), blocks[n - 1]
    )
    weights_in = [expert_in[0]] + [swap(first_in, "ctx", m << 1) for m in range(1, n // 2)]
    weights_out = [expert_out[0]] + [swap(first_out, "ctx", m << 1) for m in range(1, n // 2)]

    up_line = after(jnp.concatenate(up_arrived, axis=0), blocks[n - 1])
    up_line = jnp.concatenate([up_line[None], swap(up_line, "ctx", 1)[None]], axis=0)
    up_all = jnp.concatenate([up_line[None], swap(up_line, "dp", 1)[None]], axis=0)
    up_chunks = [
        up_all[:, :, c[0] * capacity : (c[-1] + 1) * capacity].reshape(-1, width) for c in chunks
    ]

    mixed = jnp.concatenate(
        [mixed_own[:rows]]
        + [swap(mixed_own[r * rows : (r + 1) * rows], "ctx", r) for r in range(1, n)],
        axis=1,
    )
    inputs = inputs_low.astype(F32)
    hidden = inputs + matmul(mixed, out_turned)
    inverse_two = lax.rsqrt(jnp.mean(hidden * hidden, axis=-1, keepdims=True) + eps)
    ffn_low = (hidden * inverse_two * gain_ffn).astype(BF16)

    arrived = send_rows(dispatch(ffn_low))
    row_chunks = [
        spread(jnp.concatenate([arrived[k] for k in c], axis=0) if len(c) > 1 else arrived[c[0]])
        for c in chunks
    ]

    acts = []
    grad_pres = []
    back = []
    for c, row_chunk, up_chunk in zip(chunks, row_chunks, up_chunks):
        act_m = []
        pre_m = []
        partial = None
        for w_in, w_o in zip(weights_in, weights_out):
            value, slope = gelu_parts(matmul(row_chunk, w_in))
            grad_pre = (slope * matmul_nt(up_chunk, w_o)).astype(BF16)
            act_m.append(value.astype(BF16))
            pre_m.append(grad_pre)
            term = matmul_nt(grad_pre, w_in)
            partial = term if partial is None else partial + term
        acts.append(act_m)
        grad_pres.append(pre_m)
        own = unspread(partial).astype(BF16)
        for i, k in enumerate(c):
            piece = own[i * capacity : (i + 1) * capacity]
            back.append(piece if k == 0 else swap(piece, "expert", k))
    grad_rows = matmul(places, jnp.concatenate(back, axis=0))

    up_f = upstream.astype(F32)
    scaled = grad_rows * gain_ffn
    inner = jnp.mean(scaled * hidden, axis=-1, keepdims=True)
    grad_hidden = up_f + inverse_two * scaled - hidden * inverse_two**3 * inner
    branch_grad = grad_hidden.astype(BF16)
    ffn_part = jnp.sum(grad_rows * hidden * inverse_two, axis=0)
    grad_gain_ffn = jnp.sum(
        lax.all_gather(ffn_part, ("expert", "ctx", "dp"), axis=0, tiled=False), axis=0
    )

    grad_att = matmul_nt(branch_grad, out_turned).astype(BF16)
    grad_att_own = jnp.concatenate(
        [grad_att[:, :group]]
        + [swap(grad_att[:, r * group : (r + 1) * group], "ctx", r) for r in range(1, n)],
        axis=0,
    )

    produced = []
    for act_m in acts:
        total = None
        for act, w_o in zip(act_m, weights_out):
            term = matmul(act, w_o)
            total = term if total is None else total + term
        produced.append(total)
    def joined(parts):
        return jnp.concatenate(parts, axis=0)

    rows_all = joined(row_chunks)
    ups_all = joined(up_chunks)
    slots_m = range(len(weights_in))
    grads_in = [matmul_tn(rows_all, joined([g[m] for g in grad_pres])) for m in slots_m]
    grads_out = [matmul_tn(joined([a[m] for a in acts]), ups_all) for m in slots_m]
    grad_expert_out = grads_out[0]
    grad_expert_in = grads_in[0]
    for m in range(1, n // 2):
        grad_expert_out += swap(grads_out[m].astype(BF16), "ctx", m << 1).astype(F32)
        grad_expert_in += swap(grads_in[m].astype(BF16), "ctx", m << 1).astype(F32)

    made = jnp.concatenate(
        [
            total.reshape(4, len(c) * capacity, width) for c, total in zip(chunks, produced)
        ],
        axis=1,
    ).reshape(-1, width)
    made_own = unspread(made).astype(BF16)
    returned = jnp.concatenate(send_rows(made_own), axis=0)
    block_out = (hidden + matmul(places, returned)).astype(BF16)

    def gather_sum(partial_pieces, sum_ctx):
        pass

    d_pairs = [
        attend_backward(ids, starts, proj, att, tot, grad_att_own, p, n, rows) for p in range(pairs)
    ]

    def reduce_z(own):
        piece = own.shape[0] // owners
        parts = [
            lax.dynamic_slice_in_dim(own, (z ^ k) * piece, piece, 0) for k in range(owners)
        ]
        low = [part.astype(BF16) for part in parts]
        total = parts[0].astype(F32)
        for k in range(1, owners):
            total = total + swap(low[k], "expert", k).astype(F32)
        return total.astype(BF16)

    def gather_all(piece):
        line = jnp.concatenate(
            [piece] + [swap(piece, "expert", k) for k in range(1, owners)], axis=0
        )
        plane = jnp.concatenate(gather_blocks(line, "ctx"), axis=0)
        return plane, swap(plane, "dp", 1)

    def halves(value, axis):
        size = value.shape[axis] // 2
        mine = lax.dynamic_slice_in_dim(value, core * size, size, axis)
        theirs = lax.dynamic_slice_in_dim(value, (1 - core) * size, size, axis)
        return mine, theirs

    out_full = matmul_tn(mixed, branch_grad)
    mine, theirs = halves(out_full, 1)
    out_half = mine + swap(theirs.astype(BF16), "dp", 1).astype(F32)
    out_group = scatter_sum(
        [out_half[:group]] + [out_half[r * group : (r + 1) * group].astype(BF16) for r in range(1, n)],
        "ctx",
    )
    out_own, out_other = gather_all(reduce_z(out_group))

    def shaped(value):
        return value.reshape(n, owners, -1, value.shape[-1])

    grad_w_out = out_out(ids, shaped(out_own), shaped(out_other), n, owners)

    qkv_own = []
    qkv_other = []
    for d_pair in d_pairs:
        full = matmul_tn(normed, d_pair)
        mine, theirs = halves(full, 0)
        half = mine + swap(theirs.astype(BF16), "dp", 1).astype(F32)
        own, other = gather_all(reduce_z(half))
        qkv_own.append(shaped(own))
        qkv_other.append(shaped(other))
    grad_w_qkv, gain_sums = qkv_out(ids, qkv_own, qkv_other, w_qkv, n, owners)
    grad_gain_attn = jnp.sum(gain_sums, axis=1) / gain_attn

    d_own = jnp.concatenate(d_pairs, axis=1)
    d_rows = jnp.concatenate(
        [d_own[:rows]] + [swap(d_own[r * rows : (r + 1) * rows], "ctx", r) for r in range(1, n)],
        axis=1,
    )
    grad_normed = matmul_nt(d_rows, w_turned)
    scaled = grad_normed * gain_attn
    inner = jnp.mean(scaled * inputs, axis=-1, keepdims=True)
    grad_inputs = grad_hidden + inverse_one * scaled - inputs * inverse_one**3 * inner
    return (
        block_out[None],
        grad_inputs[None],
        grad_w_qkv,
        grad_w_out,
        grad_gain_attn,
        grad_gain_ffn,
        grad_expert_in[None],
        grad_expert_out[None],
    )


def solution(mesh):
    rows = P(("expert", "dp"), "ctx", None)
    placed = (
        rows,
        rows,
        P(("expert", "dp"), "ctx"),
        P(),
        P(("expert", "dp"), None),
        P(),
        P(),
        P(),
        P(),
        P("expert", None, ("ctx", "dp")),
        P("expert", ("ctx", "dp"), None),
    )
    return jax.shard_map(
        on_device,
        mesh=mesh,
        in_specs=placed,
        out_specs=(
            rows,
            rows,
            P(),
            P(),
            P(),
            P(),
            P("expert", None, ("ctx", "dp")),
            P("expert", ("ctx", "dp"), None),
        ),
        check_vma=False,
    )
```

```python
import functools
import jax
import jax.numpy as jnp
from jax import lax
from jax.experimental import pallas as pl
from jax.experimental.pallas import tpu as pltpu
from jax.sharding import PartitionSpec as P

HEADS = 16
HEAD = 64
PAIR = 2 * HEAD

eps = 1e-06
score_scale = 0.125
F32 = jnp.float32
BF16 = jnp.bfloat16
VMEM = pl.BlockSpec(memory_space=pltpu.VMEM)
SMEM = pl.BlockSpec(memory_space=pltpu.SMEM)
shaped = jax.ShapeDtypeStruct


def swap(value, axis, bits):
    size = lax.axis_size(axis)
    return lax.ppermute(value, axis, [(i, i ^ bits) for i in range(size)])


def exchange(value, axis):
    return lax.all_to_all(value, axis, split_axis=0, concat_axis=0, tiled=True)


def spread_to(value, axis):
    return exchange(jnp.broadcast_to(value[None], (lax.axis_size(axis),) + value.shape), axis)


def after(value, *others):
    return lax.optimization_barrier((value,) + others)[0]


def matmul(a, b):
    return jnp.dot(a, b, preferred_element_type=F32)


def matmul_nt(a, b):
    return lax.dot_general(a, b, (((1,), (1,)), ((), ())), preferred_element_type=F32)


def matmul_tn(a, b):
    return lax.dot_general(a, b, (((0,), (0,)), ((), ())), preferred_element_type=F32)


def params(mib):
    return pltpu.CompilerParams(vmem_limit_bytes=mib << 20)


def cost(flops, moved, transcendentals=0):
    return pl.CostEstimate(
        flops=int(flops / 4), bytes_accessed=int(moved / 4), transcendentals=int(transcendentals / 4)
    )


def distances(bits):
    found = [0]
    for bit in reversed(bits):
        found = found + [value ^ bit for value in found]
    return found


def gelu_parts(pre):
    c = 0.7978845608028654
    square = pre * pre
    t = jnp.tanh(c * (pre + 0.044715 * pre * square))
    half = 0.5 * (1.0 + t)
    slope = half + 0.5 * pre * (1.0 - t * t) * (c * (1.0 + 3.0 * 0.044715 * square))
    return pre * half, slope


def forward_kernel(ids_ref, ends_ref, gain_ref, *refs, n, rows):
    blocks = refs[:n]
    weights = refs[n : n + 3]
    normed_ref, inv_ref, q_ref, k_ref, v_ref, mixed_ref, att_ref, tot_ref = refs[n + 3 :]
    rank = ids_ref[0]
    pairs = mixed_ref.shape[1] // PAIR
    for r in range(n):
        x = blocks[r][...].astype(F32)
        inverse = lax.rsqrt(jnp.mean(x * x, axis=-1, keepdims=True) + eps)
        if r == 0:
            inv_ref[...] = inverse
        here = pl.ds(pl.multiple_of((rank ^ r) * rows, rows), rows)
        normed = (x * inverse * gain_ref[...]).astype(BF16)
        normed_ref[here, :] = normed
        q_ref[here, :] = (matmul(normed, weights[0][...]) * score_scale).astype(BF16)
        k_ref[here, :] = matmul(normed, weights[1][...]).astype(BF16)
        v_ref[here, :] = matmul(normed, weights[2][...]).astype(BF16)
    low = lax.broadcasted_iota(jnp.int32, (rows, PAIR), 1) < HEAD
    q_iota = lax.broadcasted_iota(jnp.int32, (rows, rows), 0)
    k_iota = lax.broadcasted_iota(jnp.int32, (rows, rows), 1)
    one = jnp.ones((), BF16)
    zero = jnp.zeros((), BF16)
    for i in range(n):
        q_at = slice(i * rows, (i + 1) * rows)
        for p in range(pairs):
            out = slice(p * PAIR, (p + 1) * PAIR)
            q2 = q_ref[q_at, out]
            qs = (jnp.where(low, q2, zero), jnp.where(low, zero, q2))
            sums = [None, None]
            for j in range(i + 1):
                k_at = slice(j * rows, (j + 1) * rows)
                k2 = k_ref[k_at, out]
                v2 = v_ref[k_at, out]
                vs = (jnp.where(low, v2, one), jnp.where(low, one, v2))
                seen = q_iota + i * rows < ends_ref[:, j * rows : (j + 1) * rows]
                if i == j:
                    seen = seen & (k_iota <= q_iota)
                for h in range(2):
                    w = jnp.where(seen, jnp.exp(matmul_nt(qs[h], k2)), 0.0).astype(BF16)
                    part = matmul(w, vs[h])
                    sums[h] = part if sums[h] is None else sums[h] + part
            total = jnp.where(low, pltpu.roll(sums[0], HEAD, 1), pltpu.roll(sums[1], HEAD, 1))
            att = jnp.where(low, sums[0], sums[1]) / total
            att_ref[q_at, out] = att
            mixed_ref[q_at, out] = att.astype(BF16)
            tot_ref[q_at, out] = total


def attend_forward(ids, ends, gain, blocks, w_qkv, n):
    rows, width = blocks[0].shape
    group = width // n
    length = n * rows
    count = n * (n + 1) // 2 * (group // HEAD)

    def whole(*shape):
        return pl.BlockSpec(shape, lambda s, ids_ref: (0, 0))

    def columns(part):
        return pl.BlockSpec((width, group), lambda s, ids_ref: (0, part * n + ids_ref[0]))

    own = (length, group)
    return pl.pallas_call(
        functools.partial(forward_kernel, n=n, rows=rows),
        out_shape=(
            shaped((length, width), BF16),
            shaped((rows, 1), F32),
            shaped(own, BF16),
            shaped(own, BF16),
            shaped(own, BF16),
            shaped(own, BF16),
            shaped(own, F32),
            shaped(own, F32),
        ),
        grid_spec=pltpu.PrefetchScalarGridSpec(
            num_scalar_prefetch=1,
            grid=(1,),
            in_specs=[whole(1, length), whole(1, width)]
            + [whole(rows, width)] * n
            + [columns(0), columns(1), columns(2)],
            out_specs=[whole(length, width), whole(rows, 1)] + [whole(*own)] * 6,
        ),
        compiler_params=params(48),
        cost_estimate=cost(
            count * rows * rows * PAIR * 4 + 6 * length * width * group,
            length * width * 4 + length * group * 16 + 6 * width * group,
            count * rows * rows,
        ),
    )(ids, ends, gain, *blocks, w_qkv, w_qkv, w_qkv)


def middle_kernel(ids_ref, *refs, n):
    parts = refs[:n]
    w_ref, x_ref, gain_ref, picks_ref, hidden_ref, inv_ref, sent_ref = refs[n:]
    group = parts[0].shape[1]
    hidden = x_ref[...].astype(F32)
    for r in range(n):
        at = pl.ds(pl.multiple_of((ids_ref[0] ^ r) * group, group), group)
        hidden = hidden + matmul(parts[r][...], w_ref[at, :])
    hidden_ref[...] = hidden
    inverse = lax.rsqrt(jnp.mean(hidden * hidden, axis=-1, keepdims=True) + eps)
    inv_ref[...] = inverse
    low = (hidden * inverse * gain_ref[...]).astype(BF16)
    sent_ref[...] = matmul(picks_ref[...], low).astype(BF16)


def middle(ids, parts, w_out, x, gain, picks):
    rows, width = x.shape
    slots = picks.shape[0]
    return pl.pallas_call(
        functools.partial(middle_kernel, n=len(parts)),
        out_shape=(
            shaped((rows, width), F32),
            shaped((rows, 1), F32),
            shaped((slots, width), BF16),
        ),
        in_specs=[SMEM] + [VMEM] * (len(parts) + 4),
        out_specs=(VMEM, VMEM, VMEM),
        compiler_params=params(24),
        cost_estimate=cost(2 * rows * width * (width + slots), 6 * width * width),
    )(ids, *parts, w_out, x, gain, picks)


def place_columns(out_ref, where, middle_ref, last_ref, units):
    width = out_ref.shape[1]
    size = last_ref.shape[0]
    for b in range(width // units):
        if b * units < width // 2:
            source, at = middle_ref, middle_ref.shape[0] - size + b * units
        else:
            source, at = last_ref, b * units - size
        out_ref[where, b * units : (b + 1) * units] = source[at : at + units]


def expert_kernel(*refs, m):
    row_ref, up_ref, w_in, w_out = refs[:4]
    firsts, middles, lasts = (refs[4 + m * i : 4 + m * (i + 1)] for i in range(3))
    own_ref, other_ref, act_out, pre_out, in_ref, out_ref, act_ref, pre_ref, sems = refs[4 + 3 * m :]
    width, units = w_in.shape
    in_ref[:, :units] = w_in[...]
    out_ref[:units, :] = w_out[...]
    for i in range(m):
        cols = slice((i + 1) * units, (i + 2) * units)
        top = firsts[i].shape[0]
        in_ref[:top, cols] = firsts[i][...]
        in_ref[top:, cols] = middles[i][: width - top]
        place_columns(out_ref, cols, middles[i], lasts[i], units)
    value, slope = gelu_parts(matmul(row_ref[...], in_ref[...]))
    act_ref[...] = value.astype(BF16)
    keep_act = pltpu.make_async_copy(act_ref, act_out, sems.at[0])
    keep_act.start()
    pre_ref[...] = (slope * matmul_nt(up_ref[...], out_ref[...])).astype(BF16)
    keep_pre = pltpu.make_async_copy(pre_ref, pre_out, sems.at[1])
    keep_pre.start()
    half = own_ref.shape[0]
    other_ref[...] = matmul_nt(pre_ref[half:, :], in_ref[...]).astype(BF16)
    own_ref[...] = matmul_nt(pre_ref[:half, :], in_ref[...]).astype(BF16)
    keep_act.wait()
    keep_pre.wait()


def expert_rows(row_chunk, up_chunk, w_in, w_out, firsts, middles, lasts):
    count, width = row_chunk.shape
    m = len(firsts)
    hidden = (m + 1) * w_in.shape[1]
    anywhere = pl.BlockSpec(memory_space=pl.ANY)
    return pl.pallas_call(
        functools.partial(expert_kernel, m=m),
        out_shape=[shaped((count // 2, width), BF16)] * 2 + [shaped((count, hidden), BF16)] * 2,
        in_specs=[VMEM] * (4 + 3 * m),
        out_specs=[VMEM] * 2 + [anywhere] * 2,
        scratch_shapes=[
            pltpu.VMEM((width, hidden), BF16),
            pltpu.VMEM((hidden, width), BF16),
            pltpu.VMEM((count, hidden), BF16),
            pltpu.VMEM((count, hidden), BF16),
            pltpu.SemaphoreType.DMA((2,)),
        ],
        compiler_params=params(40),
        cost_estimate=cost(6 * count * width * hidden, 4 * width * hidden + 8 * count * width),
    )(row_chunk, up_chunk, w_in, w_out, *firsts, *middles, *lasts)


def turn_kernel(ids_ref, *refs, n, owners):
    backs, mixed = refs[:owners], refs[owners : owners + n]
    places_ref, hidden_ref, up_ref, inv_ref, gain_ref, w_ref = refs[owners + n : owners + n + 6]
    grad_ref, part_ref, mine_ref, theirs_ref, branch_ref, full_ref = refs[owners + n + 6 :]
    group = part_ref.shape[2]
    width = hidden_ref.shape[1]
    grad_rows = None
    for k in range(owners):
        term = matmul(places_ref[k], backs[k][...])
        grad_rows = term if grad_rows is None else grad_rows + term
    hidden = hidden_ref[...]
    inverse = inv_ref[...]
    scaled = grad_rows * gain_ref[...]
    inner = jnp.mean(scaled * hidden, axis=-1, keepdims=True)
    grad = up_ref[...].astype(F32) + inverse * scaled - hidden * (inverse**3 * inner)
    grad_ref[...] = grad
    branch_ref[...] = grad.astype(BF16)
    for r in range(n):
        at = pl.ds(pl.multiple_of((ids_ref[0] ^ r) * group, group), group)
        part_ref[r] = matmul_nt(branch_ref[...], w_ref[at, :]).astype(BF16)
    sums = jnp.sum(grad_rows * hidden * inverse, axis=0, keepdims=True)
    blocks = width // (2 * PAIR)
    piece = group // owners
    for r in range(n):
        full_ref[...] = matmul_tn(mixed[r][...], branch_ref[...])
        for s, out_ref in ((0, mine_ref), (1, theirs_ref)):
            for k in range(owners):
                row_at = pl.ds(pl.multiple_of((ids_ref[1] ^ k) * piece, piece), piece)
                for b in range(blocks):
                    col = pl.multiple_of(((ids_ref[2] ^ s) * blocks + b) * PAIR, PAIR)
                    at = ((r * owners + k) * blocks + b) * piece
                    out_ref[at : at + piece, :] = full_ref[row_at, pl.ds(col, PAIR)].astype(
                        out_ref.dtype
                    )
    size = mine_ref.shape[0]
    cols = width // PAIR
    lines = [sums[:, i * PAIR : (i + 1) * PAIR] for i in range(cols)]
    lines = jnp.concatenate(lines + [jnp.zeros((-cols % 16, PAIR), F32)], axis=0)
    theirs_ref[size : size + lines.shape[0], :] = lines.astype(BF16)


def turn(ids, backs, mixed, places, hidden, up, inverse, gain, w_out):
    rows, width = hidden.shape
    n = len(mixed)
    size = width * width // (2 * PAIR)
    extra = -(-width // PAIR // 16) * 16
    return pl.pallas_call(
        functools.partial(turn_kernel, n=n, owners=len(backs)),
        out_shape=(
            shaped((rows, width), F32),
            shaped((n, rows, width // n), BF16),
            shaped((size, PAIR), F32),
            shaped((size + extra, PAIR), BF16),
        ),
        in_specs=[SMEM] + [VMEM] * (len(backs) + n + 6),
        out_specs=(VMEM,) * 4,
        scratch_shapes=[pltpu.VMEM((rows, width), BF16), pltpu.VMEM((width // n, width), F32)],
        compiler_params=params(32),
        cost_estimate=cost(4 * rows * width * (width + rows), 10 * width * width),
    )(ids, *backs, *mixed, places, hidden, up, inverse, gain, w_out)


def weight_grad_kernel(*refs, chunks, sizes):
    a_refs = refs[:chunks]
    b_refs = refs[chunks : 2 * chunks]
    outs = refs[2 * chunks :]
    total = None
    for a_ref, b_ref in zip(a_refs, b_refs):
        term = matmul_tn(a_ref[...], b_ref[...])
        total = term if total is None else total + term
    at = 0
    for out_ref, size in zip(outs, sizes):
        out_ref[...] = total[:, at : at + size].astype(out_ref.dtype)
        at += size


def weight_grads(row_chunks, per_chunk, sizes):
    width = row_chunks[0].shape[1]
    tile = 256
    total = sum(chunk.shape[0] for chunk in row_chunks)
    return pl.pallas_call(
        functools.partial(weight_grad_kernel, chunks=len(row_chunks), sizes=sizes),
        out_shape=[shaped((width, size), BF16 if i else F32) for i, size in enumerate(sizes)],
        grid=(width // tile,),
        in_specs=[pl.BlockSpec((chunk.shape[0], tile), lambda i: (0, i)) for chunk in row_chunks]
        + [pl.BlockSpec(value.shape, lambda i: (0, 0)) for value in per_chunk],
        out_specs=[pl.BlockSpec((tile, size), lambda i: (i, 0)) for size in sizes],
        compiler_params=params(40),
        cost_estimate=cost(2 * width * sum(sizes) * total, 8 * width * sum(sizes)),
    )(*row_chunks, *per_chunk)


def weight_out_kernel(*refs, chunks, sizes, tile):
    acts = refs[:chunks]
    ups = refs[chunks : 2 * chunks]
    outs = refs[2 * chunks :]
    total = None
    for act, up in zip(acts, ups):
        term = matmul_tn(act[...], up[...])
        total = term if total is None else total + term
    first = 0
    for out_ref, size in zip(outs, sizes):
        steps = size // tile

        @pl.when((pl.program_id(0) >= first) & (pl.program_id(0) < first + steps))
        def _():
            out_ref[...] = total.astype(out_ref.dtype)

        first += steps


def weight_grads_out(acts, up_chunks, sizes):
    width = up_chunks[0].shape[1]
    tile = min(256, min(sizes))
    total = sum(chunk.shape[0] for chunk in up_chunks)
    specs = []
    first = 0
    for size in sizes:
        steps = size // tile
        specs.append(
            pl.BlockSpec(
                (tile, width), lambda i, first=first, steps=steps: (jnp.clip(i - first, 0, steps - 1), 0)
            )
        )
        first += steps
    return pl.pallas_call(
        functools.partial(weight_out_kernel, chunks=len(acts), sizes=sizes, tile=tile),
        out_shape=[shaped((size, width), BF16 if i else F32) for i, size in enumerate(sizes)],
        grid=(first,),
        in_specs=[pl.BlockSpec((act.shape[0], tile), lambda i: (0, i)) for act in acts]
        + [pl.BlockSpec(chunk.shape, lambda i: (0, 0)) for chunk in up_chunks],
        out_specs=specs,
        compiler_params=params(40),
        cost_estimate=cost(2 * width * sum(sizes) * total, 8 * width * sum(sizes)),
    )(*acts, *up_chunks)


def produce_kernel(*refs, chunks, m, sizes):
    acts = refs[:chunks]
    w_out = refs[chunks]
    middles = refs[chunks + 1 : chunks + 1 + m]
    lasts = refs[chunks + 1 + m : chunks + 1 + 2 * m]
    own_ref, other_ref, out_ref = refs[chunks + 1 + 2 * m :]
    units, width = w_out.shape
    out_ref[:units, :] = w_out[...]
    for i in range(m):
        cols = slice((i + 1) * units, (i + 2) * units)
        place_columns(out_ref, cols, middles[i], lasts[i], units)
    at = 0
    for c in range(chunks):
        total = matmul(acts[c][...], out_ref[...])
        size = sizes[c]
        for b in range(2):
            own_ref[b, at : at + size, :] = total[b * size : (b + 1) * size].astype(BF16)
            other_ref[b, at : at + size, :] = total[(2 + b) * size : (3 + b) * size].astype(BF16)
        at += size


def produce(acts, w_out, middles, lasts, sizes):
    width = w_out.shape[1]
    hidden = acts[0].shape[1]
    shape = (2, sum(sizes), width)
    return pl.pallas_call(
        functools.partial(produce_kernel, chunks=len(acts), m=len(middles), sizes=sizes),
        out_shape=(shaped(shape, BF16), shaped(shape, BF16)),
        in_specs=[VMEM] * (len(acts) + 1 + 2 * len(middles)),
        out_specs=(VMEM, VMEM),
        scratch_shapes=[pltpu.VMEM((hidden, width), BF16)],
        compiler_params=params(40),
        cost_estimate=cost(
            8 * sum(sizes) * width * hidden, 2 * hidden * width + 16 * sum(sizes) * width
        ),
    )(*acts, w_out, *middles, *lasts)


def backward_kernel(
    ids_ref,
    starts_ref,
    normed_ref,
    q_ref,
    k_ref,
    v_ref,
    att_ref,
    tot_ref,
    g_ref,
    *refs,
    n,
    rows,
    owners,
):
    out_ref, mine_ref, theirs_ref, dq_ref, do_ref, sh_ref, full_ref = refs
    rank = ids_ref[0]
    pairs = q_ref.shape[1] // PAIR
    low = lax.broadcasted_iota(jnp.int32, (rows, PAIR), 1) < HEAD
    k_iota = lax.broadcasted_iota(jnp.int32, (rows, rows), 0)
    q_iota = lax.broadcasted_iota(jnp.int32, (rows, rows), 1)
    zero = jnp.zeros((), BF16)

    def both(value):
        return jnp.where(low, value, zero), jnp.where(low, zero, value)

    for p in range(pairs):
        cols = slice(p * PAIR, (p + 1) * PAIR)
        for i in range(n):
            here = slice(i * rows, (i + 1) * rows)
            at = pl.ds(pl.multiple_of((rank ^ i) * rows, rows), rows)
            scaled = g_ref[at, cols].astype(F32) / tot_ref[here, cols]
            do_ref[here, :] = scaled.astype(BF16)
            turned = (scaled * att_ref[here, cols]).T
            sh_ref[0:1, here] = jnp.sum(turned[:HEAD], axis=0, keepdims=True)
            sh_ref[1:2, here] = jnp.sum(turned[HEAD:], axis=0, keepdims=True)
        for j in range(n):
            k_at = slice(j * rows, (j + 1) * rows)
            k2 = k_ref[k_at, cols]
            v2 = v_ref[k_at, cols]
            ks = both(k2)
            dk = None
            dv = None
            for i in range(j, n):
                here = slice(i * rows, (i + 1) * rows)
                qs = both(q_ref[here, cols])
                dos = both(do_ref[here, :])
                seen = k_iota + j * rows >= starts_ref[:, here]
                if i == j:
                    seen = seen & (k_iota <= q_iota)
                dq = None
                for h in range(2):
                    weights = jnp.where(seen, jnp.exp(matmul_nt(k2, qs[h])), 0.0)
                    slope = matmul_nt(v2, dos[h]) - sh_ref[h : h + 1, here]
                    ds = (weights * slope).astype(BF16)
                    dv_part = matmul(weights.astype(BF16), dos[h])
                    dk_part = matmul(ds, qs[h])
                    dq_part = matmul_tn(ds, ks[h])
                    dv = dv_part if dv is None else dv + dv_part
                    dk = dk_part if dk is None else dk + dk_part
                    dq = dq_part if dq is None else dq + dq_part
                if j == 0:
                    dq_ref[here, :] = dq
                else:
                    dq_ref[here, :] += dq
            out_ref[j, 1, :, cols] = dk.astype(BF16)
            out_ref[j, 2, :, cols] = dv.astype(BF16)
            out_ref[j, 0, :, cols] = (dq_ref[k_at, :] * score_scale).astype(BF16)
    for part in range(3):
        total = None
        for j in range(n):
            term = matmul_tn(normed_ref[j * rows : (j + 1) * rows, :], out_ref[j, part])
            total = term if total is None else total + term
        full_ref[part] = total
    piece = full_ref.shape[1] // (2 * owners)
    for s, to_ref in ((0, mine_ref), (1, theirs_ref)):
        for k in range(owners):
            row = ((ids_ref[2] ^ s) * owners + (ids_ref[1] ^ k)) * piece
            row_at = pl.ds(pl.multiple_of(row, piece), piece)
            for part in range(3):
                for p in range(pairs):
                    at = (part * pairs + p) * piece
                    to_ref[k, at : at + piece, :] = full_ref[
                        part, row_at, p * PAIR : (p + 1) * PAIR
                    ].astype(to_ref.dtype)


def attend_backward(ids, starts, normed, q, k, v, att, tot, g, n, owners):
    length, width = normed.shape
    group = q.shape[1]
    rows = length // n
    count = n * (n + 1) // 2 * (group // HEAD)
    size = (owners, width // (2 * owners) * 3 * group // PAIR, PAIR)
    return pl.pallas_call(
        functools.partial(backward_kernel, n=n, rows=rows, owners=owners),
        out_shape=(
            shaped((n, 3, rows, group), BF16),
            shaped(size, F32),
            shaped(size, BF16),
        ),
        in_specs=[SMEM] + [VMEM] * 8,
        out_specs=(VMEM,) * 3,
        scratch_shapes=[
            pltpu.VMEM((length, PAIR), F32),
            pltpu.VMEM((length, PAIR), BF16),
            pltpu.VMEM((8, length), F32),
            pltpu.VMEM((3, width, group), F32),
        ],
        compiler_params=params(48),
        cost_estimate=cost(
            count * rows * rows * PAIR * 10 + 6 * length * width * group,
            length * group * 24 + 2 * length * width + 9 * width * group,
            count * rows * rows,
        ),
    )(ids, starts, normed, q, k, v, att, tot, g)


def join_kernel(*refs, owners):
    mine_ref, got_ref, out_ref, near_ref = refs[:4]
    count = len(refs) - 4 - owners - 1
    others = refs[4 : 4 + count]
    own_ref, gain_ref = refs[4 + count : 6 + count]
    sent = refs[6 + count :]
    rows = mine_ref.shape[1]
    size = out_ref.shape[0]
    tall = size // owners
    out = out_ref[...]
    gains = [near_ref[...].astype(F32)]
    for other in others:
        out = out + other[:size, :].astype(F32)
        gains.append(other[size:, :].astype(F32))
    while len(gains) > 1:
        gains = [gains[i] + gains[i + 1] for i in range(0, len(gains), 2)]
    gain = gains[0].astype(BF16)
    gain_ref[...] = gain
    for k in range(owners):
        total = mine_ref[k] + got_ref[k].astype(F32)
        part = out[k * tall : (k + 1) * tall]
        if k == 0:
            own_ref[:rows, :] = total
            own_ref[rows:, :] = part
        else:
            sent[k - 1][:rows, :] = total.astype(BF16)
            sent[k - 1][rows : rows + tall, :] = part.astype(BF16)
            sent[k - 1][rows + tall :, :] = gain


def join_sums(mine, got, out_total, gain, others):
    owners, rows, _ = mine.shape
    size = out_total.shape[0]
    tall = rows + size // owners
    extra = gain.shape[0]
    return pl.pallas_call(
        functools.partial(join_kernel, owners=owners),
        out_shape=[shaped((tall, PAIR), F32), shaped((extra, PAIR), BF16)]
        + [shaped((tall + extra, PAIR), BF16)] * (owners - 1),
        in_specs=[VMEM] * (4 + len(others)),
        out_specs=[VMEM] * (owners + 1),
        compiler_params=params(24),
        cost_estimate=cost(owners * tall * PAIR * 4, owners * tall * PAIR * 10),
    )(mine, got, out_total, gain, *others)


def dense_out_kernel(ids_ref, near_ref, *refs, counts, s, n, owners, pairs, width):
    far = refs[: sum(counts)]
    w_ref = refs[sum(counts)]
    out_ref, dense_ref, sum_ref, held_ref, sems = refs[-5:]
    group = pairs * PAIR
    rows = out_ref.shape[0]
    tall = held_ref.shape[2]
    step = pl.program_id(0)

    def copies(k):
        found = []
        low, high = (k - 1) * tall, k * tall
        for r in range(n):
            if k == 0:
                source, target = near_ref.at[ids_ref[0] ^ r], held_ref.at[0, r]
                found.append(pltpu.make_async_copy(source, target, sems.at[0, r, 0]))
                continue
            begin = 0
            first = sum(counts[:r])
            for i, part in enumerate(far[first : first + counts[r]]):
                end = begin + part.shape[0]
                lo, hi = max(low, begin), min(high, end)
                if lo < hi:
                    source = part.at[pl.ds(lo - begin, hi - lo)]
                    target = held_ref.at[k % 2, r, pl.ds(lo - low, hi - lo)]
                    found.append(pltpu.make_async_copy(source, target, sems.at[k % 2, r, i]))
                begin = end
        return found

    @pl.when(step == 0)
    def _():
        for copy in copies(0):
            copy.start()

    for k in range(owners):

        @pl.when(step == k)
        def _():
            if k + 1 < owners:
                for copy in copies(k + 1):
                    copy.start()
            for copy in copies(k):
                copy.wait()

    slot = lax.rem(step, 2)
    out_rows = group // owners
    blocks = width // (2 * PAIR)
    for r in range(n):
        g = ids_ref[0] ^ r
        for part in range(3):
            for p in range(pairs):
                to = pl.multiple_of(part * width + g * group + p * PAIR, PAIR)
                at = (part * pairs + p) * rows
                out_ref[:, pl.ds(to, PAIR)] = held_ref[slot, r, at : at + rows, :].astype(F32)
        row = g * group + (ids_ref[1] ^ step) * out_rows
        row_at = pl.ds(pl.multiple_of(row, out_rows), out_rows)
        for b in range(blocks):
            at = 3 * pairs * rows + b * out_rows
            dense_ref[row_at, b * PAIR : (b + 1) * PAIR] = held_ref[
                slot, r, at : at + out_rows, :
            ].astype(F32)
    total = None
    for at in range(0, 3 * width, PAIR):
        term = out_ref[:, at : at + PAIR] * w_ref[:, at : at + PAIR].astype(F32)
        total = term if total is None else total + term
    sum_ref[...] = total


def dense_out(ids, near, far, w_qkv, s, owners, before=()):
    width = w_qkv.shape[0]
    n, tall, _ = near.shape
    rows = width // (2 * owners)
    anywhere = pl.BlockSpec(memory_space=pl.ANY)
    counts = [len(parts) for parts in far]
    parts = [part for line in far for part in line]

    def place(k, ids_ref):
        return ((ids_ref[2] ^ s) * owners + (ids_ref[1] ^ k), 0)

    return pl.pallas_call(
        functools.partial(
            dense_out_kernel,
            counts=counts,
            s=s,
            n=n,
            owners=owners,
            pairs=width // n // PAIR,
            width=width,
        ),
        out_shape=(
            shaped((width, 3 * width), F32),
            shaped((width, width), F32),
            shaped((width, PAIR), F32),
        ),
        grid_spec=pltpu.PrefetchScalarGridSpec(
            num_scalar_prefetch=1,
            grid=(owners,),
            in_specs=[anywhere] * (1 + len(parts))
            + [pl.BlockSpec((rows, 3 * width), place)]
            + [anywhere] * len(before),
            out_specs=(
                pl.BlockSpec((rows, 3 * width), place),
                pl.BlockSpec((width, width // 2), lambda k, ids_ref: (0, ids_ref[2] ^ s)),
                pl.BlockSpec((rows, PAIR), place),
            ),
            scratch_shapes=[
                pltpu.VMEM((2, n, tall, PAIR), BF16),
                pltpu.SemaphoreType.DMA((2, n, 2)),
            ],
        ),
        input_output_aliases={3 + len(parts) + i: i for i in range(len(before))},
        compiler_params=params(40),
        cost_estimate=cost(3 * width * width, 16 * width * width),
    )(ids, near, *parts, w_qkv, *before)


def back_kernel(d_ref, w_ref, x_ref, inv_ref, gain_ref, grad_ref, out_ref):
    n, _, _, group = d_ref.shape
    width = x_ref.shape[1]
    total = None
    for g in range(n):
        for part in range(3):
            at = part * width + g * group
            term = matmul_nt(d_ref[g, part], w_ref[:, at : at + group])
            total = term if total is None else total + term
    x = x_ref[...].astype(F32)
    inverse = inv_ref[...]
    scaled = total * gain_ref[...]
    inner = jnp.mean(scaled * x, axis=-1, keepdims=True)
    out_ref[...] = grad_ref[...] + inverse * scaled - x * (inverse**3 * inner)


def back_to_tokens(d, w_qkv, x, inverse, gain, grad_hidden):
    rows, width = x.shape
    return pl.pallas_call(
        back_kernel,
        out_shape=shaped((rows, width), F32),
        in_specs=[VMEM] * 6,
        out_specs=VMEM,
        compiler_params=params(32),
        cost_estimate=cost(6 * rows * width * width, 10 * width * width),
    )(d, w_qkv, x, inverse, gain, grad_hidden)


def on_device(
    tokens,
    out_grad,
    token_ids,
    hash_table,
    doc_lengths,
    w_qkv,
    w_out,
    gain_attn,
    gain_ffn,
    expert_in,
    expert_out,
):
    rows = tokens.shape[1]
    width = tokens.shape[2]
    n = lax.axis_size("ctx")
    owners = lax.axis_size("expert")
    rank = lax.axis_index("ctx")
    z = lax.axis_index("expert")
    core = lax.axis_index("dp")
    group = width // n
    pairs = group // PAIR
    length = n * rows
    ids = jnp.stack([rank, z, core]).astype(jnp.int32)

    inputs_low = tokens[0]

    capacity = rows * 5 // (4 * owners)
    slots = owners * capacity
    chosen = jnp.take(hash_table, token_ids[0], axis=0)
    order = jnp.arange(rows, dtype=jnp.int32)
    ahead = (chosen[:, None] == chosen[None, :]) & (order[None, :] < order[:, None])
    slot = jnp.sum(ahead.astype(jnp.int32), axis=1)
    code = (chosen ^ z) * capacity + slot
    picks = (jnp.arange(slots, dtype=jnp.int32)[:, None] == code[None, :]).astype(BF16)
    spots = jnp.arange(slots, dtype=jnp.int32).reshape(owners, 1, capacity)
    places = (code[None, :, None] == spots).astype(BF16)

    def send_rows(matrix):
        far = {}
        for k in list(range(owners // 2, owners)) + list(range(1, owners // 2)):
            far[k] = swap(matrix[k * capacity : (k + 1) * capacity], "expert", k)
        return [matrix[:capacity]] + [far[k] for k in range(1, owners)]

    def spread(piece):
        line = jnp.concatenate([piece, swap(piece, "ctx", 1)], axis=0)
        return jnp.concatenate([line, swap(line, "dp", 1)], axis=0)

    upstream = out_grad[0]
    w_in, w_o = expert_in[0], expert_out[0]
    units = w_in.shape[1]
    top = width * 3 // 4
    upper = w_in[:top]
    up_rows = matmul(picks, upstream).astype(BF16)
    up_arrived = send_rows(up_rows)
    late_low = after(inputs_low, up_rows)
    blocks = [inputs_low] + [
        swap(inputs_low if r & (r - 1) == 0 else late_low, "ctx", r) for r in range(1, n)
    ]
    chunks = [list(range(0, owners // 2)), list(range(owners // 2, owners))]

    doc_ends = jnp.cumsum(doc_lengths[0])
    spots = jnp.arange(length, dtype=jnp.int32)
    later = doc_ends[:, None] > spots[None, :]
    ends = jnp.min(jnp.where(later, doc_ends[:, None], length), axis=0)[None, :].astype(jnp.int32)
    starts = jnp.max(jnp.where(later, 0, doc_ends[:, None]), axis=0)[None, :].astype(jnp.int32)
    normed, inverse_one, q_own, k_own, v_own, mixed_own, att, tot = attend_forward(
        ids, ends, gain_attn[None, :], blocks, w_qkv, n
    )

    cut = width // 2
    middle_w = jnp.concatenate(
        [w_in[top:]] + [w_o[:, at : at + units] for at in range(0, cut, units)], axis=0
    )
    last_w = jnp.concatenate([w_o[:, at : at + units] for at in range(cut, width, units)], axis=0)
    first = after(upper, *blocks[1:])
    firsts = [swap(first, "ctx", m << 1) for m in range(1, n // 2)]
    mixed_own = after(mixed_own, firsts)
    up_line = after(jnp.concatenate(up_arrived, axis=0), mixed_own)
    up_line = jnp.concatenate([up_line[None], swap(up_line, "ctx", 1)[None]], axis=0)
    up_all = jnp.concatenate([up_line[None], swap(up_line, "dp", 1)[None]], axis=0)
    up_chunks = [
        up_all[:, :, c[0] * capacity : (c[-1] + 1) * capacity].reshape(-1, width) for c in chunks
    ]

    mixed_sent = [lax.dynamic_slice_in_dim(mixed_own, (rank ^ r) * rows, rows, 0) for r in range(n)]
    mixed_parts = [mixed_sent[0]] + [swap(mixed_sent[r], "ctx", r) for r in range(1, n)]
    middle_w, last_w = after((middle_w, last_w), mixed_parts)
    middles = [swap(middle_w, "ctx", m << 1) for m in range(1, n // 2)]
    lasts = [swap(last_w, "ctx", m << 1) for m in range(1, n // 2)]
    hidden, inverse_two, row_sent = middle(
        ids, mixed_parts, w_out, inputs_low, gain_ffn[None, :], picks
    )

    near, far = chunks
    arrived = {0: row_sent[:capacity]}
    for k in near[1:] + far:
        arrived[k] = swap(row_sent[k * capacity : (k + 1) * capacity], "expert", k)
    near_rows = jnp.concatenate([arrived[k] for k in near], axis=0)
    far_rows = after(jnp.concatenate([arrived[k] for k in far], axis=0), near_rows, middles)
    row_chunks = [spread(near_rows), spread(far_rows)]
    sizes = [units] * (n // 2)
    acts = []
    grad_pres = []
    far_back = {}
    x_sent = []
    for c, row_chunk, up_chunk in list(zip(chunks, row_chunks, up_chunks))[::-1]:
        if acts:
            row_chunk = after(row_chunk, theirs)
        mine, theirs, act, grad_pre = expert_rows(
            row_chunk, up_chunk, w_in, w_o, firsts, middles, lasts
        )
        acts.append(act)
        grad_pres.append(grad_pre)
        line = mine.astype(F32) + swap(theirs, "dp", 1).astype(F32)
        half = line.shape[0] // 2
        x_sent.append(line[half:].astype(BF16))
        own = (line[:half] + swap(x_sent[-1], "ctx", 1).astype(F32)).astype(BF16)
        for i, k in reversed(list(enumerate(c))):
            piece = own[i * capacity : (i + 1) * capacity]
            far_back[k] = piece if k == 0 else swap(piece, "expert", k)
    back = [far_back[k] for k in range(owners)]
    acts, grad_pres = acts[::-1], grad_pres[::-1]
    last_own = own

    grads_out = weight_grads_out(after(acts, x_sent[0]), up_chunks, sizes)

    def others(grads):
        return [swap(grads[i], "ctx", i << 1) for i in range(1, len(grads))]

    out_others = others(grads_out)
    made, made_other = produce(
        after(acts, x_sent[1]), w_o, middles, lasts, [len(c) * capacity for c in chunks]
    )
    grads_in = weight_grads(row_chunks, after(grad_pres, x_sent[1]), sizes)
    back = after(back, made, grads_in)
    made_other = swap(made_other, "dp", 1)

    grad_hidden, grad_parts, mine, theirs = turn(
        ids, back, mixed_parts, places, hidden, upstream, inverse_two, gain_ffn[None, :], w_out
    )
    grad_parts = after(grad_parts, out_others)
    grad_att_own = jnp.concatenate(
        [grad_parts[0]] + [swap(grad_parts[r], "ctx", r) for r in range(1, n)], axis=0
    )

    def add_others(own, parts):
        for part in parts:
            own = own + part.astype(F32)
        return own

    cols = width // PAIR
    size = mine.shape[0]
    got = swap(theirs, "dp", 1)
    gain_low = (theirs[size:].astype(F32) + got[size:].astype(F32)).astype(BF16)
    total = mine + got[:size].astype(F32)
    piece = size // n
    out_sent = [
        jnp.concatenate([total[r * piece : (r + 1) * piece].astype(BF16), gain_low], axis=0)
        for r in range(1, n)
    ]
    out_sent = after(out_sent, grad_att_own)
    out_got = [swap(out_sent[r - 1], "ctx", r) for r in range(1, n)]

    held = after(grad_att_own, out_sent)
    d_own, mine, theirs = attend_backward(
        ids, starts, normed, q_own, k_own, v_own, att, tot, held, n, owners
    )
    d_own, theirs = after((d_own, theirs), out_got)
    d_pieces = exchange(d_own, "ctx")
    in_others = others(after(grads_in, d_pieces))
    made_line = made.astype(F32) + after(made_other, d_pieces).astype(F32)
    sent = made_line[1].astype(BF16)
    made_own = (made_line[0] + swap(sent, "ctx", 1).astype(F32)).astype(BF16)
    order = list(range(owners // 2, owners)) + list(range(1, owners // 2))
    own, gain_low, *messages = join_sums(
        mine, swap(theirs, "dp", 1), total[: total.shape[0] // n], gain_low, out_got
    )
    tall = own.shape[0]
    got = {k: swap(messages[k - 1], "expert", k) for k in order}
    piece = own
    gains = [gain_low.astype(F32)]
    for k in range(1, owners):
        piece = piece + got[k][:tall].astype(F32)
        gains.append(got[k][tall:].astype(F32))
    while len(gains) > 1:
        gains = [gains[i] + gains[i + 1] for i in range(0, len(gains), 2)]
    grad_gain_ffn = gains[0][:cols].reshape(width)
    piece = piece.astype(BF16)
    grad_inputs = back_to_tokens(
        d_pieces,
        w_qkv,
        inputs_low,
        inverse_one,
        gain_attn[None, :],
        grad_hidden,
    )
    arrived = {k: swap(piece, "expert", k) for k in order}
    near_lines = spread_to(piece, "ctx")
    line = jnp.concatenate([arrived[k] for k in range(1, owners)], axis=0)
    line = after(line, in_others, made_own, near_lines)
    if n == 4:
        half = line.shape[0] // 2
        one, two = swap(line, "ctx", 1), swap(line, "ctx", 2)
        last = [swap(one[:half], "ctx", 2), swap(two[half:], "ctx", 1)]
        far_lines = [[line], [one], [two], last]
    else:
        far_lines = [[line]] + [[swap(line, "ctx", r)] for r in range(1, n)]
    grad_expert_out = add_others(grads_out[0], out_others)
    grad_expert_in = add_others(grads_in[0], in_others)
    returned = jnp.concatenate(send_rows(after(made_own, line)), axis=0)
    block_out = (
        hidden + matmul(places.transpose(1, 0, 2).reshape(rows, slots), returned)
    ).astype(BF16)
    near_other = swap(near_lines, "dp", 1)
    far_lines[n - 1] = after(
        far_lines[n - 1], block_out, grad_inputs, grad_expert_out, grad_expert_in, near_other
    )
    first = dense_out(ids, near_lines, far_lines, w_qkv, 0, owners)
    far_other = [[swap(part, "dp", 1) for part in parts] for parts in far_lines]
    grad_w_qkv, grad_w_out, gain_sums = dense_out(
        ids, near_other, far_other, w_qkv, 1, owners, first
    )
    grad_gain_attn = jnp.sum(gain_sums, axis=1) / gain_attn

    return (
        block_out[None],
        grad_inputs[None],
        grad_w_qkv,
        grad_w_out,
        grad_gain_attn,
        grad_gain_ffn,
        grad_expert_in[None],
        grad_expert_out[None],
    )


def solution(mesh):
    rows = P(("expert", "dp"), "ctx", None)
    placed = (
        rows,
        rows,
        P(("expert", "dp"), "ctx"),
        P(),
        P(("expert", "dp"), None),
        P(),
        P(),
        P(),
        P(),
        P("expert", None, ("ctx", "dp")),
        P("expert", ("ctx", "dp"), None),
    )
    return jax.shard_map(
        on_device,
        mesh=mesh,
        in_specs=placed,
        out_specs=(
            rows,
            rows,
            P(),
            P(),
            P(),
            P(),
            P("expert", None, ("ctx", "dp")),
            P("expert", ("ctx", "dp"), None),
        ),
        check_vma=False,
    )
```

```python
import functools
import jax
import jax.numpy as jnp
from jax import lax
from jax.experimental import pallas as pl
from jax.experimental.pallas import tpu as pltpu
from jax.sharding import PartitionSpec as P

HEADS = 16
HEAD = 64
PAIR = 2 * HEAD

eps = 1e-06
score_scale = 0.125
F32 = jnp.float32
BF16 = jnp.bfloat16
VMEM = pl.BlockSpec(memory_space=pltpu.VMEM)
SMEM = pl.BlockSpec(memory_space=pltpu.SMEM)
shaped = jax.ShapeDtypeStruct


def swap(value, axis, bits):
    size = lax.axis_size(axis)
    return lax.ppermute(value, axis, [(i, i ^ bits) for i in range(size)])


def exchange(value, axis):
    return lax.all_to_all(value, axis, split_axis=0, concat_axis=0, tiled=True)


def spread_to(value, axis):
    return exchange(jnp.broadcast_to(value[None], (lax.axis_size(axis),) + value.shape), axis)


def after(value, *others):
    return lax.optimization_barrier((value,) + others)[0]


def matmul(a, b):
    return jnp.dot(a, b, preferred_element_type=F32)


def matmul_nt(a, b):
    return lax.dot_general(a, b, (((1,), (1,)), ((), ())), preferred_element_type=F32)


def matmul_tn(a, b):
    return lax.dot_general(a, b, (((0,), (0,)), ((), ())), preferred_element_type=F32)


def params(mib):
    return pltpu.CompilerParams(vmem_limit_bytes=mib << 20)


def cost(flops, moved, transcendentals=0):
    return pl.CostEstimate(
        flops=int(flops / 4), bytes_accessed=int(moved / 4), transcendentals=int(transcendentals / 4)
    )


def distances(bits):
    found = [0]
    for bit in reversed(bits):
        found = found + [value ^ bit for value in found]
    return found


def gelu_parts(pre):
    c = 0.7978845608028654
    square = pre * pre
    t = jnp.tanh(c * (pre + 0.044715 * pre * square))
    half = 0.5 * (1.0 + t)
    slope = half + 0.5 * pre * (1.0 - t * t) * (c * (1.0 + 3.0 * 0.044715 * square))
    return pre * half, slope


def forward_kernel(ids_ref, ends_ref, gain_ref, *refs, n, rows):
    blocks = refs[:n]
    weights = refs[n : n + 3]
    normed_ref, inv_ref, q_ref, k_ref, v_ref, mixed_ref, att_ref, tot_ref = refs[n + 3 :]
    rank = ids_ref[0]
    pairs = mixed_ref.shape[1] // PAIR
    for r in range(n):
        x = blocks[r][...].astype(F32)
        inverse = lax.rsqrt(jnp.mean(x * x, axis=-1, keepdims=True) + eps)
        if r == 0:
            inv_ref[...] = inverse
        here = pl.ds(pl.multiple_of((rank ^ r) * rows, rows), rows)
        normed = (x * inverse * gain_ref[...]).astype(BF16)
        normed_ref[here, :] = normed
        q_ref[here, :] = (matmul(normed, weights[0][...]) * score_scale).astype(BF16)
        k_ref[here, :] = matmul(normed, weights[1][...]).astype(BF16)
        v_ref[here, :] = matmul(normed, weights[2][...]).astype(BF16)
    low = lax.broadcasted_iota(jnp.int32, (rows, PAIR), 1) < HEAD
    q_iota = lax.broadcasted_iota(jnp.int32, (rows, rows), 0)
    k_iota = lax.broadcasted_iota(jnp.int32, (rows, rows), 1)
    one = jnp.ones((), BF16)
    zero = jnp.zeros((), BF16)

    @pl.loop(0, pairs)
    def _(p):
        out = pl.ds(pl.multiple_of(p * PAIR, PAIR), PAIR)
        for i in range(n):
            q_at = slice(i * rows, (i + 1) * rows)
            q2 = q_ref[q_at, out]
            qs = (jnp.where(low, q2, zero), jnp.where(low, zero, q2))
            sums = [None, None]
            for j in range(i + 1):
                k_at = slice(j * rows, (j + 1) * rows)
                k2 = k_ref[k_at, out]
                v2 = v_ref[k_at, out]
                vs = (jnp.where(low, v2, one), jnp.where(low, one, v2))
                seen = q_iota + i * rows < ends_ref[:, j * rows : (j + 1) * rows]
                if i == j:
                    seen = seen & (k_iota <= q_iota)
                for h in range(2):
                    w = jnp.where(seen, jnp.exp(matmul_nt(qs[h], k2)), 0.0).astype(BF16)
                    part = matmul(w, vs[h])
                    sums[h] = part if sums[h] is None else sums[h] + part
            total = jnp.where(low, pltpu.roll(sums[0], HEAD, 1), pltpu.roll(sums[1], HEAD, 1))
            att = jnp.where(low, sums[0], sums[1]) / total
            att_ref[q_at, out] = att
            mixed_ref[q_at, out] = att.astype(BF16)
            tot_ref[q_at, out] = total


def attend_forward(ids, ends, gain, blocks, w_qkv, n):
    rows, width = blocks[0].shape
    group = width // n
    length = n * rows
    count = n * (n + 1) // 2 * (group // HEAD)

    def whole(*shape):
        return pl.BlockSpec(shape, lambda s, ids_ref: (0, 0))

    def columns(part):
        return pl.BlockSpec((width, group), lambda s, ids_ref: (0, part * n + ids_ref[0]))

    own = (length, group)
    return pl.pallas_call(
        functools.partial(forward_kernel, n=n, rows=rows),
        out_shape=(
            shaped((length, width), BF16),
            shaped((rows, 1), F32),
            shaped(own, BF16),
            shaped(own, BF16),
            shaped(own, BF16),
            shaped(own, BF16),
            shaped(own, F32),
            shaped(own, F32),
        ),
        grid_spec=pltpu.PrefetchScalarGridSpec(
            num_scalar_prefetch=1,
            grid=(1,),
            in_specs=[whole(1, length), whole(1, width)]
            + [whole(rows, width)] * n
            + [columns(0), columns(1), columns(2)],
            out_specs=[whole(length, width), whole(rows, 1)] + [whole(*own)] * 6,
        ),
        compiler_params=params(48),
        cost_estimate=cost(
            count * rows * rows * PAIR * 4 + 6 * length * width * group,
            length * width * 4 + length * group * 16 + 6 * width * group,
            count * rows * rows,
        ),
    )(ids, ends, gain, *blocks, w_qkv, w_qkv, w_qkv)


def middle_kernel(ids_ref, *refs, n):
    parts = refs[:n]
    w_ref, x_ref, gain_ref, picks_ref, hidden_ref, inv_ref, sent_ref = refs[n:]
    group = parts[0].shape[1]
    hidden = x_ref[...].astype(F32)
    for r in range(n):
        at = pl.ds(pl.multiple_of((ids_ref[0] ^ r) * group, group), group)
        hidden = hidden + matmul(parts[r][...], w_ref[at, :])
    hidden_ref[...] = hidden
    inverse = lax.rsqrt(jnp.mean(hidden * hidden, axis=-1, keepdims=True) + eps)
    inv_ref[...] = inverse
    low = (hidden * inverse * gain_ref[...]).astype(BF16)
    sent_ref[...] = matmul(picks_ref[...], low).astype(BF16)


def middle(ids, parts, w_out, x, gain, picks):
    rows, width = x.shape
    slots = picks.shape[0]
    return pl.pallas_call(
        functools.partial(middle_kernel, n=len(parts)),
        out_shape=(
            shaped((rows, width), F32),
            shaped((rows, 1), F32),
            shaped((slots, width), BF16),
        ),
        in_specs=[SMEM] + [VMEM] * (len(parts) + 4),
        out_specs=(VMEM, VMEM, VMEM),
        compiler_params=params(24),
        cost_estimate=cost(2 * rows * width * (width + slots), 6 * width * width),
    )(ids, *parts, w_out, x, gain, picks)


def place_columns(out_ref, where, rest_ref, units):
    width = out_ref.shape[1]
    for b in range(width // units):
        at = rest_ref.shape[0] - width + b * units
        out_ref[where, b * units : (b + 1) * units] = rest_ref[at : at + units]


def expert_kernel(*refs, m):
    row_ref, up_ref, w_in, w_out = refs[:4]
    firsts, rests = refs[4 : 4 + m], refs[4 + m : 4 + 2 * m]
    own_ref, other_ref, act_out, pre_out, in_ref, out_ref, act_ref, pre_ref, sems = refs[4 + 2 * m :]
    width, units = w_in.shape
    in_ref[:, :units] = w_in[...]
    out_ref[:units, :] = w_out[...]
    for i in range(m):
        cols = slice((i + 1) * units, (i + 2) * units)
        top = firsts[i].shape[0]
        in_ref[:top, cols] = firsts[i][...]
        in_ref[top:, cols] = rests[i][: width - top]
        place_columns(out_ref, cols, rests[i], units)
    half = own_ref.shape[0]
    size = half

    @pl.loop(0, 2 * half // size)
    def _(i):
        here = pl.ds(pl.multiple_of(i * size, size), size)
        value, slope = gelu_parts(matmul(row_ref[here, :], in_ref[...]))
        act_ref[here, :] = value.astype(BF16)
        grad_pre = (slope * matmul_nt(up_ref[here, :], out_ref[...])).astype(BF16)
        pre_ref[here, :] = grad_pre
        part = matmul_nt(grad_pre, in_ref[...]).astype(BF16)

        @pl.when(i * size < half)
        def _():
            own_ref[here, :] = part

        @pl.when(i * size >= half)
        def _():
            other_ref[pl.ds(pl.multiple_of(i * size - half, size), size), :] = part

    keep_act = pltpu.make_async_copy(act_ref, act_out, sems.at[0])
    keep_act.start()
    keep_pre = pltpu.make_async_copy(pre_ref, pre_out, sems.at[1])
    keep_pre.start()
    keep_act.wait()
    keep_pre.wait()


def expert_rows(row_chunk, up_chunk, w_in, w_out, firsts, rests):
    count, width = row_chunk.shape
    m = len(firsts)
    hidden = (m + 1) * w_in.shape[1]
    anywhere = pl.BlockSpec(memory_space=pl.ANY)
    return pl.pallas_call(
        functools.partial(expert_kernel, m=m),
        out_shape=[shaped((count // 2, width), BF16)] * 2 + [shaped((count, hidden), BF16)] * 2,
        in_specs=[VMEM] * (4 + 2 * m),
        out_specs=[VMEM] * 2 + [anywhere] * 2,
        scratch_shapes=[
            pltpu.VMEM((width, hidden), BF16),
            pltpu.VMEM((hidden, width), BF16),
            pltpu.VMEM((count, hidden), BF16),
            pltpu.VMEM((count, hidden), BF16),
            pltpu.SemaphoreType.DMA((2,)),
        ],
        compiler_params=params(40),
        cost_estimate=cost(6 * count * width * hidden, 4 * width * hidden + 8 * count * width),
    )(row_chunk, up_chunk, w_in, w_out, *firsts, *rests)


def turn_kernel(ids_ref, *refs, n, owners):
    backs, mixed = refs[:owners], refs[owners : owners + n]
    places_ref, hidden_ref, up_ref, inv_ref, gain_ref, w_ref = refs[owners + n : owners + n + 6]
    grad_ref, part_ref, mine_ref, theirs_ref, branch_ref, full_ref, mixed_ref = refs[owners + n + 6 :]
    group = part_ref.shape[2]
    width = hidden_ref.shape[1]
    grad_rows = None
    for k in range(owners):
        term = matmul(places_ref[k], backs[k][...])
        grad_rows = term if grad_rows is None else grad_rows + term
    hidden = hidden_ref[...]
    inverse = inv_ref[...]
    scaled = grad_rows * gain_ref[...]
    inner = jnp.mean(scaled * hidden, axis=-1, keepdims=True)
    grad = up_ref[...].astype(F32) + inverse * scaled - hidden * (inverse**3 * inner)
    grad_ref[...] = grad
    branch_ref[...] = grad.astype(BF16)
    for r in range(n):
        at = pl.ds(pl.multiple_of((ids_ref[0] ^ r) * group, group), group)
        part_ref[r] = matmul_nt(branch_ref[...], w_ref[at, :]).astype(BF16)
    sums = jnp.sum(grad_rows * hidden * inverse, axis=0, keepdims=True)
    blocks = width // (2 * PAIR)
    piece = group // owners
    for r in range(n):
        mixed_ref[r] = mixed[r][...]

    @pl.loop(0, n)
    def _(r):
        full_ref[...] = matmul_tn(mixed_ref[r], branch_ref[...])
        for s, out_ref in ((0, mine_ref), (1, theirs_ref)):
            for k in range(owners):
                row_at = pl.ds(pl.multiple_of((ids_ref[1] ^ k) * piece, piece), piece)
                for b in range(blocks):
                    col = pl.multiple_of(((ids_ref[2] ^ s) * blocks + b) * PAIR, PAIR)
                    at = pl.multiple_of(((r * owners + k) * blocks + b) * piece, piece)
                    out_ref[pl.ds(at, piece), :] = full_ref[row_at, pl.ds(col, PAIR)].astype(
                        out_ref.dtype
                    )
    size = mine_ref.shape[0]
    cols = width // PAIR
    lines = [sums[:, i * PAIR : (i + 1) * PAIR] for i in range(cols)]
    lines = jnp.concatenate(lines + [jnp.zeros((-cols % 16, PAIR), F32)], axis=0)
    theirs_ref[size : size + lines.shape[0], :] = lines.astype(BF16)


def turn(ids, backs, mixed, places, hidden, up, inverse, gain, w_out):
    rows, width = hidden.shape
    n = len(mixed)
    size = width * width // (2 * PAIR)
    extra = -(-width // PAIR // 16) * 16
    return pl.pallas_call(
        functools.partial(turn_kernel, n=n, owners=len(backs)),
        out_shape=(
            shaped((rows, width), F32),
            shaped((n, rows, width // n), BF16),
            shaped((size, PAIR), F32),
            shaped((size + extra, PAIR), BF16),
        ),
        in_specs=[SMEM] + [VMEM] * (len(backs) + n + 6),
        out_specs=(VMEM,) * 4,
        scratch_shapes=[pltpu.VMEM((rows, width), BF16), pltpu.VMEM((width // n, width), F32), pltpu.VMEM((n, rows, width // n), BF16)],
        compiler_params=params(32),
        cost_estimate=cost(4 * rows * width * (width + rows), 10 * width * width),
    )(ids, *backs, *mixed, places, hidden, up, inverse, gain, w_out)


def weight_grad_kernel(*refs, chunks, sizes):
    a_refs = refs[:chunks]
    b_refs = refs[chunks : 2 * chunks]
    outs = refs[2 * chunks :]
    total = None
    for a_ref, b_ref in zip(a_refs, b_refs):
        term = matmul_tn(a_ref[...], b_ref[...])
        total = term if total is None else total + term
    at = 0
    for out_ref, size in zip(outs, sizes):
        out_ref[...] = total[:, at : at + size].astype(out_ref.dtype)
        at += size


def weight_grads(row_chunks, per_chunk, sizes):
    width = row_chunks[0].shape[1]
    tile = 256
    total = sum(chunk.shape[0] for chunk in row_chunks)
    return pl.pallas_call(
        functools.partial(weight_grad_kernel, chunks=len(row_chunks), sizes=sizes),
        out_shape=[shaped((width, size), BF16 if i else F32) for i, size in enumerate(sizes)],
        grid=(width // tile,),
        in_specs=[pl.BlockSpec((chunk.shape[0], tile), lambda i: (0, i)) for chunk in row_chunks]
        + [pl.BlockSpec(value.shape, lambda i: (0, 0)) for value in per_chunk],
        out_specs=[pl.BlockSpec((tile, size), lambda i: (i, 0)) for size in sizes],
        compiler_params=params(40),
        cost_estimate=cost(2 * width * sum(sizes) * total, 8 * width * sum(sizes)),
    )(*row_chunks, *per_chunk)


def weight_out_kernel(*refs, chunks, sizes, tile):
    acts = refs[:chunks]
    ups = refs[chunks : 2 * chunks]
    outs = refs[2 * chunks :]
    total = None
    for act, up in zip(acts, ups):
        term = matmul_tn(act[...], up[...])
        total = term if total is None else total + term
    first = 0
    for out_ref, size in zip(outs, sizes):
        steps = size // tile

        @pl.when((pl.program_id(0) >= first) & (pl.program_id(0) < first + steps))
        def _():
            out_ref[...] = total.astype(out_ref.dtype)

        first += steps


def weight_grads_out(acts, up_chunks, sizes):
    width = up_chunks[0].shape[1]
    tile = min(256, min(sizes))
    total = sum(chunk.shape[0] for chunk in up_chunks)
    specs = []
    first = 0
    for size in sizes:
        steps = size // tile
        specs.append(
            pl.BlockSpec(
                (tile, width), lambda i, first=first, steps=steps: (jnp.clip(i - first, 0, steps - 1), 0)
            )
        )
        first += steps
    return pl.pallas_call(
        functools.partial(weight_out_kernel, chunks=len(acts), sizes=sizes, tile=tile),
        out_shape=[shaped((size, width), BF16 if i else F32) for i, size in enumerate(sizes)],
        grid=(first,),
        in_specs=[pl.BlockSpec((act.shape[0], tile), lambda i: (0, i)) for act in acts]
        + [pl.BlockSpec(chunk.shape, lambda i: (0, 0)) for chunk in up_chunks],
        out_specs=specs,
        compiler_params=params(40),
        cost_estimate=cost(2 * width * sum(sizes) * total, 8 * width * sum(sizes)),
    )(*acts, *up_chunks)


def produce_kernel(*refs, chunks, m, sizes):
    acts = refs[:chunks]
    w_out = refs[chunks]
    rests = refs[chunks + 1 : chunks + 1 + m]
    own_ref, other_ref, out_ref = refs[chunks + 1 + m :]
    units, width = w_out.shape
    out_ref[:units, :] = w_out[...]
    for i in range(m):
        cols = slice((i + 1) * units, (i + 2) * units)
        place_columns(out_ref, cols, rests[i], units)
    at = 0
    for c in range(chunks):
        size = sizes[c]

        @pl.loop(0, 2)
        def _(h):
            here = pl.ds(pl.multiple_of(h * 2 * size, 2 * size), 2 * size)
            total = matmul(acts[c][here, :], out_ref[...]).astype(BF16)

            @pl.when(h == 0)
            def _():
                for b in range(2):
                    own_ref[b, at : at + size, :] = total[b * size : (b + 1) * size]

            @pl.when(h == 1)
            def _():
                for b in range(2):
                    other_ref[b, at : at + size, :] = total[b * size : (b + 1) * size]

        at += size


def produce(acts, w_out, rests, sizes):
    width = w_out.shape[1]
    hidden = acts[0].shape[1]
    shape = (2, sum(sizes), width)
    return pl.pallas_call(
        functools.partial(produce_kernel, chunks=len(acts), m=len(rests), sizes=sizes),
        out_shape=(shaped(shape, BF16), shaped(shape, BF16)),
        in_specs=[VMEM] * (len(acts) + 1 + len(rests)),
        out_specs=(VMEM, VMEM),
        scratch_shapes=[pltpu.VMEM((hidden, width), BF16)],
        compiler_params=params(40),
        cost_estimate=cost(
            8 * sum(sizes) * width * hidden, 2 * hidden * width + 16 * sum(sizes) * width
        ),
    )(*acts, w_out, *rests)


def backward_kernel(
    ids_ref,
    starts_ref,
    normed_ref,
    q_ref,
    k_ref,
    v_ref,
    att_ref,
    tot_ref,
    g_ref,
    *refs,
    n,
    rows,
    owners,
):
    out_ref, mine_ref, theirs_ref, dq_ref, do_ref, sh_ref, full_ref = refs
    rank = ids_ref[0]
    pairs = q_ref.shape[1] // PAIR
    low = lax.broadcasted_iota(jnp.int32, (rows, PAIR), 1) < HEAD
    k_iota = lax.broadcasted_iota(jnp.int32, (rows, rows), 0)
    q_iota = lax.broadcasted_iota(jnp.int32, (rows, rows), 1)
    zero = jnp.zeros((), BF16)

    def both(value):
        return jnp.where(low, value, zero), jnp.where(low, zero, value)

    @pl.loop(0, pairs)
    def _(p):
        cols = pl.ds(pl.multiple_of(p * PAIR, PAIR), PAIR)
        for i in range(n):
            here = slice(i * rows, (i + 1) * rows)
            at = pl.ds(pl.multiple_of((rank ^ i) * rows, rows), rows)
            scaled = g_ref[at, cols].astype(F32) / tot_ref[here, cols]
            do_ref[here, :] = scaled.astype(BF16)
            turned = (scaled * att_ref[here, cols]).T
            sh_ref[0:1, here] = jnp.sum(turned[:HEAD], axis=0, keepdims=True)
            sh_ref[1:2, here] = jnp.sum(turned[HEAD:], axis=0, keepdims=True)
        for j in range(n):
            k_at = slice(j * rows, (j + 1) * rows)
            k2 = k_ref[k_at, cols]
            v2 = v_ref[k_at, cols]
            ks = both(k2)
            dk = None
            dv = None
            for i in range(j, n):
                here = slice(i * rows, (i + 1) * rows)
                qs = both(q_ref[here, cols])
                dos = both(do_ref[here, :])
                seen = k_iota + j * rows >= starts_ref[:, here]
                if i == j:
                    seen = seen & (k_iota <= q_iota)
                dq = None
                for h in range(2):
                    weights = jnp.where(seen, jnp.exp(matmul_nt(k2, qs[h])), 0.0)
                    slope = matmul_nt(v2, dos[h]) - sh_ref[h : h + 1, here]
                    ds = (weights * slope).astype(BF16)
                    dv_part = matmul(weights.astype(BF16), dos[h])
                    dk_part = matmul(ds, qs[h])
                    dq_part = matmul_tn(ds, ks[h])
                    dv = dv_part if dv is None else dv + dv_part
                    dk = dk_part if dk is None else dk + dk_part
                    dq = dq_part if dq is None else dq + dq_part
                if j == 0:
                    dq_ref[here, :] = dq
                else:
                    dq_ref[here, :] += dq
            out_ref[j, 1, :, cols] = dk.astype(BF16)
            out_ref[j, 2, :, cols] = dv.astype(BF16)
            out_ref[j, 0, :, cols] = (dq_ref[k_at, :] * score_scale).astype(BF16)

    @pl.loop(0, 3)
    def _(part):
        total = None
        for j in range(n):
            term = matmul_tn(normed_ref[j * rows : (j + 1) * rows, :], out_ref[j, part])
            total = term if total is None else total + term
        full_ref[part] = total

    piece = full_ref.shape[1] // (2 * owners)
    for s, to_ref in ((0, mine_ref), (1, theirs_ref)):
        for k in range(owners):
            row = ((ids_ref[2] ^ s) * owners + (ids_ref[1] ^ k)) * piece
            row_at = pl.ds(pl.multiple_of(row, piece), piece)
            for part in range(3):
                for p in range(pairs):
                    at = (part * pairs + p) * piece
                    to_ref[k, at : at + piece, :] = full_ref[
                        part, row_at, p * PAIR : (p + 1) * PAIR
                    ].astype(to_ref.dtype)


def attend_backward(ids, starts, normed, q, k, v, att, tot, g, n, owners):
    length, width = normed.shape
    group = q.shape[1]
    rows = length // n
    count = n * (n + 1) // 2 * (group // HEAD)
    size = (owners, width // (2 * owners) * 3 * group // PAIR, PAIR)
    return pl.pallas_call(
        functools.partial(backward_kernel, n=n, rows=rows, owners=owners),
        out_shape=(
            shaped((n, 3, rows, group), BF16),
            shaped(size, F32),
            shaped(size, BF16),
        ),
        in_specs=[SMEM] + [VMEM] * 8,
        out_specs=(VMEM,) * 3,
        scratch_shapes=[
            pltpu.VMEM((length, PAIR), F32),
            pltpu.VMEM((length, PAIR), BF16),
            pltpu.VMEM((8, length), F32),
            pltpu.VMEM((3, width, group), F32),
        ],
        compiler_params=params(48),
        cost_estimate=cost(
            count * rows * rows * PAIR * 10 + 6 * length * width * group,
            length * group * 24 + 2 * length * width + 9 * width * group,
            count * rows * rows,
        ),
    )(ids, starts, normed, q, k, v, att, tot, g)


def join_kernel(*refs, owners):
    mine_ref, got_ref, out_ref, near_ref = refs[:4]
    count = len(refs) - 4 - owners - 1
    others = refs[4 : 4 + count]
    own_ref, gain_ref = refs[4 + count : 6 + count]
    sent = refs[6 + count :]
    rows = mine_ref.shape[1]
    size = out_ref.shape[0]
    tall = size // owners
    out = out_ref[...]
    gains = [near_ref[...].astype(F32)]
    for other in others:
        out = out + other[:size, :].astype(F32)
        gains.append(other[size:, :].astype(F32))
    while len(gains) > 1:
        gains = [gains[i] + gains[i + 1] for i in range(0, len(gains), 2)]
    gain = gains[0].astype(BF16)
    gain_ref[...] = gain
    for k in range(owners):
        total = mine_ref[k] + got_ref[k].astype(F32)
        part = out[k * tall : (k + 1) * tall]
        if k == 0:
            own_ref[:rows, :] = total
            own_ref[rows:, :] = part
        else:
            sent[k - 1][:rows, :] = total.astype(BF16)
            sent[k - 1][rows : rows + tall, :] = part.astype(BF16)
            sent[k - 1][rows + tall :, :] = gain


def join_sums(mine, got, out_total, gain, others):
    owners, rows, _ = mine.shape
    size = out_total.shape[0]
    tall = rows + size // owners
    extra = gain.shape[0]
    return pl.pallas_call(
        functools.partial(join_kernel, owners=owners),
        out_shape=[shaped((tall, PAIR), F32), shaped((extra, PAIR), BF16)]
        + [shaped((tall + extra, PAIR), BF16)] * (owners - 1),
        in_specs=[VMEM] * (4 + len(others)),
        out_specs=[VMEM] * (owners + 1),
        compiler_params=params(24),
        cost_estimate=cost(owners * tall * PAIR * 4, owners * tall * PAIR * 10),
    )(mine, got, out_total, gain, *others)


def dense_out_kernel(ids_ref, near_ref, *refs, counts, s, n, owners, pairs, width):
    far = refs[: sum(counts)]
    w_ref = refs[sum(counts)]
    out_ref, dense_ref, sum_ref, held_ref, sems = refs[-5:]
    group = pairs * PAIR
    rows = out_ref.shape[0]
    tall = held_ref.shape[2]
    step = pl.program_id(0)

    def copies(k):
        found = []
        low, high = (k - 1) * tall, k * tall
        for r in range(n):
            if k == 0:
                source, target = near_ref.at[ids_ref[0] ^ r], held_ref.at[0, r]
                found.append(pltpu.make_async_copy(source, target, sems.at[0, r, 0]))
                continue
            begin = 0
            first = sum(counts[:r])
            for i, part in enumerate(far[first : first + counts[r]]):
                end = begin + part.shape[0]
                lo, hi = max(low, begin), min(high, end)
                if lo < hi:
                    source = part.at[pl.ds(lo - begin, hi - lo)]
                    target = held_ref.at[k % 2, r, pl.ds(lo - low, hi - lo)]
                    found.append(pltpu.make_async_copy(source, target, sems.at[k % 2, r, i]))
                begin = end
        return found

    @pl.when(step == 0)
    def _():
        for copy in copies(0):
            copy.start()

    for k in range(owners):

        @pl.when(step == k)
        def _():
            if k + 1 < owners:
                for copy in copies(k + 1):
                    copy.start()
            for copy in copies(k):
                copy.wait()

    slot = lax.rem(step, 2)
    out_rows = group // owners
    blocks = width // (2 * PAIR)
    for r in range(n):
        g = ids_ref[0] ^ r
        for part in range(3):
            for p in range(pairs):
                to = pl.multiple_of(part * width + g * group + p * PAIR, PAIR)
                at = (part * pairs + p) * rows
                out_ref[:, pl.ds(to, PAIR)] = held_ref[slot, r, at : at + rows, :].astype(F32)
        row = g * group + (ids_ref[1] ^ step) * out_rows
        row_at = pl.ds(pl.multiple_of(row, out_rows), out_rows)
        for b in range(blocks):
            at = 3 * pairs * rows + b * out_rows
            dense_ref[row_at, b * PAIR : (b + 1) * PAIR] = held_ref[
                slot, r, at : at + out_rows, :
            ].astype(F32)
    total = None
    for at in range(0, 3 * width, PAIR):
        term = out_ref[:, at : at + PAIR] * w_ref[:, at : at + PAIR].astype(F32)
        total = term if total is None else total + term
    sum_ref[...] = total


def dense_out(ids, near, far, w_qkv, s, owners, before=()):
    width = w_qkv.shape[0]
    n, tall, _ = near.shape
    rows = width // (2 * owners)
    anywhere = pl.BlockSpec(memory_space=pl.ANY)
    counts = [len(parts) for parts in far]
    parts = [part for line in far for part in line]

    def place(k, ids_ref):
        return ((ids_ref[2] ^ s) * owners + (ids_ref[1] ^ k), 0)

    return pl.pallas_call(
        functools.partial(
            dense_out_kernel,
            counts=counts,
            s=s,
            n=n,
            owners=owners,
            pairs=width // n // PAIR,
            width=width,
        ),
        out_shape=(
            shaped((width, 3 * width), F32),
            shaped((width, width), F32),
            shaped((width, PAIR), F32),
        ),
        grid_spec=pltpu.PrefetchScalarGridSpec(
            num_scalar_prefetch=1,
            grid=(owners,),
            in_specs=[anywhere] * (1 + len(parts))
            + [pl.BlockSpec((rows, 3 * width), place)]
            + [anywhere] * len(before),
            out_specs=(
                pl.BlockSpec((rows, 3 * width), place),
                pl.BlockSpec((width, width // 2), lambda k, ids_ref: (0, ids_ref[2] ^ s)),
                pl.BlockSpec((rows, PAIR), place),
            ),
            scratch_shapes=[
                pltpu.VMEM((2, n, tall, PAIR), BF16),
                pltpu.SemaphoreType.DMA((2, n, 2)),
            ],
        ),
        input_output_aliases={3 + len(parts) + i: i for i in range(len(before))},
        compiler_params=params(40),
        cost_estimate=cost(3 * width * width, 16 * width * width),
    )(ids, near, *parts, w_qkv, *before)


def back_kernel(d_ref, w_ref, x_ref, inv_ref, gain_ref, grad_ref, out_ref):
    n, _, _, group = d_ref.shape
    width = x_ref.shape[1]
    out_ref[...] = jnp.zeros_like(out_ref)

    @pl.loop(0, n)
    def _(g):
        for part in range(3):
            at = pl.ds(pl.multiple_of(part * width + g * group, group), group)
            out_ref[...] += matmul_nt(d_ref[g, part], w_ref[:, at])

    x = x_ref[...].astype(F32)
    inverse = inv_ref[...]
    scaled = out_ref[...] * gain_ref[...]
    inner = jnp.mean(scaled * x, axis=-1, keepdims=True)
    out_ref[...] = grad_ref[...] + inverse * scaled - x * (inverse**3 * inner)


def back_to_tokens(d, w_qkv, x, inverse, gain, grad_hidden):
    rows, width = x.shape
    return pl.pallas_call(
        back_kernel,
        out_shape=shaped((rows, width), F32),
        in_specs=[VMEM] * 6,
        out_specs=VMEM,
        compiler_params=params(32),
        cost_estimate=cost(6 * rows * width * width, 10 * width * width),
    )(d, w_qkv, x, inverse, gain, grad_hidden)


def on_device(
    tokens,
    out_grad,
    token_ids,
    hash_table,
    doc_lengths,
    w_qkv,
    w_out,
    gain_attn,
    gain_ffn,
    expert_in,
    expert_out,
):
    rows = tokens.shape[1]
    width = tokens.shape[2]
    n = lax.axis_size("ctx")
    owners = lax.axis_size("expert")
    rank = lax.axis_index("ctx")
    z = lax.axis_index("expert")
    core = lax.axis_index("dp")
    group = width // n
    pairs = group // PAIR
    length = n * rows
    ids = jnp.stack([rank, z, core]).astype(jnp.int32)

    inputs_low = tokens[0]

    capacity = rows * 5 // (4 * owners)
    slots = owners * capacity
    chosen = jnp.take(hash_table, token_ids[0], axis=0)
    order = jnp.arange(rows, dtype=jnp.int32)
    ahead = (chosen[:, None] == chosen[None, :]) & (order[None, :] < order[:, None])
    slot = jnp.sum(ahead.astype(jnp.int32), axis=1)
    code = (chosen ^ z) * capacity + slot
    picks = (jnp.arange(slots, dtype=jnp.int32)[:, None] == code[None, :]).astype(BF16)
    spots = jnp.arange(slots, dtype=jnp.int32).reshape(owners, 1, capacity)
    places = (code[None, :, None] == spots).astype(BF16)

    def send_rows(matrix):
        far = {}
        for k in list(range(owners // 2, owners)) + list(range(1, owners // 2)):
            far[k] = swap(matrix[k * capacity : (k + 1) * capacity], "expert", k)
        return [matrix[:capacity]] + [far[k] for k in range(1, owners)]

    def spread(piece, before=()):
        line = after(jnp.concatenate([piece, swap(piece, "ctx", 1)], axis=0), *before)
        return jnp.concatenate([line, swap(line, "dp", 1)], axis=0)

    upstream = out_grad[0]
    w_in, w_o = expert_in[0], expert_out[0]
    units = w_in.shape[1]
    top = width * 3 // 4
    upper = w_in[:top]
    up_rows = matmul(picks, upstream).astype(BF16)
    up_arrived = send_rows(up_rows)
    late_low = after(inputs_low, up_rows)
    blocks = [inputs_low] + [
        swap(inputs_low if r & (r - 1) == 0 else late_low, "ctx", r) for r in range(1, n)
    ]
    chunks = [list(range(0, owners // 2)), list(range(owners // 2, owners))]

    doc_ends = jnp.cumsum(doc_lengths[0])
    spots = jnp.arange(length, dtype=jnp.int32)
    later = doc_ends[:, None] > spots[None, :]
    ends = jnp.min(jnp.where(later, doc_ends[:, None], length), axis=0)[None, :].astype(jnp.int32)
    starts = jnp.max(jnp.where(later, 0, doc_ends[:, None]), axis=0)[None, :].astype(jnp.int32)
    normed, inverse_one, q_own, k_own, v_own, mixed_own, att, tot = attend_forward(
        ids, ends, gain_attn[None, :], blocks, w_qkv, n
    )

    rest = jnp.concatenate(
        [w_in[top:]] + [w_o[:, at : at + units] for at in range(0, width, units)], axis=0
    )
    first = after(upper, *blocks[1:])
    firsts = [swap(first, "ctx", m << 1) for m in range(1, n // 2)]
    mixed_own = after(mixed_own, firsts)
    up_line = after(jnp.concatenate(up_arrived, axis=0), mixed_own)
    up_line = jnp.concatenate([up_line[None], swap(up_line, "ctx", 1)[None]], axis=0)
    up_all = jnp.concatenate([up_line[None], swap(up_line, "dp", 1)[None]], axis=0)
    up_chunks = [
        up_all[:, :, c[0] * capacity : (c[-1] + 1) * capacity].reshape(-1, width) for c in chunks
    ]

    mixed_sent = [lax.dynamic_slice_in_dim(mixed_own, (rank ^ r) * rows, rows, 0) for r in range(n)]
    mixed_parts = [mixed_sent[0]] + [swap(mixed_sent[r], "ctx", r) for r in range(1, n)]
    rest = after(rest, mixed_parts)
    rests = [swap(rest, "ctx", m << 1) for m in range(1, n // 2)]
    hidden, inverse_two, row_sent = middle(
        ids, mixed_parts, w_out, inputs_low, gain_ffn[None, :], picks
    )

    near, far = chunks
    arrived = {0: row_sent[:capacity]}
    for k in near[1:] + far:
        arrived[k] = swap(row_sent[k * capacity : (k + 1) * capacity], "expert", k)
    near_rows = jnp.concatenate([arrived[k] for k in near], axis=0)
    far_rows = after(jnp.concatenate([arrived[k] for k in far], axis=0), near_rows)
    row_chunks = [spread(near_rows), spread(far_rows, rests)]
    sizes = [units] * (n // 2)
    acts = []
    grad_pres = []
    far_back = {}
    x_sent = []
    for c, row_chunk, up_chunk in list(zip(chunks, row_chunks, up_chunks))[::-1]:
        if acts:
            row_chunk = after(row_chunk, theirs)
        mine, theirs, act, grad_pre = expert_rows(
            row_chunk, up_chunk, w_in, w_o, firsts, rests
        )
        acts.append(act)
        grad_pres.append(grad_pre)
        line = mine.astype(F32) + swap(theirs, "dp", 1).astype(F32)
        half = line.shape[0] // 2
        x_sent.append(line[half:].astype(BF16))
        own = (line[:half] + swap(x_sent[-1], "ctx", 1).astype(F32)).astype(BF16)
        for i, k in reversed(list(enumerate(c))):
            piece = own[i * capacity : (i + 1) * capacity]
            far_back[k] = piece if k == 0 else swap(piece, "expert", k)
    back = [far_back[k] for k in range(owners)]
    acts, grad_pres = acts[::-1], grad_pres[::-1]
    last_own = own

    grads_out = weight_grads_out(after(acts, x_sent[0]), up_chunks, sizes)

    def others(grads):
        return [swap(grads[i], "ctx", i << 1) for i in range(1, len(grads))]

    out_others = others(grads_out)
    made, made_other = produce(
        after(acts, x_sent[1]), w_o, rests, [len(c) * capacity for c in chunks]
    )
    grads_in = weight_grads(row_chunks, after(grad_pres, x_sent[1]), sizes)
    back = after(back, made, grads_in)
    made_other = swap(made_other, "dp", 1)

    grad_hidden, grad_parts, mine, theirs = turn(
        ids, back, mixed_parts, places, hidden, upstream, inverse_two, gain_ffn[None, :], w_out
    )
    grad_parts = after(grad_parts, out_others)
    grad_att_own = jnp.concatenate(
        [grad_parts[0]] + [swap(grad_parts[r], "ctx", r) for r in range(1, n)], axis=0
    )

    def add_others(own, parts):
        for part in parts:
            own = own + part.astype(F32)
        return own

    cols = width // PAIR
    size = mine.shape[0]
    got = swap(theirs, "dp", 1)
    gain_low = (theirs[size:].astype(F32) + got[size:].astype(F32)).astype(BF16)
    total = mine + got[:size].astype(F32)
    piece = size // n
    out_sent = [
        jnp.concatenate([total[r * piece : (r + 1) * piece].astype(BF16), gain_low], axis=0)
        for r in range(1, n)
    ]
    out_sent = after(out_sent, grad_att_own)
    out_got = [swap(out_sent[r - 1], "ctx", r) for r in range(1, n)]

    held = after(grad_att_own, out_sent)
    d_own, mine, theirs = attend_backward(
        ids, starts, normed, q_own, k_own, v_own, att, tot, held, n, owners
    )
    d_own, theirs = after((d_own, theirs), out_got)
    d_pieces = exchange(d_own, "ctx")
    in_others = others(after(grads_in, d_pieces))
    made_line = made.astype(F32) + after(made_other, d_pieces).astype(F32)
    sent = made_line[1].astype(BF16)
    made_own = (made_line[0] + swap(sent, "ctx", 1).astype(F32)).astype(BF16)
    order = list(range(owners // 2, owners)) + list(range(1, owners // 2))
    own, gain_low, *messages = join_sums(
        mine, swap(theirs, "dp", 1), total[: total.shape[0] // n], gain_low, out_got
    )
    tall = own.shape[0]
    got = {k: swap(messages[k - 1], "expert", k) for k in order}
    piece = own
    gains = [gain_low.astype(F32)]
    for k in range(owners - 1, 0, -1):
        piece = piece + got[k][:tall].astype(F32)
    for k in range(1, owners):
        gains.append(got[k][tall:].astype(F32))
    while len(gains) > 1:
        gains = [gains[i] + gains[i + 1] for i in range(0, len(gains), 2)]
    grad_gain_ffn = gains[0][:cols].reshape(width)
    piece = piece.astype(BF16)
    arrived = {k: swap(piece, "expert", k) for k in order}
    near_lines = spread_to(piece, "ctx")
    line = jnp.concatenate([arrived[k] for k in range(1, owners)], axis=0)
    line = after(line, in_others, made_own, near_lines)
    if n == 4:
        half = line.shape[0] // 2
        one, two = swap(line, "ctx", 1), swap(line, "ctx", 2)
        sent = (one[:half], two[half:])
        last = [swap(sent[0], "ctx", 2), swap(sent[1], "ctx", 1)]
        far_lines = [[line], [one], [two], last]
        in_others, out_others, d_pieces = after((in_others, out_others, d_pieces), sent)
    else:
        far_lines = [[line]] + [[swap(line, "ctx", r)] for r in range(1, n)]
    grad_inputs = back_to_tokens(
        d_pieces,
        w_qkv,
        inputs_low,
        inverse_one,
        gain_attn[None, :],
        grad_hidden,
    )
    grad_expert_out = add_others(grads_out[0], out_others)
    grad_expert_in = add_others(grads_in[0], in_others)
    returned = jnp.concatenate(send_rows(after(made_own, line)), axis=0)
    block_out = (
        hidden + matmul(places.transpose(1, 0, 2).reshape(rows, slots), returned)
    ).astype(BF16)
    near_other = swap(near_lines, "dp", 1)
    far_lines[n - 1] = after(
        far_lines[n - 1], block_out, grad_inputs, grad_expert_out, grad_expert_in, near_other
    )
    first = dense_out(ids, near_lines, far_lines, w_qkv, 0, owners)
    far_other = [[swap(part, "dp", 1) for part in parts] for parts in far_lines]
    grad_w_qkv, grad_w_out, gain_sums = dense_out(
        ids, near_other, far_other, w_qkv, 1, owners, first
    )
    grad_gain_attn = jnp.sum(gain_sums, axis=1) / gain_attn

    return (
        block_out[None],
        grad_inputs[None],
        grad_w_qkv,
        grad_w_out,
        grad_gain_attn,
        grad_gain_ffn,
        grad_expert_in[None],
        grad_expert_out[None],
    )


def solution(mesh):
    rows = P(("expert", "dp"), "ctx", None)
    placed = (
        rows,
        rows,
        P(("expert", "dp"), "ctx"),
        P(),
        P(("expert", "dp"), None),
        P(),
        P(),
        P(),
        P(),
        P("expert", None, ("ctx", "dp")),
        P("expert", ("ctx", "dp"), None),
    )
    return jax.shard_map(
        on_device,
        mesh=mesh,
        in_specs=placed,
        out_specs=(
            rows,
            rows,
            P(),
            P(),
            P(),
            P(),
            P("expert", None, ("ctx", "dp")),
            P("expert", ("ctx", "dp"), None),
        ),
        check_vma=False,
    )
```

```python
import functools
import jax
import jax.numpy as jnp
from jax import lax
from jax.experimental import pallas as pl
from jax.experimental.pallas import tpu as pltpu
from jax.sharding import PartitionSpec as P

HEADS = 16
HEAD = 64
PAIR = 2 * HEAD

eps = 1e-06
score_scale = 0.125
F32 = jnp.float32
BF16 = jnp.bfloat16
VMEM = pl.BlockSpec(memory_space=pltpu.VMEM)
SMEM = pl.BlockSpec(memory_space=pltpu.SMEM)
shaped = jax.ShapeDtypeStruct


def swap(value, axis, bits):
    size = lax.axis_size(axis)
    return lax.ppermute(value, axis, [(i, i ^ bits) for i in range(size)])


def exchange(value, axis):
    return lax.all_to_all(value, axis, split_axis=0, concat_axis=0, tiled=True)


def spread_to(value, axis):
    return exchange(jnp.broadcast_to(value[None], (lax.axis_size(axis),) + value.shape), axis)


def after(value, *others):
    return lax.optimization_barrier((value,) + others)[0]


def matmul(a, b):
    return jnp.dot(a, b, preferred_element_type=F32)


def matmul_nt(a, b):
    return lax.dot_general(a, b, (((1,), (1,)), ((), ())), preferred_element_type=F32)


def matmul_tn(a, b):
    return lax.dot_general(a, b, (((0,), (0,)), ((), ())), preferred_element_type=F32)


def params(mib):
    return pltpu.CompilerParams(vmem_limit_bytes=mib << 20)


def cost(flops, moved, transcendentals=0):
    return pl.CostEstimate(
        flops=int(flops / 4), bytes_accessed=int(moved / 4), transcendentals=int(transcendentals / 4)
    )


def distances(bits):
    found = [0]
    for bit in reversed(bits):
        found = found + [value ^ bit for value in found]
    return found


def gelu_parts(pre):
    c = 0.7978845608028654
    square = pre * pre
    t = jnp.tanh(c * (pre + 0.044715 * pre * square))
    half = 0.5 * (1.0 + t)
    slope = half + 0.5 * pre * (1.0 - t * t) * (c * (1.0 + 3.0 * 0.044715 * square))
    return pre * half, slope


def forward_kernel(ids_ref, ends_ref, gain_ref, *refs, n, rows):
    blocks = refs[:n]
    weights = refs[n : n + 3]
    normed_ref, inv_ref, q_ref, k_ref, v_ref, mixed_ref, att_ref, tot_ref = refs[n + 3 :]
    rank = ids_ref[0]
    pairs = mixed_ref.shape[1] // PAIR
    for r in range(n):
        x = blocks[r][...].astype(F32)
        inverse = lax.rsqrt(jnp.mean(x * x, axis=-1, keepdims=True) + eps)
        if r == 0:
            inv_ref[...] = inverse
        here = pl.ds(pl.multiple_of((rank ^ r) * rows, rows), rows)
        normed = (x * inverse * gain_ref[...]).astype(BF16)
        normed_ref[here, :] = normed
        q_ref[here, :] = (matmul(normed, weights[0][...]) * score_scale).astype(BF16)
        k_ref[here, :] = matmul(normed, weights[1][...]).astype(BF16)
        v_ref[here, :] = matmul(normed, weights[2][...]).astype(BF16)
    low = lax.broadcasted_iota(jnp.int32, (rows, PAIR), 1) < HEAD
    q_iota = lax.broadcasted_iota(jnp.int32, (rows, rows), 0)
    k_iota = lax.broadcasted_iota(jnp.int32, (rows, rows), 1)
    one = jnp.ones((), BF16)
    zero = jnp.zeros((), BF16)

    @pl.loop(0, pairs)
    def _(p):
        out = pl.ds(pl.multiple_of(p * PAIR, PAIR), PAIR)
        for i in range(n):
            q_at = slice(i * rows, (i + 1) * rows)
            q2 = q_ref[q_at, out]
            qs = (jnp.where(low, q2, zero), jnp.where(low, zero, q2))
            sums = [None, None]
            for j in range(i + 1):
                k_at = slice(j * rows, (j + 1) * rows)
                k2 = k_ref[k_at, out]
                v2 = v_ref[k_at, out]
                vs = (jnp.where(low, v2, one), jnp.where(low, one, v2))
                seen = q_iota + i * rows < ends_ref[:, j * rows : (j + 1) * rows]
                if i == j:
                    seen = seen & (k_iota <= q_iota)
                for h in range(2):
                    w = jnp.where(seen, jnp.exp(matmul_nt(qs[h], k2)), 0.0).astype(BF16)
                    part = matmul(w, vs[h])
                    sums[h] = part if sums[h] is None else sums[h] + part
            total = jnp.where(low, pltpu.roll(sums[0], HEAD, 1), pltpu.roll(sums[1], HEAD, 1))
            att = jnp.where(low, sums[0], sums[1]) / total
            att_ref[q_at, out] = att
            mixed_ref[q_at, out] = att.astype(BF16)
            tot_ref[q_at, out] = total


def attend_forward(ids, ends, gain, blocks, w_qkv, n):
    rows, width = blocks[0].shape
    group = width // n
    length = n * rows
    count = n * (n + 1) // 2 * (group // HEAD)

    def whole(*shape):
        return pl.BlockSpec(shape, lambda s, ids_ref: (0, 0))

    def columns(part):
        return pl.BlockSpec((width, group), lambda s, ids_ref: (0, part * n + ids_ref[0]))

    own = (length, group)
    return pl.pallas_call(
        functools.partial(forward_kernel, n=n, rows=rows),
        out_shape=(
            shaped((length, width), BF16),
            shaped((rows, 1), F32),
            shaped(own, BF16),
            shaped(own, BF16),
            shaped(own, BF16),
            shaped(own, BF16),
            shaped(own, F32),
            shaped(own, F32),
        ),
        grid_spec=pltpu.PrefetchScalarGridSpec(
            num_scalar_prefetch=1,
            grid=(1,),
            in_specs=[whole(1, length), whole(1, width)]
            + [whole(rows, width)] * n
            + [columns(0), columns(1), columns(2)],
            out_specs=[whole(length, width), whole(rows, 1)] + [whole(*own)] * 6,
        ),
        compiler_params=params(48),
        cost_estimate=cost(
            count * rows * rows * PAIR * 4 + 6 * length * width * group,
            length * width * 4 + length * group * 16 + 6 * width * group,
            count * rows * rows,
        ),
    )(ids, ends, gain, *blocks, w_qkv, w_qkv, w_qkv)


def middle_kernel(ids_ref, *refs, n):
    parts = refs[:n]
    w_ref, x_ref, gain_ref, picks_ref, hidden_ref, inv_ref, sent_ref = refs[n:]
    group = parts[0].shape[1]
    hidden = x_ref[...].astype(F32)
    for r in range(n):
        at = pl.ds(pl.multiple_of((ids_ref[0] ^ r) * group, group), group)
        hidden = hidden + matmul(parts[r][...], w_ref[at, :])
    hidden_ref[...] = hidden
    inverse = lax.rsqrt(jnp.mean(hidden * hidden, axis=-1, keepdims=True) + eps)
    inv_ref[...] = inverse
    low = (hidden * inverse * gain_ref[...]).astype(BF16)
    sent_ref[...] = matmul(picks_ref[...], low).astype(BF16)


def middle(ids, parts, w_out, x, gain, picks):
    rows, width = x.shape
    slots = picks.shape[0]
    return pl.pallas_call(
        functools.partial(middle_kernel, n=len(parts)),
        out_shape=(
            shaped((rows, width), F32),
            shaped((rows, 1), F32),
            shaped((slots, width), BF16),
        ),
        in_specs=[SMEM] + [VMEM] * (len(parts) + 4),
        out_specs=(VMEM, VMEM, VMEM),
        compiler_params=params(24),
        cost_estimate=cost(2 * rows * width * (width + slots), 6 * width * width),
    )(ids, *parts, w_out, x, gain, picks)


def place_columns(out_ref, where, rest_ref, units):
    width = out_ref.shape[1]
    for b in range(width // units):
        at = rest_ref.shape[0] - width + b * units
        out_ref[where, b * units : (b + 1) * units] = rest_ref[at : at + units]


def expert_kernel(*refs, m):
    row_ref, up_ref, w_in, w_out = refs[:4]
    firsts, rests = refs[4 : 4 + m], refs[4 + m : 4 + 2 * m]
    own_ref, other_ref, act_out, pre_out, in_ref, out_ref, act_ref, pre_ref, sems = refs[4 + 2 * m :]
    width, units = w_in.shape
    in_ref[:, :units] = w_in[...]
    out_ref[:units, :] = w_out[...]
    for i in range(m):
        cols = slice((i + 1) * units, (i + 2) * units)
        top = firsts[i].shape[0]
        in_ref[:top, cols] = firsts[i][...]
        in_ref[top:, cols] = rests[i][: width - top]
        place_columns(out_ref, cols, rests[i], units)
    half = own_ref.shape[0]
    size = half

    @pl.loop(0, 2 * half // size)
    def _(i):
        here = pl.ds(pl.multiple_of(i * size, size), size)
        value, slope = gelu_parts(matmul(row_ref[here, :], in_ref[...]))
        act_ref[here, :] = value.astype(BF16)
        grad_pre = (slope * matmul_nt(up_ref[here, :], out_ref[...])).astype(BF16)
        pre_ref[here, :] = grad_pre
        part = matmul_nt(grad_pre, in_ref[...]).astype(BF16)

        @pl.when(i * size < half)
        def _():
            own_ref[here, :] = part

        @pl.when(i * size >= half)
        def _():
            other_ref[pl.ds(pl.multiple_of(i * size - half, size), size), :] = part

    keep_act = pltpu.make_async_copy(act_ref, act_out, sems.at[0])
    keep_act.start()
    keep_pre = pltpu.make_async_copy(pre_ref, pre_out, sems.at[1])
    keep_pre.start()
    keep_act.wait()
    keep_pre.wait()


def expert_rows(row_chunk, up_chunk, w_in, w_out, firsts, rests):
    count, width = row_chunk.shape
    m = len(firsts)
    hidden = (m + 1) * w_in.shape[1]
    anywhere = pl.BlockSpec(memory_space=pl.ANY)
    return pl.pallas_call(
        functools.partial(expert_kernel, m=m),
        out_shape=[shaped((count // 2, width), BF16)] * 2 + [shaped((count, hidden), BF16)] * 2,
        in_specs=[VMEM] * (4 + 2 * m),
        out_specs=[VMEM] * 2 + [anywhere] * 2,
        scratch_shapes=[
            pltpu.VMEM((width, hidden), BF16),
            pltpu.VMEM((hidden, width), BF16),
            pltpu.VMEM((count, hidden), BF16),
            pltpu.VMEM((count, hidden), BF16),
            pltpu.SemaphoreType.DMA((2,)),
        ],
        compiler_params=params(40),
        cost_estimate=cost(6 * count * width * hidden, 4 * width * hidden + 8 * count * width),
    )(row_chunk, up_chunk, w_in, w_out, *firsts, *rests)


def turn_kernel(ids_ref, *refs, n, owners):
    backs, mixed = refs[:owners], refs[owners : owners + n]
    places_ref, hidden_ref, up_ref, inv_ref, gain_ref, w_ref = refs[owners + n : owners + n + 6]
    grad_ref, part_ref, mine_ref, theirs_ref, branch_ref, full_ref, mixed_ref = refs[owners + n + 6 :]
    group = part_ref.shape[2]
    width = hidden_ref.shape[1]
    grad_rows = None
    for k in range(owners):
        term = matmul(places_ref[k], backs[k][...])
        grad_rows = term if grad_rows is None else grad_rows + term
    hidden = hidden_ref[...]
    inverse = inv_ref[...]
    scaled = grad_rows * gain_ref[...]
    inner = jnp.mean(scaled * hidden, axis=-1, keepdims=True)
    grad = up_ref[...].astype(F32) + inverse * scaled - hidden * (inverse**3 * inner)
    grad_ref[...] = grad
    branch_ref[...] = grad.astype(BF16)
    for r in range(n):
        at = pl.ds(pl.multiple_of((ids_ref[0] ^ r) * group, group), group)
        part_ref[r] = matmul_nt(branch_ref[...], w_ref[at, :]).astype(BF16)
    sums = jnp.sum(grad_rows * hidden * inverse, axis=0, keepdims=True)
    blocks = width // (2 * PAIR)
    piece = group // owners
    for r in range(n):
        mixed_ref[r] = mixed[r][...]

    @pl.loop(0, n)
    def _(r):
        full_ref[...] = matmul_tn(mixed_ref[r], branch_ref[...])
        for s, out_ref in ((0, mine_ref), (1, theirs_ref)):
            for k in range(owners):
                row_at = pl.ds(pl.multiple_of((ids_ref[1] ^ k) * piece, piece), piece)
                for b in range(blocks):
                    col = pl.multiple_of(((ids_ref[2] ^ s) * blocks + b) * PAIR, PAIR)
                    at = pl.multiple_of(((r * owners + k) * blocks + b) * piece, piece)
                    out_ref[pl.ds(at, piece), :] = full_ref[row_at, pl.ds(col, PAIR)].astype(
                        out_ref.dtype
                    )
    size = mine_ref.shape[0]
    cols = width // PAIR
    lines = [sums[:, i * PAIR : (i + 1) * PAIR] for i in range(cols)]
    lines = jnp.concatenate(lines + [jnp.zeros((-cols % 16, PAIR), F32)], axis=0)
    theirs_ref[size : size + lines.shape[0], :] = lines.astype(BF16)


def turn(ids, backs, mixed, places, hidden, up, inverse, gain, w_out):
    rows, width = hidden.shape
    n = len(mixed)
    size = width * width // (2 * PAIR)
    extra = -(-width // PAIR // 16) * 16
    return pl.pallas_call(
        functools.partial(turn_kernel, n=n, owners=len(backs)),
        out_shape=(
            shaped((rows, width), F32),
            shaped((n, rows, width // n), BF16),
            shaped((size, PAIR), F32),
            shaped((size + extra, PAIR), BF16),
        ),
        in_specs=[SMEM] + [VMEM] * (len(backs) + n + 6),
        out_specs=(VMEM,) * 4,
        scratch_shapes=[pltpu.VMEM((rows, width), BF16), pltpu.VMEM((width // n, width), F32), pltpu.VMEM((n, rows, width // n), BF16)],
        compiler_params=params(32),
        cost_estimate=cost(4 * rows * width * (width + rows), 10 * width * width),
    )(ids, *backs, *mixed, places, hidden, up, inverse, gain, w_out)


def weight_grad_kernel(*refs, chunks, sizes):
    a_refs = refs[:chunks]
    b_refs = refs[chunks : 2 * chunks]
    outs = refs[2 * chunks :]
    total = None
    for a_ref, b_ref in zip(a_refs, b_refs):
        term = matmul_tn(a_ref[...], b_ref[...])
        total = term if total is None else total + term
    at = 0
    for out_ref, size in zip(outs, sizes):
        out_ref[...] = total[:, at : at + size].astype(out_ref.dtype)
        at += size


def weight_grads(row_chunks, per_chunk, sizes):
    width = row_chunks[0].shape[1]
    tile = 256
    total = sum(chunk.shape[0] for chunk in row_chunks)
    return pl.pallas_call(
        functools.partial(weight_grad_kernel, chunks=len(row_chunks), sizes=sizes),
        out_shape=[shaped((width, size), BF16 if i else F32) for i, size in enumerate(sizes)],
        grid=(width // tile,),
        in_specs=[pl.BlockSpec((chunk.shape[0], tile), lambda i: (0, i)) for chunk in row_chunks]
        + [pl.BlockSpec(value.shape, lambda i: (0, 0)) for value in per_chunk],
        out_specs=[pl.BlockSpec((tile, size), lambda i: (i, 0)) for size in sizes],
        compiler_params=params(40),
        cost_estimate=cost(2 * width * sum(sizes) * total, 8 * width * sum(sizes)),
    )(*row_chunks, *per_chunk)


def weight_out_kernel(*refs, chunks, sizes, tile):
    acts = refs[:chunks]
    ups = refs[chunks : 2 * chunks]
    outs = refs[2 * chunks :]
    total = None
    for act, up in zip(acts, ups):
        term = matmul_tn(act[...], up[...])
        total = term if total is None else total + term
    first = 0
    for out_ref, size in zip(outs, sizes):
        steps = size // tile

        @pl.when((pl.program_id(0) >= first) & (pl.program_id(0) < first + steps))
        def _():
            out_ref[...] = total.astype(out_ref.dtype)

        first += steps


def weight_grads_out(acts, up_chunks, sizes):
    width = up_chunks[0].shape[1]
    tile = min(256, min(sizes))
    total = sum(chunk.shape[0] for chunk in up_chunks)
    specs = []
    first = 0
    for size in sizes:
        steps = size // tile
        specs.append(
            pl.BlockSpec(
                (tile, width), lambda i, first=first, steps=steps: (jnp.clip(i - first, 0, steps - 1), 0)
            )
        )
        first += steps
    return pl.pallas_call(
        functools.partial(weight_out_kernel, chunks=len(acts), sizes=sizes, tile=tile),
        out_shape=[shaped((size, width), BF16 if i else F32) for i, size in enumerate(sizes)],
        grid=(first,),
        in_specs=[pl.BlockSpec((act.shape[0], tile), lambda i: (0, i)) for act in acts]
        + [pl.BlockSpec(chunk.shape, lambda i: (0, 0)) for chunk in up_chunks],
        out_specs=specs,
        compiler_params=params(40),
        cost_estimate=cost(2 * width * sum(sizes) * total, 8 * width * sum(sizes)),
    )(*acts, *up_chunks)


def produce_kernel(*refs, chunks, m, sizes):
    acts = refs[:chunks]
    w_out = refs[chunks]
    rests = refs[chunks + 1 : chunks + 1 + m]
    own_ref, other_ref, out_ref = refs[chunks + 1 + m :]
    units, width = w_out.shape
    out_ref[:units, :] = w_out[...]
    for i in range(m):
        cols = slice((i + 1) * units, (i + 2) * units)
        place_columns(out_ref, cols, rests[i], units)
    at = 0
    for c in range(chunks):
        size = sizes[c]

        @pl.loop(0, 2)
        def _(h):
            here = pl.ds(pl.multiple_of(h * 2 * size, 2 * size), 2 * size)
            total = matmul(acts[c][here, :], out_ref[...]).astype(BF16)

            @pl.when(h == 0)
            def _():
                for b in range(2):
                    own_ref[b, at : at + size, :] = total[b * size : (b + 1) * size]

            @pl.when(h == 1)
            def _():
                for b in range(2):
                    other_ref[b, at : at + size, :] = total[b * size : (b + 1) * size]

        at += size


def produce(acts, w_out, rests, sizes):
    width = w_out.shape[1]
    hidden = acts[0].shape[1]
    shape = (2, sum(sizes), width)
    return pl.pallas_call(
        functools.partial(produce_kernel, chunks=len(acts), m=len(rests), sizes=sizes),
        out_shape=(shaped(shape, BF16), shaped(shape, BF16)),
        in_specs=[VMEM] * (len(acts) + 1 + len(rests)),
        out_specs=(VMEM, VMEM),
        scratch_shapes=[pltpu.VMEM((hidden, width), BF16)],
        compiler_params=params(40),
        cost_estimate=cost(
            8 * sum(sizes) * width * hidden, 2 * hidden * width + 16 * sum(sizes) * width
        ),
    )(*acts, w_out, *rests)


def backward_kernel(
    ids_ref,
    starts_ref,
    normed_ref,
    q_ref,
    k_ref,
    v_ref,
    att_ref,
    tot_ref,
    g_ref,
    *refs,
    n,
    rows,
    owners,
):
    out_ref, mine_ref, theirs_ref, dq_ref, do_ref, sh_ref, full_ref = refs
    rank = ids_ref[0]
    pairs = q_ref.shape[1] // PAIR
    low = lax.broadcasted_iota(jnp.int32, (rows, PAIR), 1) < HEAD
    k_iota = lax.broadcasted_iota(jnp.int32, (rows, rows), 0)
    q_iota = lax.broadcasted_iota(jnp.int32, (rows, rows), 1)
    zero = jnp.zeros((), BF16)

    def both(value):
        return jnp.where(low, value, zero), jnp.where(low, zero, value)

    @pl.loop(0, pairs)
    def _(p):
        cols = pl.ds(pl.multiple_of(p * PAIR, PAIR), PAIR)
        for i in range(n):
            here = slice(i * rows, (i + 1) * rows)
            at = pl.ds(pl.multiple_of((rank ^ i) * rows, rows), rows)
            scaled = g_ref[at, cols].astype(F32) / tot_ref[here, cols]
            do_ref[here, :] = scaled.astype(BF16)
            turned = (scaled * att_ref[here, cols]).T
            sh_ref[0:1, here] = jnp.sum(turned[:HEAD], axis=0, keepdims=True)
            sh_ref[1:2, here] = jnp.sum(turned[HEAD:], axis=0, keepdims=True)
        for j in range(n):
            k_at = slice(j * rows, (j + 1) * rows)
            k2 = k_ref[k_at, cols]
            v2 = v_ref[k_at, cols]
            ks = both(k2)
            dk = None
            dv = None
            for i in range(j, n):
                here = slice(i * rows, (i + 1) * rows)
                qs = both(q_ref[here, cols])
                dos = both(do_ref[here, :])
                seen = k_iota + j * rows >= starts_ref[:, here]
                if i == j:
                    seen = seen & (k_iota <= q_iota)
                dq = None
                for h in range(2):
                    weights = jnp.where(seen, jnp.exp(matmul_nt(k2, qs[h])), 0.0)
                    slope = matmul_nt(v2, dos[h]) - sh_ref[h : h + 1, here]
                    ds = (weights * slope).astype(BF16)
                    dv_part = matmul(weights.astype(BF16), dos[h])
                    dk_part = matmul(ds, qs[h])
                    dq_part = matmul_tn(ds, ks[h])
                    dv = dv_part if dv is None else dv + dv_part
                    dk = dk_part if dk is None else dk + dk_part
                    dq = dq_part if dq is None else dq + dq_part
                if j == 0:
                    dq_ref[here, :] = dq
                else:
                    dq_ref[here, :] += dq
            out_ref[j, 1, :, cols] = dk.astype(BF16)
            out_ref[j, 2, :, cols] = dv.astype(BF16)
            out_ref[j, 0, :, cols] = (dq_ref[k_at, :] * score_scale).astype(BF16)

    @pl.loop(0, 3)
    def _(part):
        total = None
        for j in range(n):
            term = matmul_tn(normed_ref[j * rows : (j + 1) * rows, :], out_ref[j, part])
            total = term if total is None else total + term
        full_ref[part] = total

    piece = full_ref.shape[1] // (2 * owners)
    for s, to_ref in ((0, mine_ref), (1, theirs_ref)):
        for k in range(owners):
            row = ((ids_ref[2] ^ s) * owners + (ids_ref[1] ^ k)) * piece
            row_at = pl.ds(pl.multiple_of(row, piece), piece)
            for part in range(3):
                for p in range(pairs):
                    at = (part * pairs + p) * piece
                    to_ref[k, at : at + piece, :] = full_ref[
                        part, row_at, p * PAIR : (p + 1) * PAIR
                    ].astype(to_ref.dtype)


def attend_backward(ids, starts, normed, q, k, v, att, tot, g, n, owners):
    length, width = normed.shape
    group = q.shape[1]
    rows = length // n
    count = n * (n + 1) // 2 * (group // HEAD)
    size = (owners, width // (2 * owners) * 3 * group // PAIR, PAIR)
    return pl.pallas_call(
        functools.partial(backward_kernel, n=n, rows=rows, owners=owners),
        out_shape=(
            shaped((n, 3, rows, group), BF16),
            shaped(size, F32),
            shaped(size, BF16),
        ),
        in_specs=[SMEM] + [VMEM] * 8,
        out_specs=(VMEM,) * 3,
        scratch_shapes=[
            pltpu.VMEM((length, PAIR), F32),
            pltpu.VMEM((length, PAIR), BF16),
            pltpu.VMEM((8, length), F32),
            pltpu.VMEM((3, width, group), F32),
        ],
        compiler_params=params(48),
        cost_estimate=cost(
            count * rows * rows * PAIR * 10 + 6 * length * width * group,
            length * group * 24 + 2 * length * width + 9 * width * group,
            count * rows * rows,
        ),
    )(ids, starts, normed, q, k, v, att, tot, g)


def join_kernel(*refs, owners):
    mine_ref, got_ref, out_ref, near_ref = refs[:4]
    count = len(refs) - 4 - owners - 1
    others = refs[4 : 4 + count]
    own_ref, gain_ref = refs[4 + count : 6 + count]
    sent = refs[6 + count :]
    rows = mine_ref.shape[1]
    size = out_ref.shape[0]
    tall = size // owners
    out = out_ref[...]
    gains = [near_ref[...].astype(F32)]
    for other in others:
        out = out + other[:size, :].astype(F32)
        gains.append(other[size:, :].astype(F32))
    while len(gains) > 1:
        gains = [gains[i] + gains[i + 1] for i in range(0, len(gains), 2)]
    gain = gains[0].astype(BF16)
    gain_ref[...] = gain
    for k in range(owners):
        total = mine_ref[k] + got_ref[k].astype(F32)
        part = out[k * tall : (k + 1) * tall]
        if k == 0:
            own_ref[:rows, :] = total
            own_ref[rows:, :] = part
        else:
            sent[k - 1][:rows, :] = total.astype(BF16)
            sent[k - 1][rows : rows + tall, :] = part.astype(BF16)
            sent[k - 1][rows + tall :, :] = gain


def join_sums(mine, got, out_total, gain, others):
    owners, rows, _ = mine.shape
    size = out_total.shape[0]
    tall = rows + size // owners
    extra = gain.shape[0]
    return pl.pallas_call(
        functools.partial(join_kernel, owners=owners),
        out_shape=[shaped((tall, PAIR), F32), shaped((extra, PAIR), BF16)]
        + [shaped((tall + extra, PAIR), BF16)] * (owners - 1),
        in_specs=[VMEM] * (4 + len(others)),
        out_specs=[VMEM] * (owners + 1),
        compiler_params=params(24),
        cost_estimate=cost(owners * tall * PAIR * 4, owners * tall * PAIR * 10),
    )(mine, got, out_total, gain, *others)


def dense_out_kernel(ids_ref, near_ref, *refs, counts, s, n, owners, pairs, width):
    far = refs[: sum(counts)]
    w_ref = refs[sum(counts)]
    out_ref, dense_ref, sum_ref, held_ref, sems = refs[-5:]
    group = pairs * PAIR
    rows = out_ref.shape[0]
    tall = held_ref.shape[2]
    step = pl.program_id(0)

    def copies(k):
        found = []
        low, high = (k - 1) * tall, k * tall
        for r in range(n):
            if k == 0:
                source, target = near_ref.at[ids_ref[0] ^ r], held_ref.at[0, r]
                found.append(pltpu.make_async_copy(source, target, sems.at[0, r, 0]))
                continue
            begin = 0
            first = sum(counts[:r])
            for i, part in enumerate(far[first : first + counts[r]]):
                end = begin + part.shape[0]
                lo, hi = max(low, begin), min(high, end)
                if lo < hi:
                    source = part.at[pl.ds(lo - begin, hi - lo)]
                    target = held_ref.at[k % 2, r, pl.ds(lo - low, hi - lo)]
                    found.append(pltpu.make_async_copy(source, target, sems.at[k % 2, r, i]))
                begin = end
        return found

    @pl.when(step == 0)
    def _():
        for copy in copies(0):
            copy.start()

    for k in range(owners):

        @pl.when(step == k)
        def _():
            if k + 1 < owners:
                for copy in copies(k + 1):
                    copy.start()
            for copy in copies(k):
                copy.wait()

    slot = lax.rem(step, 2)
    out_rows = group // owners
    blocks = width // (2 * PAIR)
    for r in range(n):
        g = ids_ref[0] ^ r
        for part in range(3):
            for p in range(pairs):
                to = pl.multiple_of(part * width + g * group + p * PAIR, PAIR)
                at = (part * pairs + p) * rows
                out_ref[:, pl.ds(to, PAIR)] = held_ref[slot, r, at : at + rows, :].astype(F32)
        row = g * group + (ids_ref[1] ^ step) * out_rows
        row_at = pl.ds(pl.multiple_of(row, out_rows), out_rows)
        for b in range(blocks):
            at = 3 * pairs * rows + b * out_rows
            dense_ref[row_at, b * PAIR : (b + 1) * PAIR] = held_ref[
                slot, r, at : at + out_rows, :
            ].astype(F32)
    total = None
    for at in range(0, 3 * width, PAIR):
        term = out_ref[:, at : at + PAIR] * w_ref[:, at : at + PAIR].astype(F32)
        total = term if total is None else total + term
    sum_ref[...] = total


def dense_out(ids, near, far, w_qkv, s, owners, before=()):
    width = w_qkv.shape[0]
    n, tall, _ = near.shape
    rows = width // (2 * owners)
    anywhere = pl.BlockSpec(memory_space=pl.ANY)
    counts = [len(parts) for parts in far]
    parts = [part for line in far for part in line]

    def place(k, ids_ref):
        return ((ids_ref[2] ^ s) * owners + (ids_ref[1] ^ k), 0)

    return pl.pallas_call(
        functools.partial(
            dense_out_kernel,
            counts=counts,
            s=s,
            n=n,
            owners=owners,
            pairs=width // n // PAIR,
            width=width,
        ),
        out_shape=(
            shaped((width, 3 * width), F32),
            shaped((width, width), F32),
            shaped((width, PAIR), F32),
        ),
        grid_spec=pltpu.PrefetchScalarGridSpec(
            num_scalar_prefetch=1,
            grid=(owners,),
            in_specs=[anywhere] * (1 + len(parts))
            + [pl.BlockSpec((rows, 3 * width), place)]
            + [anywhere] * len(before),
            out_specs=(
                pl.BlockSpec((rows, 3 * width), place),
                pl.BlockSpec((width, width // 2), lambda k, ids_ref: (0, ids_ref[2] ^ s)),
                pl.BlockSpec((rows, PAIR), place),
            ),
            scratch_shapes=[
                pltpu.VMEM((2, n, tall, PAIR), BF16),
                pltpu.SemaphoreType.DMA((2, n, 2)),
            ],
        ),
        input_output_aliases={3 + len(parts) + i: i for i in range(len(before))},
        compiler_params=params(40),
        cost_estimate=cost(3 * width * width, 16 * width * width),
    )(ids, near, *parts, w_qkv, *before)


def back_kernel(d_ref, w_ref, x_ref, inv_ref, gain_ref, grad_ref, out_ref):
    n, _, _, group = d_ref.shape
    width = x_ref.shape[1]
    out_ref[...] = jnp.zeros_like(out_ref)

    @pl.loop(0, n)
    def _(g):
        for part in range(3):
            at = pl.ds(pl.multiple_of(part * width + g * group, group), group)
            out_ref[...] += matmul_nt(d_ref[g, part], w_ref[:, at])

    x = x_ref[...].astype(F32)
    inverse = inv_ref[...]
    scaled = out_ref[...] * gain_ref[...]
    inner = jnp.mean(scaled * x, axis=-1, keepdims=True)
    out_ref[...] = grad_ref[...] + inverse * scaled - x * (inverse**3 * inner)


def back_to_tokens(d, w_qkv, x, inverse, gain, grad_hidden):
    rows, width = x.shape
    return pl.pallas_call(
        back_kernel,
        out_shape=shaped((rows, width), F32),
        in_specs=[VMEM] * 6,
        out_specs=VMEM,
        compiler_params=params(32),
        cost_estimate=cost(6 * rows * width * width, 10 * width * width),
    )(d, w_qkv, x, inverse, gain, grad_hidden)


def on_device(
    tokens,
    out_grad,
    token_ids,
    hash_table,
    doc_lengths,
    w_qkv,
    w_out,
    gain_attn,
    gain_ffn,
    expert_in,
    expert_out,
):
    rows = tokens.shape[1]
    width = tokens.shape[2]
    n = lax.axis_size("ctx")
    owners = lax.axis_size("expert")
    rank = lax.axis_index("ctx")
    z = lax.axis_index("expert")
    core = lax.axis_index("dp")
    group = width // n
    pairs = group // PAIR
    length = n * rows
    ids = jnp.stack([rank, z, core]).astype(jnp.int32)

    inputs_low = tokens[0]

    capacity = rows * 5 // (4 * owners)
    slots = owners * capacity
    chosen = jnp.take(hash_table, token_ids[0], axis=0)
    order = jnp.arange(rows, dtype=jnp.int32)
    ahead = (chosen[:, None] == chosen[None, :]) & (order[None, :] < order[:, None])
    slot = jnp.sum(ahead.astype(jnp.int32), axis=1)
    code = (chosen ^ z) * capacity + slot
    picks = (jnp.arange(slots, dtype=jnp.int32)[:, None] == code[None, :]).astype(BF16)
    spots = jnp.arange(slots, dtype=jnp.int32).reshape(owners, 1, capacity)
    places = (code[None, :, None] == spots).astype(BF16)

    def send_rows(matrix):
        far = {}
        for k in list(range(owners // 2, owners)) + list(range(1, owners // 2)):
            far[k] = swap(matrix[k * capacity : (k + 1) * capacity], "expert", k)
        return [matrix[:capacity]] + [far[k] for k in range(1, owners)]

    def spread(piece, before=()):
        line = after(jnp.concatenate([piece, swap(piece, "ctx", 1)], axis=0), *before)
        return jnp.concatenate([line, swap(line, "dp", 1)], axis=0)

    upstream = out_grad[0]
    w_in, w_o = expert_in[0], expert_out[0]
    units = w_in.shape[1]
    top = width * 3 // 4
    upper = w_in[:top]
    up_rows = matmul(picks, upstream).astype(BF16)
    up_arrived = send_rows(up_rows)
    late_low = after(inputs_low, up_rows)
    blocks = [inputs_low] + [
        swap(inputs_low if r & (r - 1) == 0 else late_low, "ctx", r) for r in range(1, n)
    ]
    chunks = [list(range(0, owners // 2)), list(range(owners // 2, owners))]

    doc_ends = jnp.cumsum(doc_lengths[0])
    spots = jnp.arange(length, dtype=jnp.int32)
    later = doc_ends[:, None] > spots[None, :]
    ends = jnp.min(jnp.where(later, doc_ends[:, None], length), axis=0)[None, :].astype(jnp.int32)
    starts = jnp.max(jnp.where(later, 0, doc_ends[:, None]), axis=0)[None, :].astype(jnp.int32)
    normed, inverse_one, q_own, k_own, v_own, mixed_own, att, tot = attend_forward(
        ids, ends, gain_attn[None, :], blocks, w_qkv, n
    )

    rest = jnp.concatenate(
        [w_in[top:]] + [w_o[:, at : at + units] for at in range(0, width, units)], axis=0
    )
    first = after(upper, *blocks[1:])
    firsts = [swap(first, "ctx", m << 1) for m in range(1, n // 2)]
    mixed_own = after(mixed_own, firsts)
    up_line = jnp.concatenate(after(up_arrived, mixed_own), axis=0)
    up_line = jnp.concatenate([up_line[None], swap(up_line, "ctx", 1)[None]], axis=0)
    up_all = jnp.concatenate([up_line[None], swap(up_line, "dp", 1)[None]], axis=0)
    up_chunks = [
        up_all[:, :, c[0] * capacity : (c[-1] + 1) * capacity].reshape(-1, width) for c in chunks
    ]

    mixed_sent = [lax.dynamic_slice_in_dim(mixed_own, (rank ^ r) * rows, rows, 0) for r in range(n)]
    mixed_parts = [mixed_sent[0]] + [swap(mixed_sent[r], "ctx", r) for r in range(1, n)]
    rest = after(rest, mixed_parts)
    rests = [swap(rest, "ctx", m << 1) for m in range(1, n // 2)]
    hidden, inverse_two, row_sent = middle(
        ids, mixed_parts, w_out, inputs_low, gain_ffn[None, :], picks
    )

    near, far = chunks
    arrived = {0: row_sent[:capacity]}
    for k in near[1:] + far:
        arrived[k] = swap(row_sent[k * capacity : (k + 1) * capacity], "expert", k)
    near_rows = jnp.concatenate([arrived[k] for k in near], axis=0)
    far_rows = after(jnp.concatenate([arrived[k] for k in far], axis=0), near_rows)
    row_chunks = [spread(near_rows), spread(far_rows, rests)]
    sizes = [units] * (n // 2)
    acts = []
    grad_pres = []
    far_back = {}
    x_sent = []
    for c, row_chunk, up_chunk in list(zip(chunks, row_chunks, up_chunks))[::-1]:
        if acts:
            row_chunk = after(row_chunk, theirs)
        mine, theirs, act, grad_pre = expert_rows(
            row_chunk, up_chunk, w_in, w_o, firsts, rests
        )
        acts.append(act)
        grad_pres.append(grad_pre)
        line = mine.astype(F32) + swap(theirs, "dp", 1).astype(F32)
        half = line.shape[0] // 2
        x_sent.append(line[half:].astype(BF16))
        own = (line[:half] + swap(x_sent[-1], "ctx", 1).astype(F32)).astype(BF16)
        for i, k in reversed(list(enumerate(c))):
            piece = own[i * capacity : (i + 1) * capacity]
            far_back[k] = piece if k == 0 else swap(piece, "expert", k)
    back = [far_back[k] for k in range(owners)]
    acts, grad_pres = acts[::-1], grad_pres[::-1]
    last_own = own

    grads_out = weight_grads_out(after(acts, x_sent[0]), up_chunks, sizes)

    def others(grads):
        return [swap(grads[i], "ctx", i << 1) for i in range(1, len(grads))]

    out_others = others(grads_out)
    made, made_other = produce(
        after(acts, x_sent[1]), w_o, rests, [len(c) * capacity for c in chunks]
    )
    grads_in = weight_grads(row_chunks, after(grad_pres, x_sent[1]), sizes)
    back = after(back, made, grads_in)
    made_other = swap(made_other, "dp", 1)

    grad_hidden, grad_parts, mine, theirs = turn(
        ids, back, mixed_parts, places, hidden, upstream, inverse_two, gain_ffn[None, :], w_out
    )
    grad_parts = after(grad_parts, out_others)
    grad_att_own = jnp.concatenate(
        [grad_parts[0]] + [swap(grad_parts[r], "ctx", r) for r in range(1, n)], axis=0
    )

    def add_others(own, parts):
        for part in parts:
            own = own + part.astype(F32)
        return own

    cols = width // PAIR
    size = mine.shape[0]
    got = swap(theirs, "dp", 1)
    gain_low = (theirs[size:].astype(F32) + got[size:].astype(F32)).astype(BF16)
    total = mine + got[:size].astype(F32)
    piece = size // n
    out_sent = [
        jnp.concatenate([total[r * piece : (r + 1) * piece].astype(BF16), gain_low], axis=0)
        for r in range(1, n)
    ]
    out_sent = after(out_sent, grad_att_own)
    out_got = [swap(out_sent[r - 1], "ctx", r) for r in range(1, n)]

    held = after(grad_att_own, out_sent)
    d_own, mine, theirs = attend_backward(
        ids, starts, normed, q_own, k_own, v_own, att, tot, held, n, owners
    )
    d_own, theirs = after((d_own, theirs), out_got)
    d_pieces = exchange(d_own, "ctx")
    in_others = others(after(grads_in, d_pieces))
    made_line = made.astype(F32) + after(made_other, d_pieces).astype(F32)
    sent = made_line[1].astype(BF16)
    made_own = (made_line[0] + swap(sent, "ctx", 1).astype(F32)).astype(BF16)
    order = list(range(owners // 2, owners)) + list(range(1, owners // 2))
    own, gain_low, *messages = join_sums(
        mine, swap(theirs, "dp", 1), total[: total.shape[0] // n], gain_low, out_got
    )
    tall = own.shape[0]
    got = {k: swap(messages[k - 1], "expert", k) for k in order}
    piece = own
    gains = [gain_low.astype(F32)]
    for k in range(owners - 1, 0, -1):
        piece = piece + got[k][:tall].astype(F32)
    for k in range(1, owners):
        gains.append(got[k][tall:].astype(F32))
    while len(gains) > 1:
        gains = [gains[i] + gains[i + 1] for i in range(0, len(gains), 2)]
    grad_gain_ffn = gains[0][:cols].reshape(width)
    piece = piece.astype(BF16)
    arrived = {k: swap(piece, "expert", k) for k in order}
    near_lines = spread_to(piece, "ctx")
    line = jnp.concatenate([arrived[k] for k in range(1, owners)], axis=0)
    line = after(line, in_others, made_own, near_lines)
    if n == 4:
        half = line.shape[0] // 2
        one, two = swap(line, "ctx", 1), swap(line, "ctx", 2)
        sent = (one[:half], two[half:])
        last = [swap(sent[0], "ctx", 2), swap(sent[1], "ctx", 1)]
        far_lines = [[line], [one], [two], last]
        in_others, out_others, d_pieces = after((in_others, out_others, d_pieces), sent)
    else:
        far_lines = [[line]] + [[swap(line, "ctx", r)] for r in range(1, n)]
    grad_inputs = back_to_tokens(
        d_pieces,
        w_qkv,
        inputs_low,
        inverse_one,
        gain_attn[None, :],
        grad_hidden,
    )
    grad_expert_out = add_others(grads_out[0], out_others)
    grad_expert_in = add_others(grads_in[0], in_others)
    returned = jnp.concatenate(send_rows(after(made_own, line)), axis=0)
    block_out = (
        hidden + matmul(places.transpose(1, 0, 2).reshape(rows, slots), returned)
    ).astype(BF16)
    near_other = swap(near_lines, "dp", 1)
    far_lines[n - 1] = after(
        far_lines[n - 1], block_out, grad_inputs, grad_expert_out, grad_expert_in, near_other
    )
    first = dense_out(ids, near_lines, far_lines, w_qkv, 0, owners)
    far_other = [[swap(part, "dp", 1) for part in parts] for parts in far_lines]
    grad_w_qkv, grad_w_out, gain_sums = dense_out(
        ids, near_other, far_other, w_qkv, 1, owners, first
    )
    grad_gain_attn = jnp.sum(gain_sums, axis=1) / gain_attn

    return (
        block_out[None],
        grad_inputs[None],
        grad_w_qkv,
        grad_w_out,
        grad_gain_attn,
        grad_gain_ffn,
        grad_expert_in[None],
        grad_expert_out[None],
    )


def solution(mesh):
    rows = P(("expert", "dp"), "ctx", None)
    placed = (
        rows,
        rows,
        P(("expert", "dp"), "ctx"),
        P(),
        P(("expert", "dp"), None),
        P(),
        P(),
        P(),
        P(),
        P("expert", None, ("ctx", "dp")),
        P("expert", ("ctx", "dp"), None),
    )
    return jax.shard_map(
        on_device,
        mesh=mesh,
        in_specs=placed,
        out_specs=(
            rows,
            rows,
            P(),
            P(),
            P(),
            P(),
            P("expert", None, ("ctx", "dp")),
            P("expert", ("ctx", "dp"), None),
        ),
        check_vma=False,
    )
```

```python
import functools
import jax
import jax.numpy as jnp
from jax import lax
from jax.experimental import pallas as pl
from jax.experimental.pallas import tpu as pltpu
from jax.sharding import PartitionSpec as P

HEADS = 16
HEAD = 64
PAIR = 2 * HEAD

eps = 1e-06
score_scale = 0.125
F32 = jnp.float32
BF16 = jnp.bfloat16
VMEM = pl.BlockSpec(memory_space=pltpu.VMEM)
SMEM = pl.BlockSpec(memory_space=pltpu.SMEM)
shaped = jax.ShapeDtypeStruct


def swap(value, axis, bits):
    size = lax.axis_size(axis)
    return lax.ppermute(value, axis, [(i, i ^ bits) for i in range(size)])


def exchange(value, axis):
    return lax.all_to_all(value, axis, split_axis=0, concat_axis=0, tiled=True)


def spread_to(value, axis):
    return exchange(jnp.broadcast_to(value[None], (lax.axis_size(axis),) + value.shape), axis)


def after(value, *others):
    return lax.optimization_barrier((value,) + others)[0]


def matmul(a, b):
    return jnp.dot(a, b, preferred_element_type=F32)


def matmul_nt(a, b):
    return lax.dot_general(a, b, (((1,), (1,)), ((), ())), preferred_element_type=F32)


def matmul_tn(a, b):
    return lax.dot_general(a, b, (((0,), (0,)), ((), ())), preferred_element_type=F32)


def params(mib):
    return pltpu.CompilerParams(vmem_limit_bytes=mib << 20)


def cost(flops, moved, transcendentals=0):
    return pl.CostEstimate(
        flops=int(flops / 4), bytes_accessed=int(moved / 4), transcendentals=int(transcendentals / 4)
    )


def distances(bits):
    found = [0]
    for bit in reversed(bits):
        found = found + [value ^ bit for value in found]
    return found


def gelu_parts(pre):
    c = 0.7978845608028654
    square = pre * pre
    t = jnp.tanh(c * (pre + 0.044715 * pre * square))
    half = 0.5 * (1.0 + t)
    slope = half + 0.5 * pre * (1.0 - t * t) * (c * (1.0 + 3.0 * 0.044715 * square))
    return pre * half, slope


def forward_kernel(ids_ref, ends_ref, gain_ref, *refs, n, rows):
    blocks = refs[:n]
    weights = refs[n : n + 3]
    normed_ref, inv_ref, q_ref, k_ref, v_ref, mixed_ref, att_ref, tot_ref = refs[n + 3 :]
    rank = ids_ref[0]
    pairs = mixed_ref.shape[1] // PAIR
    for r in range(n):
        x = blocks[r][...].astype(F32)
        inverse = lax.rsqrt(jnp.mean(x * x, axis=-1, keepdims=True) + eps)
        if r == 0:
            inv_ref[...] = inverse
        here = pl.ds(pl.multiple_of((rank ^ r) * rows, rows), rows)
        normed = (x * inverse * gain_ref[...]).astype(BF16)
        normed_ref[here, :] = normed
        q_ref[here, :] = (matmul(normed, weights[0][...]) * score_scale).astype(BF16)
        k_ref[here, :] = matmul(normed, weights[1][...]).astype(BF16)
        v_ref[here, :] = matmul(normed, weights[2][...]).astype(BF16)
    low = lax.broadcasted_iota(jnp.int32, (rows, PAIR), 1) < HEAD
    q_iota = lax.broadcasted_iota(jnp.int32, (rows, rows), 0)
    k_iota = lax.broadcasted_iota(jnp.int32, (rows, rows), 1)
    one = jnp.ones((), BF16)
    zero = jnp.zeros((), BF16)

    @pl.loop(0, pairs)
    def _(p):
        out = pl.ds(pl.multiple_of(p * PAIR, PAIR), PAIR)
        for i in range(n):
            q_at = slice(i * rows, (i + 1) * rows)
            q2 = q_ref[q_at, out]
            qs = (jnp.where(low, q2, zero), jnp.where(low, zero, q2))
            sums = [None, None]
            for j in range(i + 1):
                k_at = slice(j * rows, (j + 1) * rows)
                k2 = k_ref[k_at, out]
                v2 = v_ref[k_at, out]
                vs = (jnp.where(low, v2, one), jnp.where(low, one, v2))
                seen = q_iota + i * rows < ends_ref[:, j * rows : (j + 1) * rows]
                if i == j:
                    seen = seen & (k_iota <= q_iota)
                for h in range(2):
                    w = jnp.where(seen, jnp.exp(matmul_nt(qs[h], k2)), 0.0).astype(BF16)
                    part = matmul(w, vs[h])
                    sums[h] = part if sums[h] is None else sums[h] + part
            total = jnp.where(low, pltpu.roll(sums[0], HEAD, 1), pltpu.roll(sums[1], HEAD, 1))
            att = jnp.where(low, sums[0], sums[1]) / total
            att_ref[q_at, out] = att
            mixed_ref[q_at, out] = att.astype(BF16)
            tot_ref[q_at, out] = total


def attend_forward(ids, ends, gain, blocks, w_qkv, n):
    rows, width = blocks[0].shape
    group = width // n
    length = n * rows
    count = n * (n + 1) // 2 * (group // HEAD)

    def whole(*shape):
        return pl.BlockSpec(shape, lambda s, ids_ref: (0, 0))

    def columns(part):
        return pl.BlockSpec((width, group), lambda s, ids_ref: (0, part * n + ids_ref[0]))

    own = (length, group)
    return pl.pallas_call(
        functools.partial(forward_kernel, n=n, rows=rows),
        out_shape=(
            shaped((length, width), BF16),
            shaped((rows, 1), F32),
            shaped(own, BF16),
            shaped(own, BF16),
            shaped(own, BF16),
            shaped(own, BF16),
            shaped(own, F32),
            shaped(own, F32),
        ),
        grid_spec=pltpu.PrefetchScalarGridSpec(
            num_scalar_prefetch=1,
            grid=(1,),
            in_specs=[whole(1, length), whole(1, width)]
            + [whole(rows, width)] * n
            + [columns(0), columns(1), columns(2)],
            out_specs=[whole(length, width), whole(rows, 1)] + [whole(*own)] * 6,
        ),
        compiler_params=params(48),
        cost_estimate=cost(
            count * rows * rows * PAIR * 4 + 6 * length * width * group,
            length * width * 4 + length * group * 16 + 6 * width * group,
            count * rows * rows,
        ),
    )(ids, ends, gain, *blocks, w_qkv, w_qkv, w_qkv)


def middle_kernel(ids_ref, *refs, n):
    parts = refs[:n]
    w_ref, x_ref, gain_ref, picks_ref, hidden_ref, inv_ref, sent_ref = refs[n:]
    group = parts[0].shape[1]
    hidden = x_ref[...].astype(F32)
    for r in range(n):
        at = pl.ds(pl.multiple_of((ids_ref[0] ^ r) * group, group), group)
        hidden = hidden + matmul(parts[r][...], w_ref[at, :])
    hidden_ref[...] = hidden
    inverse = lax.rsqrt(jnp.mean(hidden * hidden, axis=-1, keepdims=True) + eps)
    inv_ref[...] = inverse
    low = (hidden * inverse * gain_ref[...]).astype(BF16)
    sent_ref[...] = matmul(picks_ref[...], low).astype(BF16)


def middle(ids, parts, w_out, x, gain, picks):
    rows, width = x.shape
    slots = picks.shape[0]
    return pl.pallas_call(
        functools.partial(middle_kernel, n=len(parts)),
        out_shape=(
            shaped((rows, width), F32),
            shaped((rows, 1), F32),
            shaped((slots, width), BF16),
        ),
        in_specs=[SMEM] + [VMEM] * (len(parts) + 4),
        out_specs=(VMEM, VMEM, VMEM),
        compiler_params=params(24),
        cost_estimate=cost(2 * rows * width * (width + slots), 6 * width * width),
    )(ids, *parts, w_out, x, gain, picks)


def place_columns(out_ref, where, rest_ref, units):
    width = out_ref.shape[1]
    for b in range(width // units):
        at = rest_ref.shape[0] - width + b * units
        out_ref[where, b * units : (b + 1) * units] = rest_ref[at : at + units]


def expert_kernel(*refs, m):
    row_ref, up_ref, w_in, w_out = refs[:4]
    firsts, rests = refs[4 : 4 + m], refs[4 + m : 4 + 2 * m]
    own_ref, other_ref, act_out, pre_out, in_ref, out_ref, act_ref, pre_ref, sems = refs[4 + 2 * m :]
    width, units = w_in.shape
    in_ref[:, :units] = w_in[...]
    out_ref[:units, :] = w_out[...]
    for i in range(m):
        cols = slice((i + 1) * units, (i + 2) * units)
        top = firsts[i].shape[0]
        in_ref[:top, cols] = firsts[i][...]
        in_ref[top:, cols] = rests[i][: width - top]
        place_columns(out_ref, cols, rests[i], units)
    half = own_ref.shape[0]
    size = half

    @pl.loop(0, 2 * half // size)
    def _(i):
        here = pl.ds(pl.multiple_of(i * size, size), size)
        value, slope = gelu_parts(matmul(row_ref[here, :], in_ref[...]))
        act_ref[here, :] = value.astype(BF16)
        grad_pre = (slope * matmul_nt(up_ref[here, :], out_ref[...])).astype(BF16)
        pre_ref[here, :] = grad_pre
        part = matmul_nt(grad_pre, in_ref[...]).astype(BF16)

        @pl.when(i * size < half)
        def _():
            own_ref[here, :] = part

        @pl.when(i * size >= half)
        def _():
            other_ref[pl.ds(pl.multiple_of(i * size - half, size), size), :] = part

    keep_act = pltpu.make_async_copy(act_ref, act_out, sems.at[0])
    keep_act.start()
    keep_pre = pltpu.make_async_copy(pre_ref, pre_out, sems.at[1])
    keep_pre.start()
    keep_act.wait()
    keep_pre.wait()


def expert_rows(row_chunk, up_chunk, w_in, w_out, firsts, rests):
    count, width = row_chunk.shape
    m = len(firsts)
    hidden = (m + 1) * w_in.shape[1]
    anywhere = pl.BlockSpec(memory_space=pl.ANY)
    return pl.pallas_call(
        functools.partial(expert_kernel, m=m),
        out_shape=[shaped((count // 2, width), BF16)] * 2 + [shaped((count, hidden), BF16)] * 2,
        in_specs=[VMEM] * (4 + 2 * m),
        out_specs=[VMEM] * 2 + [anywhere] * 2,
        scratch_shapes=[
            pltpu.VMEM((width, hidden), BF16),
            pltpu.VMEM((hidden, width), BF16),
            pltpu.VMEM((count, hidden), BF16),
            pltpu.VMEM((count, hidden), BF16),
            pltpu.SemaphoreType.DMA((2,)),
        ],
        compiler_params=params(40),
        cost_estimate=cost(6 * count * width * hidden, 4 * width * hidden + 8 * count * width),
    )(row_chunk, up_chunk, w_in, w_out, *firsts, *rests)


def turn_kernel(ids_ref, *refs, n, owners):
    backs, mixed = refs[:owners], refs[owners : owners + n]
    places_ref, hidden_ref, up_ref, inv_ref, gain_ref, w_ref = refs[owners + n : owners + n + 6]
    grad_ref, part_ref, mine_ref, theirs_ref, branch_ref, full_ref, mixed_ref = refs[owners + n + 6 :]
    group = part_ref.shape[2]
    width = hidden_ref.shape[1]
    grad_rows = None
    for k in range(owners):
        term = matmul(places_ref[k], backs[k][...])
        grad_rows = term if grad_rows is None else grad_rows + term
    hidden = hidden_ref[...]
    inverse = inv_ref[...]
    scaled = grad_rows * gain_ref[...]
    inner = jnp.mean(scaled * hidden, axis=-1, keepdims=True)
    grad = up_ref[...].astype(F32) + inverse * scaled - hidden * (inverse**3 * inner)
    grad_ref[...] = grad
    branch_ref[...] = grad.astype(BF16)
    for r in range(n):
        at = pl.ds(pl.multiple_of((ids_ref[0] ^ r) * group, group), group)
        part_ref[r] = matmul_nt(branch_ref[...], w_ref[at, :]).astype(BF16)
    sums = jnp.sum(grad_rows * hidden * inverse, axis=0, keepdims=True)
    blocks = width // (2 * PAIR)
    piece = group // owners
    for r in range(n):
        mixed_ref[r] = mixed[r][...]

    @pl.loop(0, n)
    def _(r):
        full_ref[...] = matmul_tn(mixed_ref[r], branch_ref[...])
        for s, out_ref in ((0, mine_ref), (1, theirs_ref)):
            for k in range(owners):
                row_at = pl.ds(pl.multiple_of((ids_ref[1] ^ k) * piece, piece), piece)
                for b in range(blocks):
                    col = pl.multiple_of(((ids_ref[2] ^ s) * blocks + b) * PAIR, PAIR)
                    at = pl.multiple_of(((r * owners + k) * blocks + b) * piece, piece)
                    out_ref[pl.ds(at, piece), :] = full_ref[row_at, pl.ds(col, PAIR)].astype(
                        out_ref.dtype
                    )
    size = mine_ref.shape[0]
    cols = width // PAIR
    lines = [sums[:, i * PAIR : (i + 1) * PAIR] for i in range(cols)]
    lines = jnp.concatenate(lines + [jnp.zeros((-cols % 16, PAIR), F32)], axis=0)
    theirs_ref[size : size + lines.shape[0], :] = lines.astype(BF16)


def turn(ids, backs, mixed, places, hidden, up, inverse, gain, w_out):
    rows, width = hidden.shape
    n = len(mixed)
    size = width * width // (2 * PAIR)
    extra = -(-width // PAIR // 16) * 16
    return pl.pallas_call(
        functools.partial(turn_kernel, n=n, owners=len(backs)),
        out_shape=(
            shaped((rows, width), F32),
            shaped((n, rows, width // n), BF16),
            shaped((size, PAIR), F32),
            shaped((size + extra, PAIR), BF16),
        ),
        in_specs=[SMEM] + [VMEM] * (len(backs) + n + 6),
        out_specs=(VMEM,) * 4,
        scratch_shapes=[pltpu.VMEM((rows, width), BF16), pltpu.VMEM((width // n, width), F32), pltpu.VMEM((n, rows, width // n), BF16)],
        compiler_params=params(32),
        cost_estimate=cost(4 * rows * width * (width + rows), 10 * width * width),
    )(ids, *backs, *mixed, places, hidden, up, inverse, gain, w_out)


def weight_grad_kernel(*refs, chunks, sizes):
    a_refs = refs[:chunks]
    b_refs = refs[chunks : 2 * chunks]
    outs = refs[2 * chunks :]
    total = None
    for a_ref, b_ref in zip(a_refs, b_refs):
        term = matmul_tn(a_ref[...], b_ref[...])
        total = term if total is None else total + term
    at = 0
    for out_ref, size in zip(outs, sizes):
        out_ref[...] = total[:, at : at + size].astype(out_ref.dtype)
        at += size


def weight_grads(row_chunks, per_chunk, sizes):
    width = row_chunks[0].shape[1]
    tile = 256
    total = sum(chunk.shape[0] for chunk in row_chunks)
    return pl.pallas_call(
        functools.partial(weight_grad_kernel, chunks=len(row_chunks), sizes=sizes),
        out_shape=[shaped((width, size), BF16 if i else F32) for i, size in enumerate(sizes)],
        grid=(width // tile,),
        in_specs=[pl.BlockSpec((chunk.shape[0], tile), lambda i: (0, i)) for chunk in row_chunks]
        + [pl.BlockSpec(value.shape, lambda i: (0, 0)) for value in per_chunk],
        out_specs=[pl.BlockSpec((tile, size), lambda i: (i, 0)) for size in sizes],
        compiler_params=params(40),
        cost_estimate=cost(2 * width * sum(sizes) * total, 8 * width * sum(sizes)),
    )(*row_chunks, *per_chunk)


def weight_out_kernel(*refs, chunks, sizes, tile):
    acts = refs[:chunks]
    ups = refs[chunks : 2 * chunks]
    outs = refs[2 * chunks :]
    total = None
    for act, up in zip(acts, ups):
        term = matmul_tn(act[...], up[...])
        total = term if total is None else total + term
    first = 0
    for out_ref, size in zip(outs, sizes):
        steps = size // tile

        @pl.when((pl.program_id(0) >= first) & (pl.program_id(0) < first + steps))
        def _():
            out_ref[...] = total.astype(out_ref.dtype)

        first += steps


def weight_grads_out(acts, up_chunks, sizes):
    width = up_chunks[0].shape[1]
    tile = min(256, min(sizes))
    total = sum(chunk.shape[0] for chunk in up_chunks)
    specs = []
    first = 0
    for size in sizes:
        steps = size // tile
        specs.append(
            pl.BlockSpec(
                (tile, width), lambda i, first=first, steps=steps: (jnp.clip(i - first, 0, steps - 1), 0)
            )
        )
        first += steps
    return pl.pallas_call(
        functools.partial(weight_out_kernel, chunks=len(acts), sizes=sizes, tile=tile),
        out_shape=[shaped((size, width), BF16 if i else F32) for i, size in enumerate(sizes)],
        grid=(first,),
        in_specs=[pl.BlockSpec((act.shape[0], tile), lambda i: (0, i)) for act in acts]
        + [pl.BlockSpec(chunk.shape, lambda i: (0, 0)) for chunk in up_chunks],
        out_specs=specs,
        compiler_params=params(40),
        cost_estimate=cost(2 * width * sum(sizes) * total, 8 * width * sum(sizes)),
    )(*acts, *up_chunks)


def produce_kernel(*refs, chunks, m, sizes):
    acts = refs[:chunks]
    w_out = refs[chunks]
    rests = refs[chunks + 1 : chunks + 1 + m]
    own_ref, other_ref, out_ref = refs[chunks + 1 + m :]
    units, width = w_out.shape
    out_ref[:units, :] = w_out[...]
    for i in range(m):
        cols = slice((i + 1) * units, (i + 2) * units)
        place_columns(out_ref, cols, rests[i], units)
    at = 0
    for c in range(chunks):
        size = sizes[c]

        @pl.loop(0, 2)
        def _(h):
            here = pl.ds(pl.multiple_of(h * 2 * size, 2 * size), 2 * size)
            total = matmul(acts[c][here, :], out_ref[...]).astype(BF16)

            @pl.when(h == 0)
            def _():
                for b in range(2):
                    own_ref[b, at : at + size, :] = total[b * size : (b + 1) * size]

            @pl.when(h == 1)
            def _():
                for b in range(2):
                    other_ref[b, at : at + size, :] = total[b * size : (b + 1) * size]

        at += size


def produce(acts, w_out, rests, sizes):
    width = w_out.shape[1]
    hidden = acts[0].shape[1]
    shape = (2, sum(sizes), width)
    return pl.pallas_call(
        functools.partial(produce_kernel, chunks=len(acts), m=len(rests), sizes=sizes),
        out_shape=(shaped(shape, BF16), shaped(shape, BF16)),
        in_specs=[VMEM] * (len(acts) + 1 + len(rests)),
        out_specs=(VMEM, VMEM),
        scratch_shapes=[pltpu.VMEM((hidden, width), BF16)],
        compiler_params=params(40),
        cost_estimate=cost(
            8 * sum(sizes) * width * hidden, 2 * hidden * width + 16 * sum(sizes) * width
        ),
    )(*acts, w_out, *rests)


def backward_kernel(
    ids_ref,
    starts_ref,
    normed_ref,
    q_ref,
    k_ref,
    v_ref,
    att_ref,
    tot_ref,
    g_ref,
    *refs,
    n,
    rows,
    owners,
):
    out_ref, mine_ref, theirs_ref, dq_ref, do_ref, sh_ref, full_ref = refs
    rank = ids_ref[0]
    pairs = q_ref.shape[1] // PAIR
    low = lax.broadcasted_iota(jnp.int32, (rows, PAIR), 1) < HEAD
    k_iota = lax.broadcasted_iota(jnp.int32, (rows, rows), 0)
    q_iota = lax.broadcasted_iota(jnp.int32, (rows, rows), 1)
    zero = jnp.zeros((), BF16)

    def both(value):
        return jnp.where(low, value, zero), jnp.where(low, zero, value)

    @pl.loop(0, pairs)
    def _(p):
        cols = pl.ds(pl.multiple_of(p * PAIR, PAIR), PAIR)
        for i in range(n):
            here = slice(i * rows, (i + 1) * rows)
            at = pl.ds(pl.multiple_of((rank ^ i) * rows, rows), rows)
            scaled = g_ref[at, cols].astype(F32) / tot_ref[here, cols]
            do_ref[here, :] = scaled.astype(BF16)
            turned = (scaled * att_ref[here, cols]).T
            sh_ref[0:1, here] = jnp.sum(turned[:HEAD], axis=0, keepdims=True)
            sh_ref[1:2, here] = jnp.sum(turned[HEAD:], axis=0, keepdims=True)
        for j in range(n):
            k_at = slice(j * rows, (j + 1) * rows)
            k2 = k_ref[k_at, cols]
            v2 = v_ref[k_at, cols]
            ks = both(k2)
            dk = None
            dv = None
            for i in range(j, n):
                here = slice(i * rows, (i + 1) * rows)
                qs = both(q_ref[here, cols])
                dos = both(do_ref[here, :])
                seen = k_iota + j * rows >= starts_ref[:, here]
                if i == j:
                    seen = seen & (k_iota <= q_iota)
                dq = None
                for h in range(2):
                    weights = jnp.where(seen, jnp.exp(matmul_nt(k2, qs[h])), 0.0)
                    slope = matmul_nt(v2, dos[h]) - sh_ref[h : h + 1, here]
                    ds = (weights * slope).astype(BF16)
                    dv_part = matmul(weights.astype(BF16), dos[h])
                    dk_part = matmul(ds, qs[h])
                    dq_part = matmul_tn(ds, ks[h])
                    dv = dv_part if dv is None else dv + dv_part
                    dk = dk_part if dk is None else dk + dk_part
                    dq = dq_part if dq is None else dq + dq_part
                if j == 0:
                    dq_ref[here, :] = dq
                else:
                    dq_ref[here, :] += dq
            out_ref[j, 1, :, cols] = dk.astype(BF16)
            out_ref[j, 2, :, cols] = dv.astype(BF16)
            out_ref[j, 0, :, cols] = (dq_ref[k_at, :] * score_scale).astype(BF16)

    @pl.loop(0, 3)
    def _(part):
        total = None
        for j in range(n):
            term = matmul_tn(normed_ref[j * rows : (j + 1) * rows, :], out_ref[j, part])
            total = term if total is None else total + term
        full_ref[part] = total

    piece = full_ref.shape[1] // (2 * owners)
    for s, to_ref in ((0, mine_ref), (1, theirs_ref)):
        for k in range(owners):
            row = ((ids_ref[2] ^ s) * owners + (ids_ref[1] ^ k)) * piece
            row_at = pl.ds(pl.multiple_of(row, piece), piece)
            for part in range(3):
                for p in range(pairs):
                    at = (part * pairs + p) * piece
                    to_ref[k, at : at + piece, :] = full_ref[
                        part, row_at, p * PAIR : (p + 1) * PAIR
                    ].astype(to_ref.dtype)


def attend_backward(ids, starts, normed, q, k, v, att, tot, g, n, owners):
    length, width = normed.shape
    group = q.shape[1]
    rows = length // n
    count = n * (n + 1) // 2 * (group // HEAD)
    size = (owners, width // (2 * owners) * 3 * group // PAIR, PAIR)
    return pl.pallas_call(
        functools.partial(backward_kernel, n=n, rows=rows, owners=owners),
        out_shape=(
            shaped((n, 3, rows, group), BF16),
            shaped(size, F32),
            shaped(size, BF16),
        ),
        in_specs=[SMEM] + [VMEM] * 8,
        out_specs=(VMEM,) * 3,
        scratch_shapes=[
            pltpu.VMEM((length, PAIR), F32),
            pltpu.VMEM((length, PAIR), BF16),
            pltpu.VMEM((8, length), F32),
            pltpu.VMEM((3, width, group), F32),
        ],
        compiler_params=params(48),
        cost_estimate=cost(
            count * rows * rows * PAIR * 10 + 6 * length * width * group,
            length * group * 24 + 2 * length * width + 9 * width * group,
            count * rows * rows,
        ),
    )(ids, starts, normed, q, k, v, att, tot, g)


def join_kernel(*refs, owners):
    mine_ref, got_ref, out_ref, near_ref = refs[:4]
    count = len(refs) - 4 - owners - 1
    others = refs[4 : 4 + count]
    own_ref, gain_ref = refs[4 + count : 6 + count]
    sent = refs[6 + count :]
    rows = mine_ref.shape[1]
    size = out_ref.shape[0]
    tall = size // owners
    out = out_ref[...]
    gains = [near_ref[...].astype(F32)]
    for other in others:
        out = out + other[:size, :].astype(F32)
        gains.append(other[size:, :].astype(F32))
    while len(gains) > 1:
        gains = [gains[i] + gains[i + 1] for i in range(0, len(gains), 2)]
    gain = gains[0].astype(BF16)
    gain_ref[...] = gain
    for k in range(owners):
        total = mine_ref[k] + got_ref[k].astype(F32)
        part = out[k * tall : (k + 1) * tall]
        if k == 0:
            own_ref[:rows, :] = total
            own_ref[rows:, :] = part
        else:
            sent[k - 1][:rows, :] = total.astype(BF16)
            sent[k - 1][rows : rows + tall, :] = part.astype(BF16)
            sent[k - 1][rows + tall :, :] = gain


def join_sums(mine, got, out_total, gain, others):
    owners, rows, _ = mine.shape
    size = out_total.shape[0]
    tall = rows + size // owners
    extra = gain.shape[0]
    return pl.pallas_call(
        functools.partial(join_kernel, owners=owners),
        out_shape=[shaped((tall, PAIR), F32), shaped((extra, PAIR), BF16)]
        + [shaped((tall + extra, PAIR), BF16)] * (owners - 1),
        in_specs=[VMEM] * (4 + len(others)),
        out_specs=[VMEM] * (owners + 1),
        compiler_params=params(24),
        cost_estimate=cost(owners * tall * PAIR * 4, owners * tall * PAIR * 10),
    )(mine, got, out_total, gain, *others)


def dense_out_kernel(ids_ref, near_ref, *refs, counts, s, n, owners, pairs, width):
    far = refs[: sum(counts)]
    w_ref = refs[sum(counts)]
    out_ref, dense_ref, sum_ref, held_ref, sems = refs[-5:]
    group = pairs * PAIR
    rows = out_ref.shape[0]
    tall = held_ref.shape[2]
    step = pl.program_id(0)

    def copies(k):
        found = []
        low, high = (k - 1) * tall, k * tall
        for r in range(n):
            if k == 0:
                source, target = near_ref.at[ids_ref[0] ^ r], held_ref.at[0, r]
                found.append(pltpu.make_async_copy(source, target, sems.at[0, r, 0]))
                continue
            begin = 0
            first = sum(counts[:r])
            for i, part in enumerate(far[first : first + counts[r]]):
                end = begin + part.shape[0]
                lo, hi = max(low, begin), min(high, end)
                if lo < hi:
                    source = part.at[pl.ds(lo - begin, hi - lo)]
                    target = held_ref.at[k % 2, r, pl.ds(lo - low, hi - lo)]
                    found.append(pltpu.make_async_copy(source, target, sems.at[k % 2, r, i]))
                begin = end
        return found

    @pl.when(step == 0)
    def _():
        for copy in copies(0):
            copy.start()

    for k in range(owners):

        @pl.when(step == k)
        def _():
            if k + 1 < owners:
                for copy in copies(k + 1):
                    copy.start()
            for copy in copies(k):
                copy.wait()

    slot = lax.rem(step, 2)
    out_rows = group // owners
    blocks = width // (2 * PAIR)
    for r in range(n):
        g = ids_ref[0] ^ r
        for part in range(3):
            for p in range(pairs):
                to = pl.multiple_of(part * width + g * group + p * PAIR, PAIR)
                at = (part * pairs + p) * rows
                out_ref[:, pl.ds(to, PAIR)] = held_ref[slot, r, at : at + rows, :].astype(F32)
        row = g * group + (ids_ref[1] ^ step) * out_rows
        row_at = pl.ds(pl.multiple_of(row, out_rows), out_rows)
        for b in range(blocks):
            at = 3 * pairs * rows + b * out_rows
            dense_ref[row_at, b * PAIR : (b + 1) * PAIR] = held_ref[
                slot, r, at : at + out_rows, :
            ].astype(F32)
    total = None
    for at in range(0, 3 * width, PAIR):
        term = out_ref[:, at : at + PAIR] * w_ref[:, at : at + PAIR].astype(F32)
        total = term if total is None else total + term
    sum_ref[...] = total


def dense_out(ids, near, far, w_qkv, s, owners, before=()):
    width = w_qkv.shape[0]
    n, tall, _ = near.shape
    rows = width // (2 * owners)
    anywhere = pl.BlockSpec(memory_space=pl.ANY)
    counts = [len(parts) for parts in far]
    parts = [part for line in far for part in line]

    def place(k, ids_ref):
        return ((ids_ref[2] ^ s) * owners + (ids_ref[1] ^ k), 0)

    return pl.pallas_call(
        functools.partial(
            dense_out_kernel,
            counts=counts,
            s=s,
            n=n,
            owners=owners,
            pairs=width // n // PAIR,
            width=width,
        ),
        out_shape=(
            shaped((width, 3 * width), F32),
            shaped((width, width), F32),
            shaped((width, PAIR), F32),
        ),
        grid_spec=pltpu.PrefetchScalarGridSpec(
            num_scalar_prefetch=1,
            grid=(owners,),
            in_specs=[anywhere] * (1 + len(parts))
            + [pl.BlockSpec((rows, 3 * width), place)]
            + [anywhere] * len(before),
            out_specs=(
                pl.BlockSpec((rows, 3 * width), place),
                pl.BlockSpec((width, width // 2), lambda k, ids_ref: (0, ids_ref[2] ^ s)),
                pl.BlockSpec((rows, PAIR), place),
            ),
            scratch_shapes=[
                pltpu.VMEM((2, n, tall, PAIR), BF16),
                pltpu.SemaphoreType.DMA((2, n, 2)),
            ],
        ),
        input_output_aliases={3 + len(parts) + i: i for i in range(len(before))},
        compiler_params=params(40),
        cost_estimate=cost(3 * width * width, 16 * width * width),
    )(ids, near, *parts, w_qkv, *before)


def back_kernel(d_ref, w_ref, x_ref, inv_ref, gain_ref, grad_ref, out_ref):
    n, _, _, group = d_ref.shape
    width = x_ref.shape[1]
    out_ref[...] = jnp.zeros_like(out_ref)

    @pl.loop(0, n)
    def _(g):
        for part in range(3):
            at = pl.ds(pl.multiple_of(part * width + g * group, group), group)
            out_ref[...] += matmul_nt(d_ref[g, part], w_ref[:, at])

    x = x_ref[...].astype(F32)
    inverse = inv_ref[...]
    scaled = out_ref[...] * gain_ref[...]
    inner = jnp.mean(scaled * x, axis=-1, keepdims=True)
    out_ref[...] = grad_ref[...] + inverse * scaled - x * (inverse**3 * inner)


def back_to_tokens(d, w_qkv, x, inverse, gain, grad_hidden):
    rows, width = x.shape
    return pl.pallas_call(
        back_kernel,
        out_shape=shaped((rows, width), F32),
        in_specs=[VMEM] * 6,
        out_specs=VMEM,
        compiler_params=params(32),
        cost_estimate=cost(6 * rows * width * width, 10 * width * width),
    )(d, w_qkv, x, inverse, gain, grad_hidden)


def on_device(
    tokens,
    out_grad,
    token_ids,
    hash_table,
    doc_lengths,
    w_qkv,
    w_out,
    gain_attn,
    gain_ffn,
    expert_in,
    expert_out,
):
    rows = tokens.shape[1]
    width = tokens.shape[2]
    n = lax.axis_size("ctx")
    owners = lax.axis_size("expert")
    rank = lax.axis_index("ctx")
    z = lax.axis_index("expert")
    core = lax.axis_index("dp")
    group = width // n
    pairs = group // PAIR
    length = n * rows
    ids = jnp.stack([rank, z, core]).astype(jnp.int32)

    inputs_low = tokens[0]

    capacity = rows * 5 // (4 * owners)
    slots = owners * capacity
    chosen = jnp.take(hash_table, token_ids[0], axis=0)
    order = jnp.arange(rows, dtype=jnp.int32)
    ahead = (chosen[:, None] == chosen[None, :]) & (order[None, :] < order[:, None])
    slot = jnp.sum(ahead.astype(jnp.int32), axis=1)
    code = (chosen ^ z) * capacity + slot
    picks = (jnp.arange(slots, dtype=jnp.int32)[:, None] == code[None, :]).astype(BF16)
    spots = jnp.arange(slots, dtype=jnp.int32).reshape(owners, 1, capacity)
    places = (code[None, :, None] == spots).astype(BF16)

    def send_rows(matrix):
        far = {}
        for k in list(range(owners // 2, owners)) + list(range(1, owners // 2)):
            far[k] = swap(matrix[k * capacity : (k + 1) * capacity], "expert", k)
        return [matrix[:capacity]] + [far[k] for k in range(1, owners)]

    def spread(piece, before=()):
        line = after(jnp.concatenate([piece, swap(piece, "ctx", 1)], axis=0), *before)
        return jnp.concatenate([line, swap(line, "dp", 1)], axis=0)

    upstream = out_grad[0]
    w_in, w_o = expert_in[0], expert_out[0]
    units = w_in.shape[1]
    top = width * 3 // 4
    upper = w_in[:top]
    up_rows = matmul(picks, upstream).astype(BF16)
    up_arrived = send_rows(up_rows)
    late_low = after(inputs_low, up_rows)
    blocks = [inputs_low] + [
        swap(inputs_low if r & (r - 1) == 0 else late_low, "ctx", r) for r in range(1, n)
    ]
    chunks = [list(range(0, owners // 2)), list(range(owners // 2, owners))]

    doc_ends = jnp.cumsum(doc_lengths[0])
    spots = jnp.arange(length, dtype=jnp.int32)
    later = doc_ends[:, None] > spots[None, :]
    ends = jnp.min(jnp.where(later, doc_ends[:, None], length), axis=0)[None, :].astype(jnp.int32)
    starts = jnp.max(jnp.where(later, 0, doc_ends[:, None]), axis=0)[None, :].astype(jnp.int32)
    normed, inverse_one, q_own, k_own, v_own, mixed_own, att, tot = attend_forward(
        ids, ends, gain_attn[None, :], blocks, w_qkv, n
    )

    rest = jnp.concatenate(
        [w_in[top:]] + [w_o[:, at : at + units] for at in range(0, width, units)], axis=0
    )
    first = after(upper, *blocks[1:])
    firsts = [swap(first, "ctx", m << 1) for m in range(1, n // 2)]
    mixed_own = after(mixed_own, firsts)
    up_line = after(jnp.concatenate(up_arrived, axis=0), mixed_own)
    up_line = jnp.concatenate([up_line[None], swap(up_line, "ctx", 1)[None]], axis=0)
    up_all = jnp.concatenate([up_line[None], swap(up_line, "dp", 1)[None]], axis=0)
    up_chunks = [
        up_all[:, :, c[0] * capacity : (c[-1] + 1) * capacity].reshape(-1, width) for c in chunks
    ]

    mixed_sent = [lax.dynamic_slice_in_dim(mixed_own, (rank ^ r) * rows, rows, 0) for r in range(n)]
    mixed_parts = [mixed_sent[0]] + [swap(mixed_sent[r], "ctx", r) for r in range(1, n)]
    rest = after(rest, mixed_parts)
    rests = [swap(rest, "ctx", m << 1) for m in range(1, n // 2)]
    hidden, inverse_two, row_sent = middle(
        ids, mixed_parts, w_out, inputs_low, gain_ffn[None, :], picks
    )

    near, far = chunks
    arrived = {0: row_sent[:capacity]}
    for k in near[1:] + far:
        arrived[k] = swap(row_sent[k * capacity : (k + 1) * capacity], "expert", k)
    near_rows = jnp.concatenate([arrived[k] for k in near], axis=0)
    far_rows = after(jnp.concatenate([arrived[k] for k in far], axis=0), near_rows)
    row_chunks = [spread(near_rows), spread(far_rows, rests)]
    sizes = [units] * (n // 2)
    acts = []
    grad_pres = []
    far_back = {}
    x_sent = []
    for c, row_chunk, up_chunk in list(zip(chunks, row_chunks, up_chunks))[::-1]:
        if acts:
            row_chunk = after(row_chunk, theirs)
        mine, theirs, act, grad_pre = expert_rows(
            row_chunk, up_chunk, w_in, w_o, firsts, rests
        )
        acts.append(act)
        grad_pres.append(grad_pre)
        line = mine.astype(F32) + swap(theirs, "dp", 1).astype(F32)
        half = line.shape[0] // 2
        x_sent.append(line[half:].astype(BF16))
        own = (line[:half] + swap(x_sent[-1], "ctx", 1).astype(F32)).astype(BF16)
        for i, k in reversed(list(enumerate(c))):
            piece = own[i * capacity : (i + 1) * capacity]
            far_back[k] = piece if k == 0 else swap(piece, "expert", k)
    back = [far_back[k] for k in range(owners)]
    acts, grad_pres = acts[::-1], grad_pres[::-1]
    last_own = own

    grads_out = weight_grads_out(after(acts, x_sent[0]), up_chunks, sizes)

    def others(grads):
        return [swap(grads[i], "ctx", i << 1) for i in range(1, len(grads))]

    out_others = others(grads_out)
    made, made_other = produce(
        after(acts, x_sent[1]), w_o, rests, [len(c) * capacity for c in chunks]
    )
    grads_in = weight_grads(row_chunks, after(grad_pres, x_sent[1]), sizes)
    back = after(back, made, grads_in)
    made_other = swap(made_other, "dp", 1)

    grad_hidden, grad_parts, mine, theirs = turn(
        ids, back, mixed_parts, places, hidden, upstream, inverse_two, gain_ffn[None, :], w_out
    )
    grad_parts = after(grad_parts, out_others)
    grad_att_own = jnp.concatenate(
        [grad_parts[0]] + [swap(grad_parts[r], "ctx", r) for r in range(1, n)], axis=0
    )

    def add_others(own, parts):
        for part in parts:
            own = own + part.astype(F32)
        return own

    cols = width // PAIR
    size = mine.shape[0]
    got = swap(theirs, "dp", 1)
    gain_low = (theirs[size:].astype(F32) + got[size:].astype(F32)).astype(BF16)
    total = mine + got[:size].astype(F32)
    piece = size // n
    out_sent = [
        jnp.concatenate([total[r * piece : (r + 1) * piece].astype(BF16), gain_low], axis=0)
        for r in range(1, n)
    ]
    out_sent = after(out_sent, grad_att_own)
    out_got = [swap(out_sent[r - 1], "ctx", r) for r in range(1, n)]

    held = after(grad_att_own, out_sent)
    d_own, mine, theirs = attend_backward(
        ids, starts, normed, q_own, k_own, v_own, att, tot, held, n, owners
    )
    d_own, theirs = after((d_own, theirs), out_got)
    d_pieces = exchange(d_own, "ctx")
    in_others = others(after(grads_in, d_pieces))
    made_line = made.astype(F32) + after(made_other, d_pieces).astype(F32)
    sent = made_line[1].astype(BF16)
    made_own = (made_line[0] + swap(sent, "ctx", 1).astype(F32)).astype(BF16)
    order = list(range(owners // 2, owners)) + list(range(1, owners // 2))
    own, gain_low, *messages = join_sums(
        mine, swap(theirs, "dp", 1), total[: total.shape[0] // n], gain_low, out_got
    )
    tall = own.shape[0]
    got = {k: swap(messages[k - 1], "expert", k) for k in order}
    piece = own
    gains = [gain_low.astype(F32)]
    for k in range(owners - 1, 0, -1):
        piece = piece + got[k][:tall].astype(F32)
    for k in range(1, owners):
        gains.append(got[k][tall:].astype(F32))
    while len(gains) > 1:
        gains = [gains[i] + gains[i + 1] for i in range(0, len(gains), 2)]
    grad_gain_ffn = gains[0][:cols].reshape(width)
    piece = piece.astype(BF16)
    arrived = {k: swap(piece, "expert", k) for k in order}
    near_lines = spread_to(piece, "ctx")
    line = jnp.concatenate([arrived[k] for k in range(1, owners)], axis=0)
    line = after(line, in_others, made_own, near_lines)
    returned = send_rows(after(made_own, line))
    if n == 4:
        half = line.shape[0] // 2
        one, two = swap(line, "ctx", 1), swap(line, "ctx", 2)
        sent = (one[:half], two[half:])
        last = [swap(sent[0], "ctx", 2), swap(sent[1], "ctx", 1)]
        far_lines = [[line], [one], [two], last]
        in_others, out_others, d_pieces, returned = after(
            (in_others, out_others, d_pieces, returned), sent
        )
    else:
        far_lines = [[line]] + [[swap(line, "ctx", r)] for r in range(1, n)]
    grad_inputs = back_to_tokens(
        d_pieces,
        w_qkv,
        inputs_low,
        inverse_one,
        gain_attn[None, :],
        grad_hidden,
    )
    grad_expert_out = add_others(grads_out[0], out_others)
    grad_expert_in = add_others(grads_in[0], in_others)
    returned = jnp.concatenate(returned, axis=0)
    block_out = (
        hidden + matmul(places.transpose(1, 0, 2).reshape(rows, slots), returned)
    ).astype(BF16)
    near_other = swap(near_lines, "dp", 1)
    far_lines[n - 1] = after(
        far_lines[n - 1], block_out, grad_inputs, grad_expert_out, grad_expert_in, near_other
    )
    first = dense_out(ids, near_lines, far_lines, w_qkv, 0, owners)
    far_other = [[swap(part, "dp", 1) for part in parts] for parts in far_lines]
    grad_w_qkv, grad_w_out, gain_sums = dense_out(
        ids, near_other, far_other, w_qkv, 1, owners, first
    )
    grad_gain_attn = jnp.sum(gain_sums, axis=1) / gain_attn

    return (
        block_out[None],
        grad_inputs[None],
        grad_w_qkv,
        grad_w_out,
        grad_gain_attn,
        grad_gain_ffn,
        grad_expert_in[None],
        grad_expert_out[None],
    )


def solution(mesh):
    rows = P(("expert", "dp"), "ctx", None)
    placed = (
        rows,
        rows,
        P(("expert", "dp"), "ctx"),
        P(),
        P(("expert", "dp"), None),
        P(),
        P(),
        P(),
        P(),
        P("expert", None, ("ctx", "dp")),
        P("expert", ("ctx", "dp"), None),
    )
    return jax.shard_map(
        on_device,
        mesh=mesh,
        in_specs=placed,
        out_specs=(
            rows,
            rows,
            P(),
            P(),
            P(),
            P(),
            P("expert", None, ("ctx", "dp")),
            P("expert", ("ctx", "dp"), None),
        ),
        check_vma=False,
    )
```

```python
import functools
import jax
import jax.numpy as jnp
from jax import lax
from jax.experimental import pallas as pl
from jax.experimental.pallas import tpu as pltpu
from jax.sharding import PartitionSpec as P

HEADS = 16
HEAD = 64
PAIR = 2 * HEAD

eps = 1e-06
score_scale = 0.125
F32 = jnp.float32
BF16 = jnp.bfloat16
VMEM = pl.BlockSpec(memory_space=pltpu.VMEM)
SMEM = pl.BlockSpec(memory_space=pltpu.SMEM)
shaped = jax.ShapeDtypeStruct


def swap(value, axis, bits):
    size = lax.axis_size(axis)
    return lax.ppermute(value, axis, [(i, i ^ bits) for i in range(size)])


def exchange(value, axis):
    return lax.all_to_all(value, axis, split_axis=0, concat_axis=0, tiled=True)


def spread_to(value, axis):
    return exchange(jnp.broadcast_to(value[None], (lax.axis_size(axis),) + value.shape), axis)


def after(value, *others):
    return lax.optimization_barrier((value,) + others)[0]


def matmul(a, b):
    return jnp.dot(a, b, preferred_element_type=F32)


def matmul_nt(a, b):
    return lax.dot_general(a, b, (((1,), (1,)), ((), ())), preferred_element_type=F32)


def matmul_tn(a, b):
    return lax.dot_general(a, b, (((0,), (0,)), ((), ())), preferred_element_type=F32)


def params(mib):
    return pltpu.CompilerParams(vmem_limit_bytes=mib << 20)


def cost(flops, moved, transcendentals=0):
    return pl.CostEstimate(
        flops=int(flops / 4), bytes_accessed=int(moved / 4), transcendentals=int(transcendentals / 4)
    )


def distances(bits):
    found = [0]
    for bit in reversed(bits):
        found = found + [value ^ bit for value in found]
    return found


def gelu_parts(pre):
    c = 0.7978845608028654
    square = pre * pre
    t = jnp.tanh(c * (pre + 0.044715 * pre * square))
    half = 0.5 * (1.0 + t)
    slope = half + 0.5 * pre * (1.0 - t * t) * (c * (1.0 + 3.0 * 0.044715 * square))
    return pre * half, slope


def forward_kernel(ids_ref, ends_ref, gain_ref, *refs, n, rows):
    blocks = refs[:n]
    weights = refs[n : n + 3]
    normed_ref, inv_ref, q_ref, k_ref, v_ref, mixed_ref, att_ref, tot_ref = refs[n + 3 :]
    rank = ids_ref[0]
    pairs = mixed_ref.shape[1] // PAIR
    for r in range(n):
        x = blocks[r][...].astype(F32)
        inverse = lax.rsqrt(jnp.mean(x * x, axis=-1, keepdims=True) + eps)
        if r == 0:
            inv_ref[...] = inverse
        here = pl.ds(pl.multiple_of((rank ^ r) * rows, rows), rows)
        normed = (x * inverse * gain_ref[...]).astype(BF16)
        normed_ref[here, :] = normed
        q_ref[here, :] = (matmul(normed, weights[0][...]) * score_scale).astype(BF16)
        k_ref[here, :] = matmul(normed, weights[1][...]).astype(BF16)
        v_ref[here, :] = matmul(normed, weights[2][...]).astype(BF16)
    low = lax.broadcasted_iota(jnp.int32, (rows, PAIR), 1) < HEAD
    q_iota = lax.broadcasted_iota(jnp.int32, (rows, rows), 0)
    k_iota = lax.broadcasted_iota(jnp.int32, (rows, rows), 1)
    one = jnp.ones((), BF16)
    zero = jnp.zeros((), BF16)

    @pl.loop(0, pairs)
    def _(p):
        out = pl.ds(pl.multiple_of(p * PAIR, PAIR), PAIR)
        for i in range(n):
            q_at = slice(i * rows, (i + 1) * rows)
            q2 = q_ref[q_at, out]
            qs = (jnp.where(low, q2, zero), jnp.where(low, zero, q2))
            sums = [None, None]
            for j in range(i + 1):
                k_at = slice(j * rows, (j + 1) * rows)
                k2 = k_ref[k_at, out]
                v2 = v_ref[k_at, out]
                vs = (jnp.where(low, v2, one), jnp.where(low, one, v2))
                seen = q_iota + i * rows < ends_ref[:, j * rows : (j + 1) * rows]
                if i == j:
                    seen = seen & (k_iota <= q_iota)
                for h in range(2):
                    w = jnp.where(seen, jnp.exp(matmul_nt(qs[h], k2)), 0.0).astype(BF16)
                    part = matmul(w, vs[h])
                    sums[h] = part if sums[h] is None else sums[h] + part
            total = jnp.where(low, pltpu.roll(sums[0], HEAD, 1), pltpu.roll(sums[1], HEAD, 1))
            att = jnp.where(low, sums[0], sums[1]) / total
            att_ref[q_at, out] = att
            mixed_ref[q_at, out] = att.astype(BF16)
            tot_ref[q_at, out] = total


def attend_forward(ids, ends, gain, blocks, w_qkv, n):
    rows, width = blocks[0].shape
    group = width // n
    length = n * rows
    count = n * (n + 1) // 2 * (group // HEAD)

    def whole(*shape):
        return pl.BlockSpec(shape, lambda s, ids_ref: (0, 0))

    def columns(part):
        return pl.BlockSpec((width, group), lambda s, ids_ref: (0, part * n + ids_ref[0]))

    own = (length, group)
    return pl.pallas_call(
        functools.partial(forward_kernel, n=n, rows=rows),
        out_shape=(
            shaped((length, width), BF16),
            shaped((rows, 1), F32),
            shaped(own, BF16),
            shaped(own, BF16),
            shaped(own, BF16),
            shaped(own, BF16),
            shaped(own, F32),
            shaped(own, F32),
        ),
        grid_spec=pltpu.PrefetchScalarGridSpec(
            num_scalar_prefetch=1,
            grid=(1,),
            in_specs=[whole(1, length), whole(1, width)]
            + [whole(rows, width)] * n
            + [columns(0), columns(1), columns(2)],
            out_specs=[whole(length, width), whole(rows, 1)] + [whole(*own)] * 6,
        ),
        compiler_params=params(48),
        cost_estimate=cost(
            count * rows * rows * PAIR * 4 + 6 * length * width * group,
            length * width * 4 + length * group * 16 + 6 * width * group,
            count * rows * rows,
        ),
    )(ids, ends, gain, *blocks, w_qkv, w_qkv, w_qkv)


def middle_kernel(ids_ref, *refs, n):
    parts = refs[:n]
    w_ref, x_ref, gain_ref, picks_ref, hidden_ref, inv_ref, sent_ref = refs[n:]
    group = parts[0].shape[1]
    hidden = x_ref[...].astype(F32)
    for r in range(n):
        at = pl.ds(pl.multiple_of((ids_ref[0] ^ r) * group, group), group)
        hidden = hidden + matmul(parts[r][...], w_ref[at, :])
    hidden_ref[...] = hidden
    inverse = lax.rsqrt(jnp.mean(hidden * hidden, axis=-1, keepdims=True) + eps)
    inv_ref[...] = inverse
    low = (hidden * inverse * gain_ref[...]).astype(BF16)
    sent_ref[...] = matmul(picks_ref[...], low).astype(BF16)


def middle(ids, parts, w_out, x, gain, picks):
    rows, width = x.shape
    slots = picks.shape[0]
    return pl.pallas_call(
        functools.partial(middle_kernel, n=len(parts)),
        out_shape=(
            shaped((rows, width), F32),
            shaped((rows, 1), F32),
            shaped((slots, width), BF16),
        ),
        in_specs=[SMEM] + [VMEM] * (len(parts) + 4),
        out_specs=(VMEM, VMEM, VMEM),
        compiler_params=params(24),
        cost_estimate=cost(2 * rows * width * (width + slots), 6 * width * width),
    )(ids, *parts, w_out, x, gain, picks)


def place_columns(out_ref, where, rest_ref, units):
    width = out_ref.shape[1]
    for b in range(width // units):
        at = rest_ref.shape[0] - width + b * units
        out_ref[where, b * units : (b + 1) * units] = rest_ref[at : at + units]


def expert_kernel(*refs, m):
    row_ref, up_ref, w_in, w_out = refs[:4]
    firsts, rests = refs[4 : 4 + m], refs[4 + m : 4 + 2 * m]
    own_ref, other_ref, act_out, pre_out, in_ref, out_ref, act_ref, pre_ref, sems = refs[4 + 2 * m :]
    width, units = w_in.shape
    in_ref[:, :units] = w_in[...]
    out_ref[:units, :] = w_out[...]
    for i in range(m):
        cols = slice((i + 1) * units, (i + 2) * units)
        top = firsts[i].shape[0]
        in_ref[:top, cols] = firsts[i][...]
        in_ref[top:, cols] = rests[i][: width - top]
        place_columns(out_ref, cols, rests[i], units)
    half = own_ref.shape[0]
    size = half

    @pl.loop(0, 2 * half // size)
    def _(i):
        here = pl.ds(pl.multiple_of(i * size, size), size)
        value, slope = gelu_parts(matmul(row_ref[here, :], in_ref[...]))
        act_ref[here, :] = value.astype(BF16)
        grad_pre = (slope * matmul_nt(up_ref[here, :], out_ref[...])).astype(BF16)
        pre_ref[here, :] = grad_pre
        part = matmul_nt(grad_pre, in_ref[...]).astype(BF16)

        @pl.when(i * size < half)
        def _():
            own_ref[here, :] = part

        @pl.when(i * size >= half)
        def _():
            other_ref[pl.ds(pl.multiple_of(i * size - half, size), size), :] = part

    keep_act = pltpu.make_async_copy(act_ref, act_out, sems.at[0])
    keep_act.start()
    keep_pre = pltpu.make_async_copy(pre_ref, pre_out, sems.at[1])
    keep_pre.start()
    keep_act.wait()
    keep_pre.wait()


def expert_rows(row_chunk, up_chunk, w_in, w_out, firsts, rests):
    count, width = row_chunk.shape
    m = len(firsts)
    hidden = (m + 1) * w_in.shape[1]
    anywhere = pl.BlockSpec(memory_space=pl.ANY)
    return pl.pallas_call(
        functools.partial(expert_kernel, m=m),
        out_shape=[shaped((count // 2, width), BF16)] * 2 + [shaped((count, hidden), BF16)] * 2,
        in_specs=[VMEM] * (4 + 2 * m),
        out_specs=[VMEM] * 2 + [anywhere] * 2,
        scratch_shapes=[
            pltpu.VMEM((width, hidden), BF16),
            pltpu.VMEM((hidden, width), BF16),
            pltpu.VMEM((count, hidden), BF16),
            pltpu.VMEM((count, hidden), BF16),
            pltpu.SemaphoreType.DMA((2,)),
        ],
        compiler_params=params(40),
        cost_estimate=cost(6 * count * width * hidden, 4 * width * hidden + 8 * count * width),
    )(row_chunk, up_chunk, w_in, w_out, *firsts, *rests)


def turn_kernel(ids_ref, *refs, n, owners):
    backs, mixed = refs[:owners], refs[owners : owners + n]
    places_ref, hidden_ref, up_ref, inv_ref, gain_ref, w_ref = refs[owners + n : owners + n + 6]
    grad_ref, part_ref, mine_ref, theirs_ref, branch_ref, full_ref, mixed_ref = refs[owners + n + 6 :]
    group = part_ref.shape[2]
    width = hidden_ref.shape[1]
    grad_rows = None
    for k in range(owners):
        term = matmul(places_ref[k], backs[k][...])
        grad_rows = term if grad_rows is None else grad_rows + term
    hidden = hidden_ref[...]
    inverse = inv_ref[...]
    scaled = grad_rows * gain_ref[...]
    inner = jnp.mean(scaled * hidden, axis=-1, keepdims=True)
    grad = up_ref[...].astype(F32) + inverse * scaled - hidden * (inverse**3 * inner)
    grad_ref[...] = grad
    branch_ref[...] = grad.astype(BF16)
    for r in range(n):
        at = pl.ds(pl.multiple_of((ids_ref[0] ^ r) * group, group), group)
        part_ref[r] = matmul_nt(branch_ref[...], w_ref[at, :]).astype(BF16)
    sums = jnp.sum(grad_rows * hidden * inverse, axis=0, keepdims=True)
    blocks = width // (2 * PAIR)
    piece = group // owners
    for r in range(n):
        mixed_ref[r] = mixed[r][...]

    @pl.loop(0, n)
    def _(r):
        full_ref[...] = matmul_tn(mixed_ref[r], branch_ref[...])
        for s, out_ref in ((0, mine_ref), (1, theirs_ref)):
            for k in range(owners):
                row_at = pl.ds(pl.multiple_of((ids_ref[1] ^ k) * piece, piece), piece)
                for b in range(blocks):
                    col = pl.multiple_of(((ids_ref[2] ^ s) * blocks + b) * PAIR, PAIR)
                    at = pl.multiple_of(((r * owners + k) * blocks + b) * piece, piece)
                    out_ref[pl.ds(at, piece), :] = full_ref[row_at, pl.ds(col, PAIR)].astype(
                        out_ref.dtype
                    )
    size = mine_ref.shape[0]
    cols = width // PAIR
    lines = [sums[:, i * PAIR : (i + 1) * PAIR] for i in range(cols)]
    lines = jnp.concatenate(lines + [jnp.zeros((-cols % 16, PAIR), F32)], axis=0)
    theirs_ref[size : size + lines.shape[0], :] = lines.astype(BF16)


def turn(ids, backs, mixed, places, hidden, up, inverse, gain, w_out):
    rows, width = hidden.shape
    n = len(mixed)
    size = width * width // (2 * PAIR)
    extra = -(-width // PAIR // 16) * 16
    return pl.pallas_call(
        functools.partial(turn_kernel, n=n, owners=len(backs)),
        out_shape=(
            shaped((rows, width), F32),
            shaped((n, rows, width // n), BF16),
            shaped((size, PAIR), F32),
            shaped((size + extra, PAIR), BF16),
        ),
        in_specs=[SMEM] + [VMEM] * (len(backs) + n + 6),
        out_specs=(VMEM,) * 4,
        scratch_shapes=[pltpu.VMEM((rows, width), BF16), pltpu.VMEM((width // n, width), F32), pltpu.VMEM((n, rows, width // n), BF16)],
        compiler_params=params(32),
        cost_estimate=cost(4 * rows * width * (width + rows), 10 * width * width),
    )(ids, *backs, *mixed, places, hidden, up, inverse, gain, w_out)


def weight_grad_kernel(*refs, chunks, sizes):
    a_refs = refs[:chunks]
    b_refs = refs[chunks : 2 * chunks]
    outs = refs[2 * chunks :]
    total = None
    for a_ref, b_ref in zip(a_refs, b_refs):
        term = matmul_tn(a_ref[...], b_ref[...])
        total = term if total is None else total + term
    at = 0
    for out_ref, size in zip(outs, sizes):
        out_ref[...] = total[:, at : at + size].astype(out_ref.dtype)
        at += size


def weight_grads(row_chunks, per_chunk, sizes):
    width = row_chunks[0].shape[1]
    tile = 256
    total = sum(chunk.shape[0] for chunk in row_chunks)
    return pl.pallas_call(
        functools.partial(weight_grad_kernel, chunks=len(row_chunks), sizes=sizes),
        out_shape=[shaped((width, size), BF16 if i else F32) for i, size in enumerate(sizes)],
        grid=(width // tile,),
        in_specs=[pl.BlockSpec((chunk.shape[0], tile), lambda i: (0, i)) for chunk in row_chunks]
        + [pl.BlockSpec(value.shape, lambda i: (0, 0)) for value in per_chunk],
        out_specs=[pl.BlockSpec((tile, size), lambda i: (i, 0)) for size in sizes],
        compiler_params=params(40),
        cost_estimate=cost(2 * width * sum(sizes) * total, 8 * width * sum(sizes)),
    )(*row_chunks, *per_chunk)


def weight_out_kernel(*refs, chunks, sizes, tile):
    acts = refs[:chunks]
    ups = refs[chunks : 2 * chunks]
    outs = refs[2 * chunks :]
    total = None
    for act, up in zip(acts, ups):
        term = matmul_tn(act[...], up[...])
        total = term if total is None else total + term
    first = 0
    for out_ref, size in zip(outs, sizes):
        steps = size // tile

        @pl.when((pl.program_id(0) >= first) & (pl.program_id(0) < first + steps))
        def _():
            out_ref[...] = total.astype(out_ref.dtype)

        first += steps


def weight_grads_out(acts, up_chunks, sizes):
    width = up_chunks[0].shape[1]
    tile = min(256, min(sizes))
    total = sum(chunk.shape[0] for chunk in up_chunks)
    specs = []
    first = 0
    for size in sizes:
        steps = size // tile
        specs.append(
            pl.BlockSpec(
                (tile, width), lambda i, first=first, steps=steps: (jnp.clip(i - first, 0, steps - 1), 0)
            )
        )
        first += steps
    return pl.pallas_call(
        functools.partial(weight_out_kernel, chunks=len(acts), sizes=sizes, tile=tile),
        out_shape=[shaped((size, width), BF16 if i else F32) for i, size in enumerate(sizes)],
        grid=(first,),
        in_specs=[pl.BlockSpec((act.shape[0], tile), lambda i: (0, i)) for act in acts]
        + [pl.BlockSpec(chunk.shape, lambda i: (0, 0)) for chunk in up_chunks],
        out_specs=specs,
        compiler_params=params(40),
        cost_estimate=cost(2 * width * sum(sizes) * total, 8 * width * sum(sizes)),
    )(*acts, *up_chunks)


def produce_kernel(*refs, chunks, m, sizes):
    acts = refs[:chunks]
    w_out = refs[chunks]
    rests = refs[chunks + 1 : chunks + 1 + m]
    own_ref, other_ref, out_ref = refs[chunks + 1 + m :]
    units, width = w_out.shape
    out_ref[:units, :] = w_out[...]
    for i in range(m):
        cols = slice((i + 1) * units, (i + 2) * units)
        place_columns(out_ref, cols, rests[i], units)
    at = 0
    for c in range(chunks):
        size = sizes[c]

        @pl.loop(0, 2)
        def _(h):
            here = pl.ds(pl.multiple_of(h * 2 * size, 2 * size), 2 * size)
            total = matmul(acts[c][here, :], out_ref[...]).astype(BF16)

            @pl.when(h == 0)
            def _():
                for b in range(2):
                    own_ref[b, at : at + size, :] = total[b * size : (b + 1) * size]

            @pl.when(h == 1)
            def _():
                for b in range(2):
                    other_ref[b, at : at + size, :] = total[b * size : (b + 1) * size]

        at += size


def produce(acts, w_out, rests, sizes):
    width = w_out.shape[1]
    hidden = acts[0].shape[1]
    shape = (2, sum(sizes), width)
    return pl.pallas_call(
        functools.partial(produce_kernel, chunks=len(acts), m=len(rests), sizes=sizes),
        out_shape=(shaped(shape, BF16), shaped(shape, BF16)),
        in_specs=[VMEM] * (len(acts) + 1 + len(rests)),
        out_specs=(VMEM, VMEM),
        scratch_shapes=[pltpu.VMEM((hidden, width), BF16)],
        compiler_params=params(40),
        cost_estimate=cost(
            8 * sum(sizes) * width * hidden, 2 * hidden * width + 16 * sum(sizes) * width
        ),
    )(*acts, w_out, *rests)


def backward_kernel(
    ids_ref,
    starts_ref,
    normed_ref,
    q_ref,
    k_ref,
    v_ref,
    att_ref,
    tot_ref,
    g_ref,
    *refs,
    n,
    rows,
    owners,
):
    out_ref, mine_ref, theirs_ref, dq_ref, do_ref, sh_ref, full_ref = refs
    rank = ids_ref[0]
    pairs = q_ref.shape[1] // PAIR
    low = lax.broadcasted_iota(jnp.int32, (rows, PAIR), 1) < HEAD
    k_iota = lax.broadcasted_iota(jnp.int32, (rows, rows), 0)
    q_iota = lax.broadcasted_iota(jnp.int32, (rows, rows), 1)
    zero = jnp.zeros((), BF16)

    def both(value):
        return jnp.where(low, value, zero), jnp.where(low, zero, value)

    @pl.loop(0, pairs)
    def _(p):
        cols = pl.ds(pl.multiple_of(p * PAIR, PAIR), PAIR)
        for i in range(n):
            here = slice(i * rows, (i + 1) * rows)
            at = pl.ds(pl.multiple_of((rank ^ i) * rows, rows), rows)
            scaled = g_ref[at, cols].astype(F32) / tot_ref[here, cols]
            do_ref[here, :] = scaled.astype(BF16)
            turned = (scaled * att_ref[here, cols]).T
            sh_ref[0:1, here] = jnp.sum(turned[:HEAD], axis=0, keepdims=True)
            sh_ref[1:2, here] = jnp.sum(turned[HEAD:], axis=0, keepdims=True)
        for j in range(n):
            k_at = slice(j * rows, (j + 1) * rows)
            k2 = k_ref[k_at, cols]
            v2 = v_ref[k_at, cols]
            ks = both(k2)
            dk = None
            dv = None
            for i in range(j, n):
                here = slice(i * rows, (i + 1) * rows)
                qs = both(q_ref[here, cols])
                dos = both(do_ref[here, :])
                seen = k_iota + j * rows >= starts_ref[:, here]
                if i == j:
                    seen = seen & (k_iota <= q_iota)
                lows = []
                slopes = []
                for h in range(2):
                    weights = jnp.where(seen, jnp.exp(matmul_nt(k2, qs[h])), 0.0)
                    slope = matmul_nt(v2, dos[h]) - sh_ref[h : h + 1, here]
                    slopes.append((weights * slope).astype(BF16))
                    lows.append(weights.astype(BF16))
                dv_part = matmul(jnp.concatenate(lows, axis=1), jnp.concatenate(dos, axis=0))
                dk_part = matmul(jnp.concatenate(slopes, axis=1), jnp.concatenate(qs, axis=0))
                dq = matmul_tn(jnp.concatenate(slopes, axis=0), jnp.concatenate(ks, axis=0))
                dv = dv_part if dv is None else dv + dv_part
                dk = dk_part if dk is None else dk + dk_part
                if j == 0:
                    dq_ref[here, :] = dq
                else:
                    dq_ref[here, :] += dq
            out_ref[j, 1, :, cols] = dk.astype(BF16)
            out_ref[j, 2, :, cols] = dv.astype(BF16)
            out_ref[j, 0, :, cols] = (dq_ref[k_at, :] * score_scale).astype(BF16)

    @pl.loop(0, 3)
    def _(part):
        total = None
        for j in range(n):
            term = matmul_tn(normed_ref[j * rows : (j + 1) * rows, :], out_ref[j, part])
            total = term if total is None else total + term
        full_ref[part] = total

    piece = full_ref.shape[1] // (2 * owners)
    for s, to_ref in ((0, mine_ref), (1, theirs_ref)):
        for k in range(owners):
            row = ((ids_ref[2] ^ s) * owners + (ids_ref[1] ^ k)) * piece
            row_at = pl.ds(pl.multiple_of(row, piece), piece)
            for part in range(3):
                for p in range(pairs):
                    at = (part * pairs + p) * piece
                    to_ref[k, at : at + piece, :] = full_ref[
                        part, row_at, p * PAIR : (p + 1) * PAIR
                    ].astype(to_ref.dtype)


def attend_backward(ids, starts, normed, q, k, v, att, tot, g, n, owners):
    length, width = normed.shape
    group = q.shape[1]
    rows = length // n
    count = n * (n + 1) // 2 * (group // HEAD)
    size = (owners, width // (2 * owners) * 3 * group // PAIR, PAIR)
    return pl.pallas_call(
        functools.partial(backward_kernel, n=n, rows=rows, owners=owners),
        out_shape=(
            shaped((n, 3, rows, group), BF16),
            shaped(size, F32),
            shaped(size, BF16),
        ),
        in_specs=[SMEM] + [VMEM] * 8,
        out_specs=(VMEM,) * 3,
        scratch_shapes=[
            pltpu.VMEM((length, PAIR), F32),
            pltpu.VMEM((length, PAIR), BF16),
            pltpu.VMEM((8, length), F32),
            pltpu.VMEM((3, width, group), F32),
        ],
        compiler_params=params(48),
        cost_estimate=cost(
            count * rows * rows * PAIR * 10 + 6 * length * width * group,
            length * group * 24 + 2 * length * width + 9 * width * group,
            count * rows * rows,
        ),
    )(ids, starts, normed, q, k, v, att, tot, g)


def join_kernel(*refs, owners):
    mine_ref, got_ref, out_ref, near_ref = refs[:4]
    count = len(refs) - 4 - owners - 1
    others = refs[4 : 4 + count]
    own_ref, gain_ref = refs[4 + count : 6 + count]
    sent = refs[6 + count :]
    rows = mine_ref.shape[1]
    size = out_ref.shape[0]
    tall = size // owners
    out = out_ref[...]
    gains = [near_ref[...].astype(F32)]
    for other in others:
        out = out + other[:size, :].astype(F32)
        gains.append(other[size:, :].astype(F32))
    while len(gains) > 1:
        gains = [gains[i] + gains[i + 1] for i in range(0, len(gains), 2)]
    gain = gains[0].astype(BF16)
    gain_ref[...] = gain
    for k in range(owners):
        total = mine_ref[k] + got_ref[k].astype(F32)
        part = out[k * tall : (k + 1) * tall]
        if k == 0:
            own_ref[:rows, :] = total
            own_ref[rows:, :] = part
        else:
            sent[k - 1][:rows, :] = total.astype(BF16)
            sent[k - 1][rows : rows + tall, :] = part.astype(BF16)
            sent[k - 1][rows + tall :, :] = gain


def join_sums(mine, got, out_total, gain, others):
    owners, rows, _ = mine.shape
    size = out_total.shape[0]
    tall = rows + size // owners
    extra = gain.shape[0]
    return pl.pallas_call(
        functools.partial(join_kernel, owners=owners),
        out_shape=[shaped((tall, PAIR), F32), shaped((extra, PAIR), BF16)]
        + [shaped((tall + extra, PAIR), BF16)] * (owners - 1),
        in_specs=[VMEM] * (4 + len(others)),
        out_specs=[VMEM] * (owners + 1),
        compiler_params=params(24),
        cost_estimate=cost(owners * tall * PAIR * 4, owners * tall * PAIR * 10),
    )(mine, got, out_total, gain, *others)


def dense_out_kernel(ids_ref, near_ref, *refs, counts, s, n, owners, pairs, width):
    far = refs[: sum(counts)]
    w_ref = refs[sum(counts)]
    out_ref, dense_ref, sum_ref, held_ref, sems = refs[-5:]
    group = pairs * PAIR
    rows = out_ref.shape[0]
    tall = held_ref.shape[2]
    step = pl.program_id(0)

    def copies(k):
        found = []
        low, high = (k - 1) * tall, k * tall
        for r in range(n):
            if k == 0:
                source, target = near_ref.at[ids_ref[0] ^ r], held_ref.at[0, r]
                found.append(pltpu.make_async_copy(source, target, sems.at[0, r, 0]))
                continue
            begin = 0
            first = sum(counts[:r])
            for i, part in enumerate(far[first : first + counts[r]]):
                end = begin + part.shape[0]
                lo, hi = max(low, begin), min(high, end)
                if lo < hi:
                    source = part.at[pl.ds(lo - begin, hi - lo)]
                    target = held_ref.at[k % 2, r, pl.ds(lo - low, hi - lo)]
                    found.append(pltpu.make_async_copy(source, target, sems.at[k % 2, r, i]))
                begin = end
        return found

    @pl.when(step == 0)
    def _():
        for copy in copies(0):
            copy.start()

    for k in range(owners):

        @pl.when(step == k)
        def _():
            if k + 1 < owners:
                for copy in copies(k + 1):
                    copy.start()
            for copy in copies(k):
                copy.wait()

    slot = lax.rem(step, 2)
    out_rows = group // owners
    blocks = width // (2 * PAIR)
    for r in range(n):
        g = ids_ref[0] ^ r
        for part in range(3):
            for p in range(pairs):
                to = pl.multiple_of(part * width + g * group + p * PAIR, PAIR)
                at = (part * pairs + p) * rows
                out_ref[:, pl.ds(to, PAIR)] = held_ref[slot, r, at : at + rows, :].astype(F32)
        row = g * group + (ids_ref[1] ^ step) * out_rows
        row_at = pl.ds(pl.multiple_of(row, out_rows), out_rows)
        for b in range(blocks):
            at = 3 * pairs * rows + b * out_rows
            dense_ref[row_at, b * PAIR : (b + 1) * PAIR] = held_ref[
                slot, r, at : at + out_rows, :
            ].astype(F32)
    total = None
    for at in range(0, 3 * width, PAIR):
        term = out_ref[:, at : at + PAIR] * w_ref[:, at : at + PAIR].astype(F32)
        total = term if total is None else total + term
    sum_ref[...] = total


def dense_out(ids, near, far, w_qkv, s, owners, before=()):
    width = w_qkv.shape[0]
    n, tall, _ = near.shape
    rows = width // (2 * owners)
    anywhere = pl.BlockSpec(memory_space=pl.ANY)
    counts = [len(parts) for parts in far]
    parts = [part for line in far for part in line]

    def place(k, ids_ref):
        return ((ids_ref[2] ^ s) * owners + (ids_ref[1] ^ k), 0)

    return pl.pallas_call(
        functools.partial(
            dense_out_kernel,
            counts=counts,
            s=s,
            n=n,
            owners=owners,
            pairs=width // n // PAIR,
            width=width,
        ),
        out_shape=(
            shaped((width, 3 * width), F32),
            shaped((width, width), F32),
            shaped((width, PAIR), F32),
        ),
        grid_spec=pltpu.PrefetchScalarGridSpec(
            num_scalar_prefetch=1,
            grid=(owners,),
            in_specs=[anywhere] * (1 + len(parts))
            + [pl.BlockSpec((rows, 3 * width), place)]
            + [anywhere] * len(before),
            out_specs=(
                pl.BlockSpec((rows, 3 * width), place),
                pl.BlockSpec((width, width // 2), lambda k, ids_ref: (0, ids_ref[2] ^ s)),
                pl.BlockSpec((rows, PAIR), place),
            ),
            scratch_shapes=[
                pltpu.VMEM((2, n, tall, PAIR), BF16),
                pltpu.SemaphoreType.DMA((2, n, 2)),
            ],
        ),
        input_output_aliases={3 + len(parts) + i: i for i in range(len(before))},
        compiler_params=params(40),
        cost_estimate=cost(3 * width * width, 16 * width * width),
    )(ids, near, *parts, w_qkv, *before)


def back_kernel(d_ref, w_ref, x_ref, inv_ref, gain_ref, grad_ref, out_ref):
    n, _, _, group = d_ref.shape
    width = x_ref.shape[1]
    out_ref[...] = jnp.zeros_like(out_ref)

    @pl.loop(0, n)
    def _(g):
        for part in range(3):
            at = pl.ds(pl.multiple_of(part * width + g * group, group), group)
            out_ref[...] += matmul_nt(d_ref[g, part], w_ref[:, at])

    x = x_ref[...].astype(F32)
    inverse = inv_ref[...]
    scaled = out_ref[...] * gain_ref[...]
    inner = jnp.mean(scaled * x, axis=-1, keepdims=True)
    out_ref[...] = grad_ref[...] + inverse * scaled - x * (inverse**3 * inner)


def back_to_tokens(d, w_qkv, x, inverse, gain, grad_hidden):
    rows, width = x.shape
    return pl.pallas_call(
        back_kernel,
        out_shape=shaped((rows, width), F32),
        in_specs=[VMEM] * 6,
        out_specs=VMEM,
        compiler_params=params(32),
        cost_estimate=cost(6 * rows * width * width, 10 * width * width),
    )(d, w_qkv, x, inverse, gain, grad_hidden)


def on_device(
    tokens,
    out_grad,
    token_ids,
    hash_table,
    doc_lengths,
    w_qkv,
    w_out,
    gain_attn,
    gain_ffn,
    expert_in,
    expert_out,
):
    rows = tokens.shape[1]
    width = tokens.shape[2]
    n = lax.axis_size("ctx")
    owners = lax.axis_size("expert")
    rank = lax.axis_index("ctx")
    z = lax.axis_index("expert")
    core = lax.axis_index("dp")
    group = width // n
    pairs = group // PAIR
    length = n * rows
    ids = jnp.stack([rank, z, core]).astype(jnp.int32)

    inputs_low = tokens[0]

    capacity = rows * 5 // (4 * owners)
    slots = owners * capacity
    chosen = jnp.take(hash_table, token_ids[0], axis=0)
    order = jnp.arange(rows, dtype=jnp.int32)
    ahead = (chosen[:, None] == chosen[None, :]) & (order[None, :] < order[:, None])
    slot = jnp.sum(ahead.astype(jnp.int32), axis=1)
    code = (chosen ^ z) * capacity + slot
    picks = (jnp.arange(slots, dtype=jnp.int32)[:, None] == code[None, :]).astype(BF16)
    spots = jnp.arange(slots, dtype=jnp.int32).reshape(owners, 1, capacity)
    places = (code[None, :, None] == spots).astype(BF16)

    def send_rows(matrix):
        far = {}
        for k in list(range(owners // 2, owners)) + list(range(1, owners // 2)):
            far[k] = swap(matrix[k * capacity : (k + 1) * capacity], "expert", k)
        return [matrix[:capacity]] + [far[k] for k in range(1, owners)]

    def spread(piece, before=()):
        line = after(jnp.concatenate([piece, swap(piece, "ctx", 1)], axis=0), *before)
        return jnp.concatenate([line, swap(line, "dp", 1)], axis=0)

    upstream = out_grad[0]
    w_in, w_o = expert_in[0], expert_out[0]
    units = w_in.shape[1]
    top = width * 3 // 4
    upper = w_in[:top]
    up_rows = matmul(picks, upstream).astype(BF16)
    up_arrived = send_rows(up_rows)
    late_low = after(inputs_low, up_rows)
    blocks = [inputs_low] + [
        swap(inputs_low if r & (r - 1) == 0 else late_low, "ctx", r) for r in range(1, n)
    ]
    chunks = [list(range(0, owners // 2)), list(range(owners // 2, owners))]

    doc_ends = jnp.cumsum(doc_lengths[0])
    spots = jnp.arange(length, dtype=jnp.int32)
    later = doc_ends[:, None] > spots[None, :]
    ends = jnp.min(jnp.where(later, doc_ends[:, None], length), axis=0)[None, :].astype(jnp.int32)
    starts = jnp.max(jnp.where(later, 0, doc_ends[:, None]), axis=0)[None, :].astype(jnp.int32)
    normed, inverse_one, q_own, k_own, v_own, mixed_own, att, tot = attend_forward(
        ids, ends, gain_attn[None, :], blocks, w_qkv, n
    )

    rest = jnp.concatenate(
        [w_in[top:]] + [w_o[:, at : at + units] for at in range(0, width, units)], axis=0
    )
    first = after(upper, *blocks[1:])
    firsts = [swap(first, "ctx", m << 1) for m in range(1, n // 2)]
    mixed_own = after(mixed_own, firsts)
    up_line = after(jnp.concatenate(up_arrived, axis=0), mixed_own)
    up_line = jnp.concatenate([up_line[None], swap(up_line, "ctx", 1)[None]], axis=0)
    up_all = jnp.concatenate([up_line[None], swap(up_line, "dp", 1)[None]], axis=0)
    up_chunks = [
        up_all[:, :, c[0] * capacity : (c[-1] + 1) * capacity].reshape(-1, width) for c in chunks
    ]

    mixed_sent = [lax.dynamic_slice_in_dim(mixed_own, (rank ^ r) * rows, rows, 0) for r in range(n)]
    mixed_parts = [mixed_sent[0]] + [swap(mixed_sent[r], "ctx", r) for r in range(1, n)]
    rest = after(rest, mixed_parts)
    rests = [swap(rest, "ctx", m << 1) for m in range(1, n // 2)]
    hidden, inverse_two, row_sent = middle(
        ids, mixed_parts, w_out, inputs_low, gain_ffn[None, :], picks
    )

    near, far = chunks
    arrived = {0: row_sent[:capacity]}
    for k in near[1:] + far:
        arrived[k] = swap(row_sent[k * capacity : (k + 1) * capacity], "expert", k)
    near_rows = jnp.concatenate([arrived[k] for k in near], axis=0)
    far_rows = after(jnp.concatenate([arrived[k] for k in far], axis=0), near_rows)
    row_chunks = [spread(near_rows), spread(far_rows, rests)]
    sizes = [units] * (n // 2)
    acts = []
    grad_pres = []
    far_back = {}
    x_sent = []
    for c, row_chunk, up_chunk in list(zip(chunks, row_chunks, up_chunks))[::-1]:
        if acts:
            row_chunk = after(row_chunk, theirs)
        mine, theirs, act, grad_pre = expert_rows(
            row_chunk, up_chunk, w_in, w_o, firsts, rests
        )
        acts.append(act)
        grad_pres.append(grad_pre)
        line = mine.astype(F32) + swap(theirs, "dp", 1).astype(F32)
        half = line.shape[0] // 2
        x_sent.append(line[half:].astype(BF16))
        own = (line[:half] + swap(x_sent[-1], "ctx", 1).astype(F32)).astype(BF16)
        for i, k in reversed(list(enumerate(c))):
            piece = own[i * capacity : (i + 1) * capacity]
            far_back[k] = piece if k == 0 else swap(piece, "expert", k)
    back = [far_back[k] for k in range(owners)]
    acts, grad_pres = acts[::-1], grad_pres[::-1]
    last_own = own

    grads_out = weight_grads_out(after(acts, x_sent[0]), up_chunks, sizes)

    def others(grads):
        return [swap(grads[i], "ctx", i << 1) for i in range(1, len(grads))]

    out_others = others(grads_out)
    made, made_other = produce(
        after(acts, x_sent[1]), w_o, rests, [len(c) * capacity for c in chunks]
    )
    grads_in = weight_grads(row_chunks, after(grad_pres, x_sent[1]), sizes)
    back = after(back, made, grads_in)
    made_other = swap(made_other, "dp", 1)

    grad_hidden, grad_parts, mine, theirs = turn(
        ids, back, mixed_parts, places, hidden, upstream, inverse_two, gain_ffn[None, :], w_out
    )
    grad_parts = after(grad_parts, out_others)
    grad_att_own = jnp.concatenate(
        [grad_parts[0]] + [swap(grad_parts[r], "ctx", r) for r in range(1, n)], axis=0
    )

    def add_others(own, parts):
        for part in parts:
            own = own + part.astype(F32)
        return own

    cols = width // PAIR
    size = mine.shape[0]
    got = swap(theirs, "dp", 1)
    gain_low = (theirs[size:].astype(F32) + got[size:].astype(F32)).astype(BF16)
    total = mine + got[:size].astype(F32)
    piece = size // n
    out_sent = [
        jnp.concatenate([total[r * piece : (r + 1) * piece].astype(BF16), gain_low], axis=0)
        for r in range(1, n)
    ]
    out_sent = after(out_sent, grad_att_own)
    out_got = [swap(out_sent[r - 1], "ctx", r) for r in range(1, n)]

    held = after(grad_att_own, out_sent)
    d_own, mine, theirs = attend_backward(
        ids, starts, normed, q_own, k_own, v_own, att, tot, held, n, owners
    )
    d_own, theirs = after((d_own, theirs), out_got)
    d_pieces = exchange(d_own, "ctx")
    in_others = others(after(grads_in, d_pieces))
    made_line = made.astype(F32) + after(made_other, d_pieces).astype(F32)
    sent = made_line[1].astype(BF16)
    made_own = (made_line[0] + swap(sent, "ctx", 1).astype(F32)).astype(BF16)
    order = list(range(owners // 2, owners)) + list(range(1, owners // 2))
    own, gain_low, *messages = join_sums(
        mine, swap(theirs, "dp", 1), total[: total.shape[0] // n], gain_low, out_got
    )
    tall = own.shape[0]
    got = {k: swap(messages[k - 1], "expert", k) for k in order}
    piece = own
    gains = [gain_low.astype(F32)]
    for k in range(owners - 1, 0, -1):
        piece = piece + got[k][:tall].astype(F32)
    for k in range(1, owners):
        gains.append(got[k][tall:].astype(F32))
    while len(gains) > 1:
        gains = [gains[i] + gains[i + 1] for i in range(0, len(gains), 2)]
    grad_gain_ffn = gains[0][:cols].reshape(width)
    piece = piece.astype(BF16)
    arrived = {k: swap(piece, "expert", k) for k in order}
    near_lines = spread_to(piece, "ctx")
    line = jnp.concatenate([arrived[k] for k in range(1, owners)], axis=0)
    line = after(line, in_others, made_own, near_lines)
    returned = send_rows(after(made_own, line))
    if n == 4:
        half = line.shape[0] // 2
        one, two = swap(line, "ctx", 1), swap(line, "ctx", 2)
        sent = (one[:half], two[half:])
        last = [swap(sent[0], "ctx", 2), swap(sent[1], "ctx", 1)]
        far_lines = [[line], [one], [two], last]
        in_others, out_others, d_pieces, returned = after(
            (in_others, out_others, d_pieces, returned), sent
        )
    else:
        far_lines = [[line]] + [[swap(line, "ctx", r)] for r in range(1, n)]
    grad_inputs = back_to_tokens(
        d_pieces,
        w_qkv,
        inputs_low,
        inverse_one,
        gain_attn[None, :],
        grad_hidden,
    )
    grad_expert_out = add_others(grads_out[0], out_others)
    grad_expert_in = add_others(grads_in[0], in_others)
    returned = jnp.concatenate(returned, axis=0)
    block_out = (
        hidden + matmul(places.transpose(1, 0, 2).reshape(rows, slots), returned)
    ).astype(BF16)
    near_other = swap(near_lines, "dp", 1)
    far_lines[n - 1] = after(
        far_lines[n - 1], block_out, grad_inputs, grad_expert_out, grad_expert_in, near_other
    )
    first = dense_out(ids, near_lines, far_lines, w_qkv, 0, owners)
    far_other = [[swap(part, "dp", 1) for part in parts] for parts in far_lines]
    grad_w_qkv, grad_w_out, gain_sums = dense_out(
        ids, near_other, far_other, w_qkv, 1, owners, first
    )
    grad_gain_attn = jnp.sum(gain_sums, axis=1) / gain_attn

    return (
        block_out[None],
        grad_inputs[None],
        grad_w_qkv,
        grad_w_out,
        grad_gain_attn,
        grad_gain_ffn,
        grad_expert_in[None],
        grad_expert_out[None],
    )


def solution(mesh):
    rows = P(("expert", "dp"), "ctx", None)
    placed = (
        rows,
        rows,
        P(("expert", "dp"), "ctx"),
        P(),
        P(("expert", "dp"), None),
        P(),
        P(),
        P(),
        P(),
        P("expert", None, ("ctx", "dp")),
        P("expert", ("ctx", "dp"), None),
    )
    return jax.shard_map(
        on_device,
        mesh=mesh,
        in_specs=placed,
        out_specs=(
            rows,
            rows,
            P(),
            P(),
            P(),
            P(),
            P("expert", None, ("ctx", "dp")),
            P("expert", ("ctx", "dp"), None),
        ),
        check_vma=False,
    )
```
